32 devices in a mesh: region: 8 (over z, y), survey: 4 (over x, core).
Axes of the slice: x: 2, y: 2, z: 4, core: 2. Of those that a mesh axis runs over, the one named last changes fastest.
Arguments:
- sensitivity: bfloat16 [128, 512, 4096], P(('region', 'survey')), may hold values from -0.09375 to 0.09375
- observed: float32 [128, 8, 512], P(('region', 'survey')), may hold values from -6 to 6
- data_weight: float32 [128, 512], P(('region', 'survey')), may hold values from 0.5 to 2
- data_counts: int32 [128], P(('region', 'survey')), may hold values from 128 to 512
- tile_bricks: int32 [128, 32], P(('region', 'survey')), may hold values from 0 to 16383, as said below
- start_model: float32 [128, 128, 8, 128], P('region', 'survey'), may hold values from -6 to 6
- active_cells: int32 [128, 128, 128], P('region', 'survey'), may hold values from 0 to 1
- face_links: int32 [128, 128, 128], P('region', 'survey'), may hold values from 0 to 63, as said below
- reg_weight: float32 [8], replicated, may hold values from 0.3 to 3
Outputs:
- final_model: float32 [128, 128, 8, 128], P('region', 'survey')
- misfit: float32 [128, 8, 512], P(('region', 'survey'))
The draws below stay inside these ranges and needn't reach their ends.
Inputs may be any that keep to these rules, and one draw needn't show every extreme that they name: `tile_bricks`: brick b lies on owning device b // 512 (region index times 4 plus survey index), at its slab's layer (b % 512) // 32 and row b % 32. The 128 entries of one device's tiles name bricks of at most 8 per owning device; one owning device, the same for all, is named exactly 8 times by every device's tiles. Entries may repeat. `face_links`: bit k (value 2^k) is 1 exactly when the cell and its neighbour n_k are both active, with k ordered as in the reference program.
All inputs are finite; a program needn't handle non-finite values.
Results may differ from the reference program's by a relative error of at most 0.0031.
Values may be sent and summed in bfloat16 or wider, within the bound.
No kernel may reach another device: no remote copies, remote signals or barrier semaphores. Data moves between devices by JAX's collectives and lax.ppermute only.
A program may use at most 128 MiB of HBM per device.

```python
import math
import jax
import jax.numpy as jnp
from jax import lax

ZS = 16
NYD = 32
NX = 128
NBT = 32
ND = 512
SAMPLES = 8
TILE_DEV = 4
ITERS = 2
SLABS = 8
STRIPS = 4
OWNERS = 32
CAP = 8
NZ = 128
NY = 128
BRICKS = 16384
TILES = 128


def draw_tile_bricks(key, part):
    slots = OWNERS * CAP
    requests = TILE_DEV * NBT
    hot_owner = jax.random.randint(jax.random.fold_in(key, 11), (), 0, OWNERS)
    slot_owner = jnp.arange(slots, dtype=jnp.int32) // CAP
    shallow = (SLABS - 1 - slot_owner // STRIPS) * 128
    forced = jnp.where(slot_owner == hot_owner, 1 << 20, 0)
    raw_scores = jax.random.randint(jax.random.fold_in(key, 12), (OWNERS, slots), 0, 4096)
    scores = (raw_scores + shallow[None, :] + forced[None, :]) * slots + jnp.arange(slots, dtype=jnp.int32)[None, :]
    chosen = lax.top_k(scores, requests)[1].astype(jnp.int32)
    order_keys = jax.random.split(jax.random.fold_in(key, 13), OWNERS)

    def shuffle_row(row_key, chosen_row):
        return chosen_row[jax.random.permutation(row_key, requests)]
    shuffled = jax.vmap(shuffle_row)(order_keys, chosen)
    owner_ids = shuffled // CAP
    local_ids = jax.random.randint(jax.random.fold_in(key, 14), (OWNERS, requests), 0, ZS * NYD)
    brick_ids = owner_ids * (ZS * NYD) + local_ids
    return brick_ids.reshape(TILES, NBT).astype(jnp.int32)


def cell_layout(key):
    surface = jax.random.randint(jax.random.fold_in(key, 21), (NY, NX), 0, 4)
    layers = jnp.arange(NZ, dtype=jnp.int32)[:, None, None]
    holes = jax.random.randint(jax.random.fold_in(key, 22), (NZ, NY, NX), 0, 16)
    return ((layers >= surface[None, :, :]) & (holes > 0)).astype(jnp.int32)


def draw_active_cells(key, part):
    return cell_layout(key)


def draw_face_links(key, part):
    live = cell_layout(key)
    padded = jnp.pad(live, 1)
    centre = padded[1:-1, 1:-1, 1:-1]
    neighbours = [padded[:-2, 1:-1, 1:-1], padded[2:, 1:-1, 1:-1], padded[1:-1, :-2, 1:-1], padded[1:-1, 2:, 1:-1], padded[1:-1, 1:-1, :-2], padded[1:-1, 1:-1, 2:]]
    coded = jnp.zeros_like(centre)
    for number in range(6):
        coded = coded + centre * neighbours[number] * 2 ** number
    return coded.astype(jnp.int32)


def set_ends(entries, key, low, largest):
    dims = entries.shape
    place = [jax.random.randint(jax.random.fold_in(key, axis), (), 0, dims[axis]) for axis in range(len(dims))]
    entries = entries.at[tuple(place)].set(low)
    longest = dims.index(max(dims))
    place[longest] = (place[longest] + 1) % dims[longest]
    return entries.at[tuple(place)].set(largest)


def block_scale(rng, shape, shards, least, largest):
    def one(position, parts):
        steps = jax.random.uniform(jax.random.fold_in(jax.random.fold_in(rng, 6), position), (parts,), jnp.float32, least / len(shards), largest / len(shards))
        return jnp.repeat(jnp.exp(steps), shape[position] // parts).reshape((-1,) + (1,) * (len(shape) - position - 1))

    loudness = one(*shards[0])
    for cut in shards[1:]:
        loudness = loudness * one(*cut)
    return loudness


def bell_draw(rng, shape, scale, most, shards=(), kind=jnp.bfloat16):
    drawn = jax.random.normal(rng, shape, jnp.float32) * scale
    if len(shards) > 0:
        drawn = block_scale(rng, shape, shards, -0.22, 0.18) * drawn
    return jnp.clip(drawn, min=-most, max=most).astype(kind)


def setup_inputs(seed: int = 0) -> dict:
    keys = jax.random.split(jax.random.key(seed), 10)
    return {
        "sensitivity": bell_draw(keys[0], (TILES, ND, NBT * NX), (NBT * NX) ** -0.5, 0.09375, ((0, 32),)),
        "observed": bell_draw(keys[1], (TILES, SAMPLES, ND), 1.0, 6.0, ((0, 32),), jnp.float32),
        "data_weight": jnp.clip(jnp.exp(math.log(2.0) - 1.3862944 * jax.random.uniform(keys[2], (TILES, ND), jnp.float32) ** block_scale(keys[2], (TILES, ND), ((0, 32),), -0.2, 0.2)), 0.5, 2.0),
        "data_counts": set_ends(jax.random.randint(keys[3], (TILES,), ND // 4, ND + 1), jax.random.fold_in(keys[3], 1), ND // 4, ND).astype(jnp.int32),
        "tile_bricks": draw_tile_bricks(jax.random.fold_in(keys[9], 71), 0),
        "start_model": bell_draw(keys[5], (NZ, NY, SAMPLES, NX), 1.0, 6.0, ((0, 8), (1, 4)), jnp.float32),
        "active_cells": draw_active_cells(jax.random.fold_in(keys[9], 71), 0),
        "face_links": draw_face_links(jax.random.fold_in(keys[9], 71), 0),
        "reg_weight": jnp.clip(jnp.exp(jax.random.uniform(keys[8], (SAMPLES,), jnp.float32, math.log(0.3), math.log(3.0))), 0.3, 3.0),
    }


EPS_SQ = 0.09

def stencil_list(padded):
    centre = padded[1:-1, 1:-1]
    zero_rim = jnp.zeros_like(centre[..., :1])
    neighbours = [padded[:-2, 1:-1], padded[2:, 1:-1], padded[1:-1, :-2], padded[1:-1, 2:], jnp.concatenate([zero_rim, centre[..., :-1]], axis=3), jnp.concatenate([centre[..., 1:], zero_rim], axis=3)]
    return (centre, neighbours)

def irls_weights(centre, neighbours, link_bits, depth_index, active, depth_count):
    smallness = active * (1.0 + 2.0 * depth_index / depth_count) / jnp.sqrt(centre * centre + EPS_SQ)
    offsets = [-1.0, 1.0, 0.0, 0.0, 0.0, 0.0]
    face_weights = []
    for number in range(6):
        depth_level = 1.0 + (2.0 * depth_index + offsets[number]) / depth_count
        difference = centre - neighbours[number]
        face_weights.append(link_bits[number] * depth_level / jnp.sqrt(difference * difference + EPS_SQ))
    return (smallness, face_weights)

def reg_gradient(centre, neighbours, smallness, face_weights):
    running = smallness * centre
    for number in range(6):
        running = running + face_weights[number] * (centre - neighbours[number])
    return running

def reg_curvature(centre, neighbours, smallness, face_weights):
    running = smallness * centre * centre
    for number in range(6):
        difference = centre - neighbours[number]
        running = running + 0.5 * face_weights[number] * difference * difference
    return lax.optimization_barrier(jnp.sum(running, axis=(0, 1, 3)))

def to_bricks(field):
    shaped = field.reshape(SLABS, ZS, STRIPS, NYD, SAMPLES, NX)
    return shaped.transpose(0, 2, 1, 3, 4, 5).reshape(BRICKS, SAMPLES, NX)

def from_bricks(flattened):
    shaped = flattened.reshape(SLABS, STRIPS, ZS, NYD, SAMPLES, NX)
    return shaped.transpose(0, 2, 1, 3, 4, 5).reshape(NZ, NY, SAMPLES, NX)

def forward(field, sensitivity, tile_bricks):
    lowered = lax.optimization_barrier(field.astype(jnp.bfloat16))
    brick_store = to_bricks(lowered)

    def per_tile(operands):
        sensor, brick_ids = operands
        picked = brick_store[brick_ids].astype(jnp.float32)
        sensor_view = sensor.reshape(ND, NBT, NX).astype(jnp.float32)
        return jnp.einsum('dbx,bsx->sd', sensor_view, picked, precision=lax.Precision.HIGHEST)
    return lax.map(per_tile, (sensitivity, tile_bricks))

def backward(weighted, sensitivity, tile_bricks):

    def per_tile(operands):
        sensor, weights_low = operands
        sensor_view = sensor.reshape(ND, NBT, NX).astype(jnp.float32)
        return jnp.einsum('sd,dbx->bsx', weights_low.astype(jnp.float32), sensor_view, precision=lax.Precision.HIGHEST)
    products = lax.map(per_tile, (sensitivity, weighted))
    flattened = jnp.zeros((BRICKS, SAMPLES, NX), jnp.float32)
    flattened = flattened.at[tile_bricks.reshape(-1)].add(products.reshape(-1, SAMPLES, NX))
    return from_bricks(flattened)

def pad_cells(field):
    return jnp.pad(field, ((1, 1), (1, 1), (0, 0), (0, 0)))

def reference(sensitivity, observed, data_weight, data_counts, tile_bricks, start_model, active_cells, face_links, reg_weight):
    active = active_cells.astype(jnp.float32)[:, :, None, :]
    link_bits = [(face_links // 2 ** number % 2).astype(jnp.float32)[:, :, None, :] for number in range(6)]
    depth_index = jnp.arange(NZ, dtype=jnp.float32).reshape(NZ, 1, 1, 1)
    row_mask = (jnp.arange(ND, dtype=jnp.int32)[None, None, :] < data_counts[:, None, None]).astype(jnp.float32)
    weight_sq = row_mask * (data_weight * data_weight)[:, None, :]
    reg_scale = reg_weight[None, None, :, None]
    model_now = start_model * active
    predicted = forward(model_now, sensitivity, tile_bricks)
    for iteration in range(ITERS):
        weighted = (weight_sq * (predicted - observed)).astype(jnp.bfloat16)
        data_grad = backward(weighted, sensitivity, tile_bricks)
        centre, neighbours = stencil_list(pad_cells(model_now))
        smallness, face_weights = irls_weights(centre, neighbours, link_bits, depth_index, active, NZ)
        gradient = active * data_grad + reg_scale * reg_gradient(centre, neighbours, smallness, face_weights)
        step_pred = forward(gradient, sensitivity, tile_bricks)
        grad_centre, grad_neighbours = stencil_list(pad_cells(gradient))
        reg_curv = reg_curvature(grad_centre, grad_neighbours, smallness, face_weights)
        grad_norm = lax.optimization_barrier(jnp.sum(gradient * gradient, axis=(0, 1, 3)))
        data_curv = lax.optimization_barrier(jnp.sum(weight_sq * step_pred * step_pred, axis=(0, 2)))
        step_length = grad_norm / (data_curv + reg_weight * reg_curv)
        model_now = model_now - step_length[None, None, :, None] * gradient
        predicted = predicted - step_length[None, :, None] * step_pred
    misfit = row_mask * data_weight[:, None, :] * (predicted - observed)
    return (model_now, misfit)
```

```python
import functools

import jax
import jax.numpy as jnp
from jax import lax
from jax.experimental import pallas as pl
from jax.experimental.pallas import tpu as pltpu
from jax.sharding import PartitionSpec as P

AXES = ("region", "survey")
EPS_SQ = 0.09
VMEM_LIMIT = 32 * 1024 * 1024


def swap(field):
    return lax.all_to_all(field, AXES, split_axis=0, concat_axis=0, tiled=True)


def edges(field):
    rims = []
    for axis, dim in (("region", 0), ("survey", 1)):
        count, length = (lax.axis_size(axis), field.shape[dim])
        up = [(i, i + 1) for i in range(count - 1)]
        down = [(i + 1, i) for i in range(count - 1)]
        last = lax.slice_in_dim(field, length - 1, length, axis=dim)
        first = lax.slice_in_dim(field, 0, 1, axis=dim)
        rims.append(lax.ppermute(last, axis, up))
        rims.append(lax.ppermute(first, axis, down))
    return rims


def neighbour_list(centre, rims):
    above, below, left, right = rims
    zero_rim = jnp.zeros_like(centre[..., :1])
    return [
        jnp.concatenate([above, centre[:-1]], axis=0),
        jnp.concatenate([centre[1:], below], axis=0),
        jnp.concatenate([left, centre[:, :-1]], axis=1),
        jnp.concatenate([centre[:, 1:], right], axis=1),
        jnp.concatenate([zero_rim, centre[..., :-1]], axis=3),
        jnp.concatenate([centre[..., 1:], zero_rim], axis=3),
    ]


def irls_weights(centre, neighbours, link_bits, depth_index, active, depth_count):
    smallness = (
        active * (1.0 + 2.0 * depth_index / depth_count) * lax.rsqrt(centre * centre + EPS_SQ)
    )
    offsets = [-1.0, 1.0, 0.0, 0.0, 0.0, 0.0]
    face_weights = []
    for number in range(6):
        depth_level = 1.0 + (2.0 * depth_index + offsets[number]) / depth_count
        difference = centre - neighbours[number]
        face_weights.append(
            link_bits[number] * depth_level * lax.rsqrt(difference * difference + EPS_SQ)
        )
    return (smallness, face_weights)


def reg_gradient(centre, neighbours, smallness, face_weights):
    running = smallness * centre
    for number in range(6):
        running = running + face_weights[number] * (centre - neighbours[number])
    return running


def reg_curvature(centre, neighbours, smallness, face_weights):
    running = smallness * centre * centre
    for number in range(6):
        difference = centre - neighbours[number]
        running = running + 0.5 * face_weights[number] * difference * difference
    return jnp.sum(running, axis=(0, 1, 3))


def gather_rows(tile, width, slot_ref, arrived_ref, rows_ref):
    cells = arrived_ref.shape[2]
    for entry in range(width):
        slot = slot_ref[tile * width + entry]
        rows_ref[:, entry * cells : (entry + 1) * cells] = arrived_ref[slot]


def scatter_rows(tile, width, slot_ref, blocks, buffer_ref):
    cells = buffer_ref.shape[2]
    for entry in range(width):
        slot = slot_ref[tile * width + entry]
        block = blocks[:, entry * cells : (entry + 1) * cells]
        buffer_ref[slot] = block.astype(buffer_ref.dtype)


def project(rows, sensor):
    return lax.dot_general(
        rows, sensor, (((1,), (1,)), ((), ())), preferred_element_type=jnp.float32
    )


def residual_kernel(
    slot_ref, arrived_ref, sensor_ref, observed_ref, weight_ref, pred_ref, buffer_ref, rows_ref
):
    tile = pl.program_id(0)
    width = slot_ref.shape[0] // pl.num_programs(0)

    @pl.when(tile == 0)
    def _():
        buffer_ref[...] = jnp.zeros_like(buffer_ref)

    gather_rows(tile, width, slot_ref, arrived_ref, rows_ref)
    pred = project(rows_ref[...], sensor_ref[0])
    pred_ref[0] = pred
    weighted = (weight_ref[0] * (pred - observed_ref[0])).astype(jnp.bfloat16)
    blocks = jnp.dot(weighted, sensor_ref[0], preferred_element_type=jnp.float32)
    scatter_rows(tile, width, slot_ref, blocks, buffer_ref)


def forward_kernel(slot_ref, arrived_ref, sensor_ref, weight_ref, pred_ref, curv_ref, rows_ref):
    tile = pl.program_id(0)
    width = slot_ref.shape[0] // pl.num_programs(0)

    @pl.when(tile == 0)
    def _():
        curv_ref[...] = jnp.zeros_like(curv_ref)

    gather_rows(tile, width, slot_ref, arrived_ref, rows_ref)
    pred = project(rows_ref[...], sensor_ref[0])
    pred_ref[0] = pred
    curv_ref[...] += weight_ref[0] * pred * pred


def backward_kernel(slot_ref, sensor_ref, pred_ref, weight_ref, buffer_ref):
    tile = pl.program_id(0)
    width = slot_ref.shape[0] // pl.num_programs(0)
    samples = pred_ref.shape[1]

    @pl.when(tile == 0)
    def _():
        buffer_ref[...] = jnp.zeros_like(buffer_ref)

    weighted = weight_ref[0] * pred_ref[0]
    upper = weighted.astype(jnp.bfloat16).astype(jnp.float32)
    both = jnp.concatenate([upper, weighted - upper], axis=0).astype(jnp.bfloat16)
    blocks = jnp.dot(both, sensor_ref[0], preferred_element_type=jnp.float32)
    scatter_rows(tile, width, slot_ref, blocks[:samples] + blocks[samples:], buffer_ref)


def tile_call(kernel, name, ids, operands, outs, scratch, fixed):
    tiles = outs[0].shape[0] if "pred" in name else operands[0].shape[0]

    def spec(array, whole):
        if whole:
            return pl.BlockSpec(array.shape, lambda t, *_: (0,) * len(array.shape))
        block = (1,) + tuple(array.shape[1:])
        return pl.BlockSpec(block, lambda t, *_: (t,) + (0,) * (len(block) - 1))

    return pl.pallas_call(
        kernel,
        name=name,
        out_shape=outs,
        grid_spec=pltpu.PrefetchScalarGridSpec(
            num_scalar_prefetch=1,
            grid=(tiles,),
            in_specs=[spec(a, f) for a, f in zip(operands, fixed[0])],
            out_specs=[spec(a, f) for a, f in zip(outs, fixed[1])],
            scratch_shapes=scratch,
        ),
        compiler_params=pltpu.CompilerParams(
            dimension_semantics=("arbitrary",), vmem_limit_bytes=VMEM_LIMIT
        ),
    )(ids, *operands)


def sum_kernel(
    first, ids_ref, arrived_ref, reg_ref, active_ref, *refs
):
    if first:
        total_ref, grad_ref, reply_ref, norm_ref = refs
    else:
        base_ref, step_ref, grad_ref, reply_ref, norm_ref, total_ref = refs
        step = step_ref[...]
    count = ids_ref.shape[0]
    bricks = grad_ref.shape[0]
    group = 8
    total_ref[...] = jnp.zeros_like(total_ref)

    def add(i, carry):
        for k in range(group):
            j = i * group + k
            row = ids_ref[j]
            total_ref[row] += arrived_ref[j].astype(jnp.float32)
        return carry

    lax.fori_loop(0, count // group, add, 0)

    def combine(i, norm):
        live = active_ref[pl.ds(pl.multiple_of(i * group, group), group), :]
        for k in range(group):
            j = i * group + k
            data = total_ref[j]
            if not first:
                data = base_ref[j] - step * data
            grad = live[k : k + 1] * data + reg_ref[j]
            grad_ref[j] = grad
            norm = norm + grad * grad
        return norm

    norm = lax.fori_loop(0, bricks // group, combine, jnp.zeros(norm_ref.shape, jnp.float32))
    norm_ref[...] = norm

    def reply(i, carry):
        for k in range(group):
            j = i * group + k
            reply_ref[j] = grad_ref[ids_ref[j]].astype(reply_ref.dtype)
        return carry

    lax.fori_loop(0, count // group, reply, 0)


def sum_call(first, ids, arrived, reg, active, *more):
    bricks, samples, cells = reg.shape
    field = jax.ShapeDtypeStruct((bricks, samples, cells), jnp.float32)
    outs = [
        field,
        jax.ShapeDtypeStruct(arrived.shape, jnp.bfloat16),
        jax.ShapeDtypeStruct((samples, cells), jnp.float32),
    ]
    scratch = []
    if first:
        outs = [field] + outs
    else:
        scratch = [pltpu.VMEM(field.shape, jnp.float32)]
    whole = pl.BlockSpec(memory_space=pltpu.VMEM)
    operands = (arrived, reg, active) + more
    return pl.pallas_call(
        functools.partial(sum_kernel, first),
        name="sum_first" if first else "sum_next",
        out_shape=outs,
        grid_spec=pltpu.PrefetchScalarGridSpec(
            num_scalar_prefetch=1,
            grid=(),
            in_specs=[whole] * len(operands),
            out_specs=[whole] * len(outs),
            scratch_shapes=scratch,
        ),
        compiler_params=pltpu.CompilerParams(vmem_limit_bytes=VMEM_LIMIT),
    )(ids, *operands)


def total_sums(owners, samples, *sums):
    packed = jnp.concatenate(sums)
    packed = jnp.pad(packed, (0, -packed.shape[0] % 128))
    sent = jnp.broadcast_to(packed[None, None, :], (owners, 1, packed.shape[0]))
    got = jnp.sum(swap(sent), axis=(0, 1))
    return [got[i * samples : (i + 1) * samples] for i in range(len(sums))]


def shards(
    sensitivity,
    observed,
    data_weight,
    data_counts,
    tile_bricks,
    start_model,
    active_cells,
    face_links,
    reg_weight,
):
    layers, strip_rows, samples, cells_x = start_model.shape
    tiles, tile_width = tile_bricks.shape
    data_slots = sensitivity.shape[1]
    owners = lax.axis_size("region") * lax.axis_size("survey")
    per_owner = layers * strip_rows
    capacity = max(2, 2 * tiles * tile_width // owners)
    slots = owners * capacity
    depth_count = layers * lax.axis_size("region")
    requests = tile_bricks.reshape(-1)
    owner_of = requests // per_owner
    local_of = requests % per_owner
    owner_hits = (owner_of[:, None] == jnp.arange(owners, dtype=jnp.int32)[None, :]).astype(
        jnp.int32
    )
    before = jnp.cumsum(owner_hits, axis=0) - owner_hits
    rank_of = jnp.sum(before * owner_hits, axis=1)
    slot_of = owner_of * capacity + rank_of
    slot_hits = slot_of[:, None] == jnp.arange(slots, dtype=jnp.int32)[None, :]
    asking = jnp.sum(jnp.where(slot_hits, local_of[:, None], 0), axis=0).reshape(owners, capacity)
    asked_ids = swap(asking).reshape(-1)

    active_rows = active_cells.astype(jnp.float32)
    active = active_rows[:, :, None, :]
    active_flat = active_rows.reshape(per_owner, cells_x)
    link_bits = [
        (face_links // 2**number % 2).astype(jnp.float32)[:, :, None, :] for number in range(6)
    ]
    depth_index = (
        (lax.axis_index("region") * layers + jnp.arange(layers, dtype=jnp.int32))
        .astype(jnp.float32)
        .reshape(layers, 1, 1, 1)
    )
    row_mask = (
        jnp.arange(data_slots, dtype=jnp.int32)[None, None, :] < data_counts[:, None, None]
    ).astype(jnp.float32)
    weight_sq = row_mask * (data_weight * data_weight)[:, None, :]
    reg_scale = reg_weight[None, None, :, None]

    model = start_model * active
    model_rims = edges(model)

    bricks = model.astype(jnp.bfloat16).reshape(per_owner, samples, cells_x)
    replies = bricks[asked_ids]
    f32 = functools.partial(jax.ShapeDtypeStruct, dtype=jnp.float32)
    pred_shape = f32((tiles, samples, data_slots))
    buffer_shape = jax.ShapeDtypeStruct((slots, samples, cells_x), jnp.bfloat16)
    rows = pltpu.VMEM((samples, tile_width * cells_x), jnp.bfloat16)

    def exchange(blocks):
        return swap(blocks.reshape(owners, capacity, samples, cells_x)).reshape(
            slots, samples, cells_x
        )

    def weights_of(field, rims):
        neighbours = neighbour_list(field, rims)
        smallness, faces = irls_weights(
            field, neighbours, link_bits, depth_index, active, depth_count
        )
        return smallness, faces, reg_scale * reg_gradient(field, neighbours, smallness, faces)

    predicted, buffer = tile_call(
        residual_kernel,
        "residual_pred",
        slot_of,
        (exchange(replies), sensitivity, observed, weight_sq),
        [pred_shape, buffer_shape],
        [rows],
        ((True, False, False, False), (False, True)),
    )

    def forward(replies):
        return tile_call(
            forward_kernel,
            "forward_pred",
            slot_of,
            (exchange(replies), sensitivity, weight_sq),
            [pred_shape, f32((samples, data_slots))],
            [rows],
            ((True, False, False), (False, True)),
        )

    def curvature(grad, rims, smallness, faces):
        return reg_curvature(grad, neighbour_list(grad, rims), smallness, faces)

    def step_of(norm, data_curv, reg_curv):
        norm, data_curv, reg_curv = total_sums(
            owners, samples, jnp.sum(norm, axis=1), jnp.sum(data_curv, axis=1), reg_curv
        )
        return norm / (data_curv + reg_weight * reg_curv)

    smallness, faces, reg = weights_of(model, model_rims)
    data_sum, grad, replies, norm = sum_call(
        True, asked_ids, exchange(buffer), reg.reshape(per_owner, samples, cells_x), active_flat
    )
    grad = grad.reshape(start_model.shape)
    grad_rims = edges(grad)
    step_pred, data_curv = forward(replies)
    reg_curv = curvature(grad, grad_rims, smallness, faces)
    step = step_of(norm, data_curv, reg_curv)
    (buffer,) = tile_call(
        backward_kernel,
        "backward",
        slot_of,
        (sensitivity, step_pred, weight_sq),
        [buffer_shape],
        [],
        ((False, False, False), (True,)),
    )
    arrived = exchange(buffer)
    step_field = step[None, None, :, None]
    model = model - step_field * grad
    model_rims = [a - step_field * b for a, b in zip(model_rims, grad_rims)]
    predicted = predicted - step[None, :, None] * step_pred

    smallness, faces, reg = weights_of(model, model_rims)
    grad, replies, norm = sum_call(
        False,
        asked_ids,
        arrived,
        reg.reshape(per_owner, samples, cells_x),
        active_flat,
        data_sum,
        jnp.broadcast_to(step[:, None], (samples, cells_x)),
    )
    grad = grad.reshape(start_model.shape)
    grad_rims = edges(grad)
    step_pred, data_curv = forward(replies)
    reg_curv = curvature(grad, grad_rims, smallness, faces)
    step = step_of(norm, data_curv, reg_curv)
    model = model - step[None, None, :, None] * grad
    predicted = predicted - step[None, :, None] * step_pred
    misfit = row_mask * data_weight[:, None, :] * (predicted - observed)
    return (model, misfit)


def solution(mesh):
    return jax.shard_map(
        shards,
        mesh=mesh,
        in_specs=(
            P(("region", "survey"), None, None),
            P(("region", "survey"), None, None),
            P(("region", "survey"), None),
            P(("region", "survey")),
            P(("region", "survey"), None),
            P("region", "survey", None, None),
            P("region", "survey", None),
            P("region", "survey", None),
            P(),
        ),
        out_specs=(P("region", "survey", None, None), P(("region", "survey"), None, None)),
        check_vma=False,
    )
```

```python
import functools

import jax
import jax.numpy as jnp
from jax import lax
from jax.experimental import pallas as pl
from jax.experimental.pallas import tpu as pltpu
from jax.sharding import PartitionSpec as P


AXES = ("region", "survey")
EPS_SQ = 0.09
KERNEL_VMEM = 32 * 1024 * 1024
PART = 256


def swap(field):
    return lax.all_to_all(field, AXES, split_axis=0, concat_axis=0, tiled=True)


def outer(field):
    return [field[0], field[-1], field[:, 0], field[:, -1]]


def edges(parts, both=True):
    rims = [[], []]
    for axis, (first, last) in (("region", parts[:2]), ("survey", parts[2:])):
        count = lax.axis_size(axis)
        rims[0].append(lax.ppermute(first, axis, [(i + 1, i) for i in range(count - 1)]))
        if both:
            rims[1].append(lax.ppermute(last, axis, [(i, i + 1) for i in range(count - 1)]))
    return rims[0] + rims[1]


def start_pads(field_ref, pad, next_refs, sem):
    layers, rows = field_ref.shape[:2]
    copy = pltpu.make_async_copy(field_ref, pad.at[pl.ds(0, layers), pl.ds(0, rows)], sem)
    copy.start()
    pad[layers, pl.ds(0, rows)] = next_refs[0][...].astype(pad.dtype)
    for layer in range(layers):
        pad[layer, rows] = next_refs[1][layer].astype(pad.dtype)
    return copy


def face(here, there, link):
    difference = here - there
    return difference, link * lax.rsqrt(difference * difference + EPS_SQ)


def levels(base, layer, depth_count):
    depth = (base + layer).astype(jnp.float32)
    return [1.0 + (2.0 * depth + offset) / depth_count for offset in (-1.0, 0.0, 1.0)]


def link_of(codes, number, level):
    return (lax.shift_right_logical(codes, number) & 1).astype(jnp.float32) * level


def next_lane(value):
    return pltpu.roll(value, value.shape[-1] - 1, value.ndim - 1)


def reg_kernel(first, depth_count, base_ref, links_ref, active_ref, scale_ref, field_ref, *refs):
    if first:
        below, right, above, left, reg_ref, out, pad, flow, sems = refs
    else:
        below, right, above, left, step_ref, grad_ref, *refs = refs
        gbelow, gright, gabove, gleft, reg_ref, new_ref, nbelow, nright, *refs = refs
        out, pad, flow, sems, gpad = refs
        step = step_ref[...]
    layers, rows = field_ref.shape[:2]
    group = 8
    base = base_ref[0]
    scale = scale_ref[...]
    copies = [start_pads(field_ref, pad, (below, right), sems.at[0])]
    if not first:
        copies.append(start_pads(grad_ref, gpad, (gbelow, gright), sems.at[1]))
    for copy in copies:
        copy.wait()
    if not first:

        def move(layer, carry):
            for row in range(rows + 1):
                pad[layer, row] = pad[layer, row] - step * gpad[layer, row]
            return carry

        lax.fori_loop(0, layers, move, 0)
        for row in range(rows):
            pad[layers, row] = pad[layers, row] - step * gpad[layers, row]
        nbelow[...] = pad[layers, pl.ds(0, rows)]
        for layer in range(layers):
            nright[layer] = pad[layer, rows]
        store = pltpu.make_async_copy(
            pad.at[pl.ds(0, layers), pl.ds(0, rows)], new_ref, sems.at[2]
        )
        store.start()
    lane = lax.broadcasted_iota(jnp.int32, (group, pad.shape[-1]), 1)
    inner = (lane < pad.shape[-1] - 1).astype(jnp.float32)

    def prior(ref, gref, index):
        value = ref[index]
        if first:
            return value
        return value - step * gref[index].astype(jnp.float32)

    for start in range(0, rows, group):
        codes = links_ref[pl.ds(start, group), :]
        link = link_of(codes, 0, levels(base, 0, depth_count)[0])
        for k in range(group):
            row = start + k
            came = prior(above, None if first else gabove, row)
            difference, weight = face(came, pad[0, row], link[k : k + 1])
            flow[row] = weight * difference

    def one(layer, carry):
        _, level, level_below = levels(base, layer, depth_count)
        flow_y = None
        for start in range(0, rows, group):
            place = pl.ds(pl.multiple_of(layer * rows + start, group), group)
            codes = links_ref[place, :]
            link_z = link_of(codes, 1, level_below)
            link_y = link_of(codes, 3, level)
            link_x = link_of(codes, 5, level) * inner
            live = active_ref[place, :] * level
            if start == 0:
                came = prior(left, None if first else gleft, layer)
                link = link_of(codes, 2, level)
                difference, weight = face(came, pad[layer, 0], link[:1])
                flow_y = weight * difference
            for k in range(group):
                row = start + k
                one_row = slice(k, k + 1)
                here = pad[layer, row]
                total = live[one_row] * lax.rsqrt(here * here + EPS_SQ) * here
                difference, weight = face(here, next_lane(here), link_x[one_row])
                flow_x = weight * difference
                total = total + flow_x - pltpu.roll(flow_x, 1, 1)
                difference, weight = face(here, pad[layer, row + 1], link_y[one_row])
                out_y = weight * difference
                total = total + out_y - flow_y
                flow_y = out_y
                difference, weight = face(here, pad[layer + 1, row], link_z[one_row])
                out_z = weight * difference
                total = total + out_z - flow[row]
                flow[row] = out_z
                out[layer, row] = scale * total
        return carry

    lax.fori_loop(0, layers, one, 0)
    final = pltpu.make_async_copy(out, reg_ref, sems.at[3])
    final.start()
    final.wait()
    if not first:
        store.wait()


def curvature_kernel(
    depth_count, base_ref, links_ref, active_ref, field_ref, below, right, grad_ref, gbelow,
    gright, curv_ref, pad, gpad, sems
):
    layers, rows = field_ref.shape[:2]
    group = 8
    base = base_ref[0]
    copies = [
        start_pads(field_ref, pad, (below, right), sems.at[0]),
        start_pads(grad_ref, gpad, (gbelow, gright), sems.at[1]),
    ]
    for copy in copies:
        copy.wait()
    lane = lax.broadcasted_iota(jnp.int32, (group, pad.shape[-1]), 1)
    inner = (lane < pad.shape[-1] - 1).astype(jnp.float32)

    def one(layer, total):
        _, level, level_below = levels(base, layer, depth_count)
        for start in range(0, rows, group):
            place = pl.ds(pl.multiple_of(layer * rows + start, group), group)
            codes = links_ref[place, :]
            link_z = link_of(codes, 1, level_below)
            link_y = link_of(codes, 3, level)
            link_x = link_of(codes, 5, level) * inner
            live = active_ref[place, :] * level
            for k in range(group):
                row = start + k
                one_row = slice(k, k + 1)
                here = pad[layer, row]
                slope = gpad[layer, row]
                part = live[one_row] * lax.rsqrt(here * here + EPS_SQ) * slope * slope
                for there, gthere, link in (
                    (next_lane(here), next_lane(slope), link_x),
                    (pad[layer, row + 1], gpad[layer, row + 1], link_y),
                    (pad[layer + 1, row], gpad[layer + 1, row], link_z),
                ):
                    _, weight = face(here, there, link[one_row])
                    change = slope - gthere
                    part = part + weight * change * change
                total = total + part
        return total

    curv_ref[...] = lax.fori_loop(0, layers, one, jnp.zeros(curv_ref.shape, jnp.float32))


def grid_call(kernel, base, operands, apart, outs, outs_apart, scratch):
    whole = pl.BlockSpec(memory_space=pltpu.VMEM)
    far = pl.BlockSpec(memory_space=pltpu.HBM)
    return pl.pallas_call(
        kernel,
        out_shape=outs,
        grid_spec=pltpu.PrefetchScalarGridSpec(
            num_scalar_prefetch=1,
            grid=(),
            in_specs=[far if i in apart else whole for i in range(len(operands))],
            out_specs=[far if i in outs_apart else whole for i in range(len(outs))],
            scratch_shapes=scratch,
        ),
        compiler_params=pltpu.CompilerParams(vmem_limit_bytes=KERNEL_VMEM),
    )(base, *operands)


def shape_f32(*shape):
    return jax.ShapeDtypeStruct(shape, jnp.float32)


def reg_call(depth_count, base, links, active, scale, field, rims, moved=()):
    layers, rows, samples, cells = field.shape
    pad = pltpu.VMEM((layers + 1, rows + 1, samples, cells), jnp.float32)
    scratch = [
        pltpu.VMEM(field.shape, jnp.float32),
        pad,
        pltpu.VMEM((rows, samples, cells), jnp.float32),
        pltpu.SemaphoreType.DMA((4,)),
    ]
    operands = [links, active, scale, field, *rims]
    outs = [shape_f32(*field.shape)]
    apart = [3]
    if moved:
        step, grad, grad_rims = moved
        operands += [step, grad, *grad_rims]
        apart.append(9)
        scratch.append(pad)
        outs += [outs[0], shape_f32(rows, samples, cells), shape_f32(layers, samples, cells)]
    return grid_call(
        functools.partial(reg_kernel, not moved, depth_count),
        base,
        operands,
        apart,
        outs,
        [0, 1],
        scratch,
    )


def curvature_call(depth_count, base, links, active, field, rims, grad, grad_rims):
    layers, rows, samples, cells = field.shape
    pad = pltpu.VMEM((layers + 1, rows + 1, samples, cells), jnp.float32)
    (curv,) = grid_call(
        functools.partial(curvature_kernel, depth_count),
        base,
        [links, active, field, *rims[:2], grad, *grad_rims[:2]],
        [2, 5],
        [shape_f32(samples, cells)],
        [],
        [pad, pad, pltpu.SemaphoreType.DMA((2,))],
    )
    return jnp.sum(curv, axis=1)


def load_sensors(sensor_ref, held_ref, sems, parts):
    height = held_ref.shape[1]
    copies = []
    for chunk in range(held_ref.shape[0]):
        rows = pl.ds(chunk % parts * height, height)
        copies.append(
            pltpu.make_async_copy(
                sensor_ref.at[chunk // parts, rows], held_ref.at[chunk], sems.at[chunk]
            )
        )
        copies[-1].start()


def wait_part(sensor_ref, held_ref, sems, tile, part, parts):
    height = held_ref.shape[1]
    chunk = tile * parts + part
    rows = pl.ds(part * height, height)
    pltpu.make_async_copy(
        sensor_ref.at[tile, rows], held_ref.at[chunk], sems.at[chunk]
    ).wait()


def gather_rows(width, slot_ref, arrived_ref, rows_ref):
    cells = arrived_ref.shape[2]

    def one(tile, carry):
        for entry in range(width):
            slot = slot_ref[tile * width + entry]
            rows_ref[tile, :, entry * cells : (entry + 1) * cells] = arrived_ref[slot]
        return carry

    lax.fori_loop(0, rows_ref.shape[0], one, 0)


def scatter_rows(tile, width, slot_ref, blocks, buffer_ref):
    cells = buffer_ref.shape[2]
    for entry in range(width):
        slot = slot_ref[tile * width + entry]
        block = blocks[:, entry * cells : (entry + 1) * cells]
        buffer_ref[slot] = block.astype(buffer_ref.dtype)


def project(rows, sensor):
    return lax.dot_general(
        rows, sensor, (((1,), (1,)), ((), ())), preferred_element_type=jnp.float32
    )


def tile_kernel(mode, slot_ref, arrived_ref, sensor_ref, weight_ref, *refs):
    if mode == "residual":
        observed_ref, pred_ref, buffer_ref, rows_ref, held_ref, sems = refs
    else:
        pred_ref, curv_ref, rows_ref, held_ref, sems = refs
    tiles, _ = pred_ref.shape[:2]
    height = held_ref.shape[1]
    parts = held_ref.shape[0] // tiles
    width = slot_ref.shape[0] // tiles
    load_sensors(sensor_ref, held_ref, sems, parts)
    if mode == "residual":
        buffer_ref[...] = jnp.zeros_like(buffer_ref)
    else:
        curv_ref[...] = jnp.zeros_like(curv_ref)
    gather_rows(width, slot_ref, arrived_ref, rows_ref)

    def one(tile, carry):
        sent = []
        for part in range(parts):
            span = slice(part * height, (part + 1) * height)
            wait_part(sensor_ref, held_ref, sems, tile, part, parts)
            pred = project(rows_ref[tile], held_ref[tile * parts + part])
            pred_ref[tile, :, span] = pred
            weight = weight_ref[tile, :, span]
            if mode == "residual":
                weighted = weight * (pred - observed_ref[tile, :, span])
                sent.append(weighted.astype(jnp.bfloat16))
                continue
            curv_ref[:, span] += weight * pred * pred
        if mode == "residual":
            blocks = 0.0
            for part in range(parts):
                blocks += jnp.dot(
                    sent[part],
                    held_ref[tile * parts + part],
                    preferred_element_type=jnp.float32,
                )
            scatter_rows(tile, width, slot_ref, blocks, buffer_ref)
        return carry

    lax.fori_loop(0, tiles, one, 0)


def back_kernel(slot_ref, sensor_ref, weight_ref, pred_ref, buffer_ref, held_ref, sems):
    tiles, samples = pred_ref.shape[:2]
    height = held_ref.shape[1]
    parts = held_ref.shape[0] // tiles
    width = slot_ref.shape[0] // tiles
    load_sensors(sensor_ref, held_ref, sems, parts)
    buffer_ref[...] = jnp.zeros_like(buffer_ref)

    def one(tile, carry):
        weighted = weight_ref[tile] * pred_ref[tile]
        upper = weighted.astype(jnp.bfloat16).astype(jnp.float32)
        both = jnp.concatenate([upper, weighted - upper], axis=0).astype(jnp.bfloat16)
        blocks = 0.0
        for part in range(parts):
            wait_part(sensor_ref, held_ref, sems, tile, part, parts)
            blocks += jnp.dot(
                both[:, part * height : (part + 1) * height],
                held_ref[tile * parts + part],
                preferred_element_type=jnp.float32,
            )
        scatter_rows(tile, width, slot_ref, blocks[:samples] + blocks[samples:], buffer_ref)
        return carry

    lax.fori_loop(0, tiles, one, 0)


def back_call(slot_of, slots, cells, sensor, weight, pred):
    tiles, data_slots, length = sensor.shape
    height = PART if data_slots % PART == 0 else data_slots
    chunks = tiles * data_slots // height
    whole = pl.BlockSpec(memory_space=pltpu.VMEM)
    return pl.pallas_call(
        back_kernel,
        name="backward",
        out_shape=jax.ShapeDtypeStruct((slots, pred.shape[1], cells), jnp.bfloat16),
        grid_spec=pltpu.PrefetchScalarGridSpec(
            num_scalar_prefetch=1,
            grid=(),
            in_specs=[pl.BlockSpec(memory_space=pltpu.HBM), whole, whole],
            out_specs=whole,
            scratch_shapes=[
                pltpu.VMEM((chunks, height, length), jnp.bfloat16),
                pltpu.SemaphoreType.DMA((chunks,)),
            ],
        ),
        compiler_params=pltpu.CompilerParams(vmem_limit_bytes=KERNEL_VMEM),
    )(slot_of, sensor, weight, pred)


def tile_call(mode, slot_of, arrived, sensor, weight, *observed):
    tiles, data_slots, length = sensor.shape
    _, samples, _ = arrived.shape
    height = PART if data_slots % PART == 0 else data_slots
    parts = data_slots // height
    outs = [jax.ShapeDtypeStruct((tiles, samples, data_slots), jnp.float32)]
    if mode == "forward":
        outs.append(jax.ShapeDtypeStruct((samples, data_slots), jnp.float32))
    else:
        outs.append(jax.ShapeDtypeStruct(arrived.shape, jnp.bfloat16))
    whole = pl.BlockSpec(memory_space=pltpu.VMEM)
    return pl.pallas_call(
        functools.partial(tile_kernel, mode),
        out_shape=outs,
        grid_spec=pltpu.PrefetchScalarGridSpec(
            num_scalar_prefetch=1,
            grid=(),
            in_specs=[whole, pl.BlockSpec(memory_space=pltpu.HBM), whole]
            + [whole] * len(observed),
            out_specs=[whole] * len(outs),
            scratch_shapes=[
                pltpu.VMEM((tiles, samples, length), jnp.bfloat16),
                pltpu.VMEM((tiles * parts, height, length), jnp.bfloat16),
                pltpu.SemaphoreType.DMA((tiles * parts,)),
            ],
        ),
        compiler_params=pltpu.CompilerParams(vmem_limit_bytes=KERNEL_VMEM),
    )(slot_of, arrived, sensor, weight, *observed)


def sum_kernel(first, layers, ids_ref, arrived_ref, active_ref, reg_ref, *refs):
    if first:
        data_ref, grad_ref, reply_ref, norm_ref, *refs = refs
        rims, (total, reg, grad, sems) = (refs[:4], refs[4:])
    else:
        base_ref, step_ref, grad_ref, reply_ref, norm_ref, *refs = refs
        rims, (total, reg, grad, sems, base) = (refs[:4], refs[4:])
        step = step_ref[...]
    count = ids_ref.shape[0]
    bricks = grad.shape[0]
    rows = bricks // layers
    group = 8
    loads = [pltpu.make_async_copy(reg_ref, reg, sems.at[0])]
    if not first:
        loads.append(pltpu.make_async_copy(base_ref, base, sems.at[1]))
    for load in loads:
        load.start()
    total[...] = jnp.zeros_like(total)

    def add(i, carry):
        for k in range(group):
            j = i * group + k
            row = ids_ref[j]
            total[row] += arrived_ref[j].astype(jnp.float32)
        return carry

    lax.fori_loop(0, count // group, add, 0)
    for load in loads:
        load.wait()

    def combine(i, norm):
        live = active_ref[pl.ds(pl.multiple_of(i * group, group), group), :]
        for k in range(group):
            j = i * group + k
            data = total[j]
            if not first:
                data = base[j] - step * data
            value = live[k : k + 1] * data + reg[j]
            grad[j] = value
            norm = norm + value * value
        return norm

    norm = lax.fori_loop(0, bricks // group, combine, jnp.zeros(norm_ref.shape, jnp.float32))
    norm_ref[...] = norm
    stores = [pltpu.make_async_copy(grad, grad_ref, sems.at[2])]
    if first:
        stores.append(pltpu.make_async_copy(total, data_ref, sems.at[3]))
    for store in stores:
        store.start()

    def reply(i, carry):
        for k in range(group):
            j = i * group + k
            reply_ref[j] = grad[ids_ref[j]].astype(reply_ref.dtype)
        return carry

    lax.fori_loop(0, count // group, reply, 0)
    top, bottom, left, right = rims
    top[...] = grad[pl.ds(0, rows)].astype(top.dtype)
    bottom[...] = grad[pl.ds(bricks - rows, rows)].astype(bottom.dtype)
    for layer in range(layers):
        left[layer] = grad[layer * rows].astype(left.dtype)
        right[layer] = grad[layer * rows + rows - 1].astype(right.dtype)
    for store in stores:
        store.wait()


def sum_call(first, layers, ids, arrived, active, reg, *more):
    bricks, samples, cells = reg.shape
    field = jax.ShapeDtypeStruct((bricks, samples, cells), jnp.float32)
    whole = pl.BlockSpec(memory_space=pltpu.VMEM)
    apart = pl.BlockSpec(memory_space=pltpu.HBM)
    outs = [
        field,
        jax.ShapeDtypeStruct(arrived.shape, jnp.bfloat16),
        jax.ShapeDtypeStruct((samples, cells), jnp.float32),
    ]
    for length in (bricks // layers, bricks // layers, layers, layers):
        outs.append(jax.ShapeDtypeStruct((length, samples, cells), jnp.bfloat16))
    out_specs = [apart] + [whole] * (len(outs) - 1)
    in_specs = [whole, whole, apart]
    scratch = [pltpu.VMEM(field.shape, jnp.float32)] * 3 + [pltpu.SemaphoreType.DMA((4,))]
    if first:
        outs = [field] + outs
        out_specs = [apart] + out_specs
    else:
        scratch.append(pltpu.VMEM(field.shape, jnp.float32))
        in_specs = in_specs + [apart, whole]
    return pl.pallas_call(
        functools.partial(sum_kernel, first, layers),
        name="sum_first" if first else "sum_next",
        out_shape=outs,
        grid_spec=pltpu.PrefetchScalarGridSpec(
            num_scalar_prefetch=1,
            grid=(),
            in_specs=in_specs,
            out_specs=out_specs,
            scratch_shapes=scratch,
        ),
        compiler_params=pltpu.CompilerParams(vmem_limit_bytes=KERNEL_VMEM),
    )(ids, arrived, active, reg, *more)


def total_sums(owners, samples, *sums):
    packed = jnp.concatenate(sums)
    packed = jnp.pad(packed, (0, -packed.shape[0] % 128))
    sent = jnp.broadcast_to(packed[None, None, :], (owners, 1, packed.shape[0]))
    got = jnp.sum(swap(sent), axis=(0, 1))
    return [got[i * samples : (i + 1) * samples] for i in range(len(sums))]


def shards(
    sensitivity,
    observed,
    data_weight,
    data_counts,
    tile_bricks,
    start_model,
    active_cells,
    face_links,
    reg_weight,
):
    layers, strip_rows, samples, cells_x = start_model.shape
    tiles, tile_width = tile_bricks.shape
    data_slots = sensitivity.shape[1]
    owners = lax.axis_size("region") * lax.axis_size("survey")
    per_owner = layers * strip_rows
    capacity = max(2, 2 * tiles * tile_width // owners)
    slots = owners * capacity
    depth_count = layers * lax.axis_size("region")
    requests = tile_bricks.reshape(-1)
    owner_of = requests // per_owner
    local_of = requests % per_owner
    owner_hits = (owner_of[:, None] == jnp.arange(owners, dtype=jnp.int32)[None, :]).astype(
        jnp.int32
    )
    before = jnp.cumsum(owner_hits, axis=0) - owner_hits
    rank_of = jnp.sum(before * owner_hits, axis=1)
    slot_of = owner_of * capacity + rank_of
    slot_hits = slot_of[:, None] == jnp.arange(slots, dtype=jnp.int32)[None, :]
    asking = jnp.sum(jnp.where(slot_hits, local_of[:, None], 0), axis=0).reshape(owners, capacity)
    asked_ids = swap(asking).reshape(-1)

    active_rows = active_cells.astype(jnp.float32)
    active_flat = active_rows.reshape(per_owner, cells_x)
    links = face_links.reshape(per_owner, cells_x)
    base = (lax.axis_index("region") * layers).astype(jnp.int32).reshape(1)
    row_mask = (
        jnp.arange(data_slots, dtype=jnp.int32)[None, None, :] < data_counts[:, None, None]
    ).astype(jnp.float32)
    weight_sq = row_mask * (data_weight * data_weight)[:, None, :]
    reg_rows = jnp.broadcast_to(reg_weight[:, None], (samples, cells_x))

    model = start_model * active_rows[:, :, None, :]
    bricks = model.astype(jnp.bfloat16).reshape(per_owner, samples, cells_x)
    replies = bricks[asked_ids]

    def exchange(blocks):
        return swap(blocks.reshape(owners, capacity, samples, cells_x)).reshape(
            slots, samples, cells_x
        )

    def flat(field):
        return field.reshape(per_owner, samples, cells_x)

    def step_of(norm, data_curv, reg_curv):
        norm, data_curv, reg_curv = total_sums(
            owners, samples, jnp.sum(norm, axis=1), jnp.sum(data_curv, axis=1), reg_curv
        )
        return norm / (data_curv + reg_weight * reg_curv)

    grid = (depth_count, base, links, active_flat)
    arrived = exchange(replies)
    model_rims = edges(outer(model))
    predicted, buffer = tile_call("residual", slot_of, arrived, sensitivity, weight_sq, observed)

    arrived = exchange(buffer)
    (reg,) = reg_call(*grid, reg_rows, model, model_rims)
    data_sum, grad, replies, norm, *rims = sum_call(
        True, layers, asked_ids, arrived, active_flat, flat(reg)
    )
    arrived = exchange(replies)
    grad_rims = edges(rims)
    grad = grad.reshape(start_model.shape)
    reg_curv = curvature_call(*grid, model, model_rims, grad, grad_rims)
    step_pred, data_curv = tile_call("forward", slot_of, arrived, sensitivity, weight_sq)
    step = step_of(norm, data_curv, reg_curv)
    buffer = back_call(slot_of, slots, cells_x, sensitivity, weight_sq, step_pred)
    arrived = exchange(buffer)
    predicted = predicted - step[None, :, None] * step_pred

    step_rows = jnp.broadcast_to(step[:, None], (samples, cells_x))
    reg, model, *model_rims = reg_call(
        *grid, reg_rows, model, model_rims, (step_rows, grad, grad_rims)
    )
    grad, replies, norm, *rims = sum_call(
        False, layers, asked_ids, arrived, active_flat, flat(reg), data_sum, step_rows
    )
    arrived = exchange(replies)
    grad_rims = edges(rims, both=False)
    grad = grad.reshape(start_model.shape)
    reg_curv = curvature_call(*grid, model, model_rims, grad, grad_rims)
    step_pred, data_curv = tile_call("forward", slot_of, arrived, sensitivity, weight_sq)
    step = step_of(norm, data_curv, reg_curv)
    model = model - step[None, None, :, None] * grad
    predicted = predicted - step[None, :, None] * step_pred
    misfit = row_mask * data_weight[:, None, :] * (predicted - observed)
    return (model, misfit)


def solution(mesh):
    return jax.shard_map(
        shards,
        mesh=mesh,
        in_specs=(
            P(("region", "survey"), None, None),
            P(("region", "survey"), None, None),
            P(("region", "survey"), None),
            P(("region", "survey")),
            P(("region", "survey"), None),
            P("region", "survey", None, None),
            P("region", "survey", None),
            P("region", "survey", None),
            P(),
        ),
        out_specs=(P("region", "survey", None, None), P(("region", "survey"), None, None)),
        check_vma=False,
    )
```

```python
import functools

import jax
import jax.numpy as jnp
from jax import lax
from jax.experimental import pallas as pl
from jax.experimental.pallas import tpu as pltpu
from jax.sharding import PartitionSpec as P


AXES = ("region", "survey")
EPS_SQ = 0.09
KERNEL_VMEM = 32 * 1024 * 1024
PART = 256
GROUP = 8


def swap(field):
    return lax.all_to_all(field, AXES, split_axis=0, concat_axis=0, tiled=True)


def edges(parts, both=True):
    rims = [[], []]
    for axis, (first, last) in (("region", parts[:2]), ("survey", parts[2:])):
        count = lax.axis_size(axis)
        rims[0].append(lax.ppermute(first, axis, [(i + 1, i) for i in range(count - 1)]))
        if both:
            rims[1].append(lax.ppermute(last, axis, [(i, i + 1) for i in range(count - 1)]))
    return rims[0] + rims[1]


WHOLE = pl.BlockSpec(memory_space=pltpu.VMEM)
FAR = pl.BlockSpec(memory_space=pltpu.HBM)


def far(array):
    return pltpu.with_memory_space_constraint(array, pltpu.HBM)


def kernel_call(kernel, table, near, distant, outs, distant_outs, scratch):
    near_specs = [WHOLE] * len(near)
    out_shapes = [pltpu.HBM(o.shape, o.dtype) for o in (*outs, *distant_outs)]
    return pl.pallas_call(
        kernel,
        out_shape=out_shapes,
        grid_spec=pltpu.PrefetchScalarGridSpec(
            num_scalar_prefetch=1,
            grid=(),
            in_specs=near_specs + [FAR] * len(distant),
            out_specs=[pl.BlockSpec(o.shape, functools.partial(origin, o.ndim)) for o in outs]
            + [FAR] * len(distant_outs),
            scratch_shapes=scratch,
        ),
        compiler_params=pltpu.CompilerParams(vmem_limit_bytes=KERNEL_VMEM),
    )(table, *near, *[far(d) for d in distant])


def origin(ndim, *_):
    return (0,) * ndim


def shape_of(dtype, *shape):
    return jax.ShapeDtypeStruct(shape, dtype)


def held(arrays):
    return [pltpu.VMEM(a.shape, a.dtype) for a in arrays] + [
        pltpu.SemaphoreType.DMA((len(arrays),))
    ]


def start_all(sources, targets, sems):
    copies = [
        pltpu.make_async_copy(source, target, sems.at[i])
        for i, (source, target) in enumerate(zip(sources, targets))
    ]
    for copy in copies:
        copy.start()
    return copies


def wait_all(copies):
    for copy in copies:
        copy.wait()


def start_pads(field_ref, pad, sem):
    layers, rows = field_ref.shape[:2]
    copy = pltpu.make_async_copy(field_ref, pad.at[pl.ds(0, layers), pl.ds(0, rows)], sem)
    copy.start()
    return copy


def fill_pads(pad, below, right):
    layers, rows = (pad.shape[0] - 1, pad.shape[1] - 1)
    pad[layers, pl.ds(0, rows)] = below[...].astype(pad.dtype)
    for layer in range(layers):
        pad[layer, rows] = right[layer].astype(pad.dtype)


def face(here, there, link):
    difference = here - there
    return difference, link * lax.rsqrt(difference * difference + EPS_SQ)


def levels(base, layer, depth_count):
    depth = (base + layer).astype(jnp.float32)
    return [1.0 + (2.0 * depth + offset) / depth_count for offset in (-1.0, 0.0, 1.0)]


def link_of(codes, number, level):
    return (lax.shift_right_logical(codes, number) & 1).astype(jnp.float32) * level


def next_lane(value):
    return pltpu.roll(value, value.shape[-1] - 1, value.ndim - 1)


def inner_lanes(cells):
    lane = lax.broadcasted_iota(jnp.int32, (GROUP, cells), 1)
    return (lane < cells - 1).astype(jnp.float32)


def step_from(got_ref, scale):
    sums = jnp.sum(got_ref[...], axis=0)
    norm, data, faces = (sums[:, i : i + 1] for i in range(3))
    return jnp.broadcast_to(norm / (data + scale[:, :1] * faces), scale.shape)


def prepare_kernel(start_ref, active_ref, model_ref, low_ref, top, bottom, left, right):
    layer = pl.program_id(0)
    rows = start_ref.shape[1]
    for start in range(0, rows, GROUP):
        live = active_ref[0, pl.ds(start, GROUP), :]
        for k in range(GROUP):
            value = start_ref[0, start + k] * live[k : k + 1]
            model_ref[0, start + k] = value
            low_ref[0, start + k] = value.astype(jnp.bfloat16)
    left[0] = model_ref[0, 0]
    right[0] = model_ref[0, rows - 1]

    @pl.when(layer == 0)
    def _():
        top[...] = model_ref[0]

    @pl.when(layer == pl.num_programs(0) - 1)
    def _():
        bottom[...] = model_ref[0]


def prepare_call(start_model, active):
    layers, rows, samples, cells = start_model.shape
    block = pl.BlockSpec((1, rows, samples, cells), lambda i: (i, 0, 0, 0))
    layer = pl.BlockSpec((rows, samples, cells), lambda i: (0, 0, 0))
    column = pl.BlockSpec((1, samples, cells), lambda i: (i, 0, 0))
    outs = [
        (start_model.shape, jnp.float32),
        (start_model.shape, jnp.bfloat16),
        *[((rows, samples, cells), jnp.float32)] * 2,
        *[((layers, samples, cells), jnp.float32)] * 2,
    ]
    return pl.pallas_call(
        prepare_kernel,
        name="prepare",
        grid=(layers,),
        in_specs=[block, pl.BlockSpec((1, rows, cells), lambda i: (i, 0, 0))],
        out_specs=[block, block, layer, layer, column, column],
        out_shape=[pltpu.HBM(*o) for o in outs],
        compiler_params=pltpu.CompilerParams(vmem_limit_bytes=KERNEL_VMEM),
    )(far(start_model), far(active))


def reg_kernel(first, depth_count, base_ref, *refs):
    if not first:
        got_ref, *refs = refs
    small_refs, refs = (refs[: 7 if first else 11], refs[7 if first else 11 :])
    if first:
        field_ref, edge_z, edge_y, reg_ref, *refs = refs
        out, pad, flow, sems, *refs = refs
    else:
        field_ref, grad_ref, edge_z, edge_y, step_ref, reg_ref, new_ref, *refs = refs
        out, pad, flow, sems, gpad, *refs = refs
    small, small_sems = (refs[:-1], refs[-1])
    copies = [start_pads(field_ref, pad, sems.at[0])]
    if not first:
        copies.append(start_pads(grad_ref, gpad, sems.at[1]))
    wait_all(start_all(small_refs, small, small_sems))
    links_ref, active_ref, scale_ref, below, right, above, left = small[:7]
    layers, rows = field_ref.shape[:2]
    base = base_ref[0]
    scale = scale_ref[...]
    fill_pads(pad, below, right)
    if not first:
        gbelow, gright, gabove, gleft = small[7:]
        fill_pads(gpad, gbelow, gright)
        step = step_from(got_ref, scale)
        step_ref[...] = step
    wait_all(copies)
    if not first:

        def move(layer, carry):
            for row in range(rows + 1):
                pad[layer, row] = pad[layer, row] - step * gpad[layer, row]
            return carry

        lax.fori_loop(0, layers, move, 0)
        for row in range(rows):
            pad[layers, row] = pad[layers, row] - step * gpad[layers, row]
        store = pltpu.make_async_copy(
            pad.at[pl.ds(0, layers), pl.ds(0, rows)], new_ref, sems.at[2]
        )
        store.start()
    inner = inner_lanes(pad.shape[-1])

    def prior(ref, gref, index):
        value = ref[index]
        if first:
            return value
        return value - step * gref[index].astype(jnp.float32)

    for start in range(0, rows, GROUP):
        codes = links_ref[pl.ds(start, GROUP), :]
        link = link_of(codes, 0, levels(base, 0, depth_count)[0])
        for k in range(GROUP):
            row = start + k
            came = prior(above, None if first else gabove, row)
            difference, weight = face(came, pad[0, row], link[k : k + 1])
            flow[row] = weight * difference

    def one(layer, carry):
        _, level, level_below = levels(base, layer, depth_count)
        flow_y = None
        for start in range(0, rows, GROUP):
            place = pl.ds(pl.multiple_of(layer * rows + start, GROUP), GROUP)
            codes = links_ref[place, :]
            link_z = link_of(codes, 1, level_below)
            link_y = link_of(codes, 3, level)
            link_x = link_of(codes, 5, level) * inner
            live = active_ref[place, :] * level
            if start == 0:
                came = prior(left, None if first else gleft, layer)
                link = link_of(codes, 2, level)
                difference, weight = face(came, pad[layer, 0], link[:1])
                flow_y = weight * difference
            for k in range(GROUP):
                row = start + k
                one_row = slice(k, k + 1)
                here = pad[layer, row]
                total = live[one_row] * lax.rsqrt(here * here + EPS_SQ) * here
                difference, weight = face(here, next_lane(here), link_x[one_row])
                flow_x = weight * difference
                total = total + flow_x - pltpu.roll(flow_x, 1, 1)
                difference, weight = face(here, pad[layer, row + 1], link_y[one_row])
                if row == rows - 1:
                    edge_y[layer] = weight
                out_y = weight * difference
                total = total + out_y - flow_y
                flow_y = out_y
                difference, weight = face(here, pad[layer + 1, row], link_z[one_row])
                edge_z[row] = weight
                out_z = weight * difference
                total = total + out_z - flow[row]
                flow[row] = out_z
                out[layer, row] = scale * total
        return carry

    lax.fori_loop(0, layers, one, 0)
    final = pltpu.make_async_copy(out, reg_ref, sems.at[3])
    final.start()
    final.wait()
    if not first:
        store.wait()


def reg_call(depth_count, base, links, active, scale, field, rims, moved=()):
    layers, rows, samples, cells = field.shape
    f32 = jnp.float32
    pad = pltpu.VMEM((layers + 1, rows + 1, samples, cells), f32)
    scratch = [
        pltpu.VMEM(field.shape, f32),
        pad,
        pltpu.VMEM((rows, samples, cells), f32),
        pltpu.SemaphoreType.DMA((4,)),
    ]
    near = []
    small = [links, active, scale, *rims]
    distant = [field]
    outs = [shape_of(f32, rows, samples, cells), shape_of(f32, layers, samples, cells)]
    distant_outs = [shape_of(f32, *field.shape)]
    if moved:
        got, grad, grad_rims = moved
        near = [got]
        small += grad_rims
        distant.append(grad)
        scratch.append(pad)
        outs.append(shape_of(f32, samples, cells))
        distant_outs *= 2
    return kernel_call(
        functools.partial(reg_kernel, not moved, depth_count),
        base,
        near,
        small + distant,
        outs,
        distant_outs,
        scratch + held(small),
    )


def curvature_kernel(
    depth_count, base_ref, links_ref, active_ref, field_ref, grad_ref, curv_ref, *refs
):
    links, active, field, grad, sems = refs
    layers, rows = field.shape[:2]
    base = base_ref[0]
    wait_all(
        start_all((field_ref, grad_ref, links_ref, active_ref), (field, grad, links, active), sems)
    )
    inner = inner_lanes(field.shape[-1])

    def one(layer, total):
        _, level, level_below = levels(base, layer, depth_count)
        below = jnp.minimum(layer + 1, layers - 1)
        level_below = jnp.where(layer + 1 < layers, level_below, 0.0)
        for start in range(0, rows, GROUP):
            place = pl.ds(pl.multiple_of(layer * rows + start, GROUP), GROUP)
            codes = links[place, :]
            link_z = link_of(codes, 1, level_below)
            link_y = link_of(codes, 3, level)
            link_x = link_of(codes, 5, level) * inner
            live = active[place, :] * level
            for k in range(GROUP):
                row = start + k
                one_row = slice(k, k + 1)
                here = field[layer, row]
                slope = grad[layer, row]
                part = live[one_row] * lax.rsqrt(here * here + EPS_SQ) * slope * slope
                pairs = [
                    (next_lane(here), next_lane(slope), link_x),
                    (field[below, row], grad[below, row], link_z),
                ]
                if row + 1 < rows:
                    pairs.append((field[layer, row + 1], grad[layer, row + 1], link_y))
                for there, gthere, link in pairs:
                    _, weight = face(here, there, link[one_row])
                    change = slope - gthere
                    part = part + weight * change * change
                total = total + part
        return total

    curv_ref[...] = lax.fori_loop(0, layers, one, jnp.zeros(curv_ref.shape, jnp.float32))


def curvature_call(depth_count, base, links, active, field, grad):
    (curv,) = kernel_call(
        functools.partial(curvature_kernel, depth_count),
        base,
        [],
        [links, active, field, grad],
        [shape_of(jnp.float32, *field.shape[2:])],
        [],
        held([links, active, field, grad]),
    )
    return curv


def load_sensors(sensor_ref, held_ref, sems, parts):
    height = held_ref.shape[1]
    copies = []
    for chunk in range(held_ref.shape[0]):
        rows = pl.ds(chunk % parts * height, height)
        copies.append(
            pltpu.make_async_copy(
                sensor_ref.at[chunk // parts, rows], held_ref.at[chunk], sems.at[chunk]
            )
        )
        copies[-1].start()


def wait_part(sensor_ref, held_ref, sems, tile, part, parts):
    height = held_ref.shape[1]
    chunk = tile * parts + part
    rows = pl.ds(part * height, height)
    pltpu.make_async_copy(
        sensor_ref.at[tile, rows], held_ref.at[chunk], sems.at[chunk]
    ).wait()


def gather_rows(width, slot_ref, arrived_ref, rows_ref):
    cells = arrived_ref.shape[2]

    def one(tile, carry):
        for entry in range(width):
            slot = slot_ref[tile * width + entry]
            rows_ref[tile, :, entry * cells : (entry + 1) * cells] = arrived_ref[slot]
        return carry

    lax.fori_loop(0, rows_ref.shape[0], one, 0)


def scatter_rows(tile, width, slot_ref, blocks, buffer_ref):
    cells = buffer_ref.shape[2]
    for entry in range(width):
        slot = slot_ref[tile * width + entry]
        block = blocks[:, entry * cells : (entry + 1) * cells]
        buffer_ref[slot] = block.astype(buffer_ref.dtype)


def project(rows, sensor):
    return lax.dot_general(
        rows, sensor, (((1,), (1,)), ((), ())), preferred_element_type=jnp.float32
    )


def forward_tile(tile, weight_of, rows_ref, held_ref, sensor_ref, sems, pred_ref, parts):
    height = held_ref.shape[1]
    given = []
    for part in range(parts):
        span = slice(part * height, (part + 1) * height)
        wait_part(sensor_ref, held_ref, sems, tile, part, parts)
        pred = project(rows_ref[tile], held_ref[tile * parts + part])
        pred_ref[tile, :, span] = pred
        given.append(weight_of(span, pred))
    return given


def backward_tile(tile, sent, held_ref, parts):
    blocks = 0.0
    for part in range(parts):
        blocks += jnp.dot(
            sent[part], held_ref[tile * parts + part], preferred_element_type=jnp.float32
        )
    return blocks


def residual_kernel(slot_ref, arrived_ref, sensor_ref, *refs):
    small_refs, refs = (refs[:2], refs[2:])
    pred_ref, buffer_ref, rows_ref, held_ref, sems, *small, small_sems = refs
    tiles = pred_ref.shape[0]
    parts = held_ref.shape[0] // tiles
    width = slot_ref.shape[0] // tiles
    copies = start_all(small_refs, small, small_sems)
    load_sensors(sensor_ref, held_ref, sems, parts)
    buffer_ref[...] = jnp.zeros_like(buffer_ref)
    gather_rows(width, slot_ref, arrived_ref, rows_ref)
    wait_all(copies)
    weight, observed = small

    def one(tile, carry):
        def weight_of(span, pred):
            residual = pred - observed[tile, :, span]
            return (weight[tile, :, span] * residual).astype(jnp.bfloat16)

        sent = forward_tile(
            tile, weight_of, rows_ref, held_ref, sensor_ref, sems, pred_ref, parts
        )
        blocks = backward_tile(tile, sent, held_ref, parts)
        scatter_rows(tile, width, slot_ref, blocks, buffer_ref)
        return carry

    lax.fori_loop(0, tiles, one, 0)


def forward_kernel(slot_ref, arrived_ref, sensor_ref, *refs):
    small_refs, refs = (refs[:9], refs[9:])
    pred_ref, sent_ref, rows_ref, held_ref, sems, *small, small_sems = refs
    tiles, samples = pred_ref.shape[:2]
    parts = held_ref.shape[0] // tiles
    width = slot_ref.shape[0] // tiles
    copies = start_all(small_refs, small, small_sems)
    load_sensors(sensor_ref, held_ref, sems, parts)
    gather_rows(width, slot_ref, arrived_ref, rows_ref)
    wait_all(copies)
    weight, norm, faces, *rims = small
    total = faces[...]
    for edge, mine, theirs in (rims[:3], rims[3:]):
        for row in range(edge.shape[0]):
            change = mine[row].astype(jnp.float32) - theirs[row].astype(jnp.float32)
            total = total + edge[row] * change * change

    def one(tile, curv):
        def weight_of(span, pred):
            return jnp.sum(weight[tile, :, span] * pred * pred, axis=1, keepdims=True)

        given = forward_tile(
            tile, weight_of, rows_ref, held_ref, sensor_ref, sems, pred_ref, parts
        )
        return curv + sum(given)

    data = lax.fori_loop(0, tiles, one, jnp.zeros((samples, 1), jnp.float32))
    sums = [jnp.sum(norm[...], axis=1, keepdims=True), data, jnp.sum(total, axis=1, keepdims=True)]
    lane = lax.broadcasted_iota(jnp.int32, total.shape, 1)
    block = jnp.zeros(total.shape, jnp.float32)
    for i, value in enumerate(sums):
        block = jnp.where(lane == i, value, block)
    sent_ref[...] = jnp.broadcast_to(block[None], sent_ref.shape)


def backward_kernel(slot_ref, sensor_ref, *refs):
    small_refs, refs = (refs[:2], refs[2:])
    buffer_ref, held_ref, sems, *small, small_sems = refs
    weight, pred = small
    tiles, samples = pred.shape[:2]
    height = held_ref.shape[1]
    parts = held_ref.shape[0] // tiles
    width = slot_ref.shape[0] // tiles
    copies = start_all(small_refs, small, small_sems)
    load_sensors(sensor_ref, held_ref, sems, parts)
    buffer_ref[...] = jnp.zeros_like(buffer_ref)
    wait_all(copies)

    def one(tile, carry):
        weighted = weight[tile] * pred[tile]
        upper = weighted.astype(jnp.bfloat16).astype(jnp.float32)
        both = jnp.concatenate([upper, weighted - upper], axis=0).astype(jnp.bfloat16)
        sent = [both[:, part * height : (part + 1) * height] for part in range(parts)]
        for part in range(parts):
            wait_part(sensor_ref, held_ref, sems, tile, part, parts)
        blocks = backward_tile(tile, sent, held_ref, parts)
        scatter_rows(tile, width, slot_ref, blocks[:samples] + blocks[samples:], buffer_ref)
        return carry

    lax.fori_loop(0, tiles, one, 0)


def tile_call(kernel, slot_of, near, sensor, small, outs, samples):
    tiles, data_slots, length = sensor.shape
    height = PART if data_slots % PART == 0 else data_slots
    chunks = tiles * data_slots // height
    scratch = [
        pltpu.VMEM((chunks, height, length), jnp.bfloat16),
        pltpu.SemaphoreType.DMA((chunks,)),
    ]
    if near:
        scratch = [pltpu.VMEM((tiles, samples, length), jnp.bfloat16)] + scratch
    return kernel_call(kernel, slot_of, near, [sensor, *small], outs, [], scratch + held(small))


def sum_kernel(first, layers, ids_ref, arrived_ref, *refs):
    active_ref, reg_ref, *refs = refs
    if not first:
        base_ref, step_ref, *refs = refs
    reply_ref, norm_ref, top, bottom, left, right, grad_ref, *refs = refs
    if first:
        data_ref, *refs = refs
        total, grad, out_sems, active, reg, sems = refs
        sources, targets = ((active_ref, reg_ref), (active, reg))
    else:
        total, grad, out_sems, active, reg, base, step_rows, sems = refs
        sources = (active_ref, reg_ref, base_ref, step_ref)
        targets = (active, reg, base, step_rows)
    copies = start_all(sources, targets, sems)
    count = ids_ref.shape[0]
    bricks = grad.shape[0]
    rows = bricks // layers
    total[...] = jnp.zeros_like(total)

    def add(i, carry):
        for k in range(GROUP):
            j = i * GROUP + k
            row = ids_ref[j]
            total[row] += arrived_ref[j].astype(jnp.float32)
        return carry

    lax.fori_loop(0, count // GROUP, add, 0)
    wait_all(copies)
    if not first:
        step = step_rows[...]

    def combine(i, norm):
        live = active[pl.ds(pl.multiple_of(i * GROUP, GROUP), GROUP), :]
        for k in range(GROUP):
            j = i * GROUP + k
            data = total[j]
            if not first:
                data = base[j] - step * data
            value = live[k : k + 1] * data + reg[j]
            grad[j] = value
            norm = norm + value * value
        return norm

    norm = lax.fori_loop(0, bricks // GROUP, combine, jnp.zeros(norm_ref.shape, jnp.float32))
    norm_ref[...] = norm
    if first:
        stores = start_all((grad, total), (grad_ref, data_ref), out_sems)
    else:
        stores = start_all((grad,), (grad_ref,), out_sems)

    def reply(i, carry):
        for k in range(GROUP):
            j = i * GROUP + k
            reply_ref[j] = grad[ids_ref[j]].astype(reply_ref.dtype)
        return carry

    lax.fori_loop(0, count // GROUP, reply, 0)
    top[...] = grad[pl.ds(0, rows)].astype(top.dtype)
    bottom[...] = grad[pl.ds(bricks - rows, rows)].astype(bottom.dtype)
    for layer in range(layers):
        left[layer] = grad[layer * rows].astype(left.dtype)
        right[layer] = grad[layer * rows + rows - 1].astype(right.dtype)
    wait_all(stores)


def sum_call(first, layers, ids, arrived, active, reg, *more):
    bricks, samples, cells = reg.shape
    small = [active, reg, *more]
    field = shape_of(jnp.float32, bricks, samples, cells)
    outs = [shape_of(jnp.bfloat16, *arrived.shape), shape_of(jnp.float32, samples, cells)]
    for length in (bricks // layers, bricks // layers, layers, layers):
        outs.append(shape_of(jnp.bfloat16, length, samples, cells))
    scratch = [
        pltpu.VMEM(field.shape, jnp.float32),
        pltpu.VMEM(field.shape, jnp.float32),
        pltpu.SemaphoreType.DMA((2 if first else 1,)),
    ]
    return kernel_call(
        functools.partial(sum_kernel, first, layers),
        ids,
        [arrived],
        small,
        outs,
        [field, field] if first else [field],
        scratch + held(small),
    )


def finish_kernel(
    got_ref, scale_ref, before_ref, mask_ref, observed_ref, pred_ref, moved_ref, last_ref,
    field_ref, grad_ref, model_ref, misfit_ref
):
    step = step_from(got_ref, scale_ref[...])
    model_ref[...] = field_ref[...] - step[None, None] * grad_ref[...]

    @pl.when(pl.program_id(0) == 0)
    def _():
        for tile in range(pred_ref.shape[0]):
            pred = pred_ref[tile] - before_ref[:, :1] * moved_ref[tile]
            pred = pred - step[:, :1] * last_ref[tile]
            misfit_ref[tile] = mask_ref[tile] * (pred - observed_ref[tile])


def finish_call(got, scale, before, mask, observed, pred, moved, last, field, grad):
    layers, rows, samples, cells = field.shape
    block = 4 if layers % 4 == 0 else 1
    spec = pl.BlockSpec((block, rows, samples, cells), lambda i: (i, 0, 0, 0))

    def fixed(array):
        return pl.BlockSpec(array.shape, lambda i: (0,) * array.ndim)

    small = [scale, before, mask, observed, pred, moved, last]
    return pl.pallas_call(
        finish_kernel,
        name="finish",
        grid=(layers // block,),
        in_specs=[WHOLE] + [fixed(a) for a in small] + [spec, spec],
        out_specs=[spec, fixed(observed)],
        out_shape=[pltpu.HBM(a.shape, a.dtype) for a in (field, observed)],
        compiler_params=pltpu.CompilerParams(vmem_limit_bytes=KERNEL_VMEM),
    )(got, *[far(a) for a in (*small, field, grad)])


def shards(
    sensitivity,
    observed,
    data_weight,
    data_counts,
    tile_bricks,
    start_model,
    active_cells,
    face_links,
    reg_weight,
):
    layers, strip_rows, samples, cells_x = start_model.shape
    tiles, tile_width = tile_bricks.shape
    data_slots = sensitivity.shape[1]
    owners = lax.axis_size("region") * lax.axis_size("survey")
    per_owner = layers * strip_rows
    capacity = max(2, 2 * tiles * tile_width // owners)
    slots = owners * capacity
    depth_count = layers * lax.axis_size("region")
    requests = tile_bricks.reshape(-1)
    owner_of = requests // per_owner
    local_of = requests % per_owner
    owner_hits = (owner_of[:, None] == jnp.arange(owners, dtype=jnp.int32)[None, :]).astype(
        jnp.int32
    )
    before = jnp.cumsum(owner_hits, axis=0) - owner_hits
    rank_of = jnp.sum(before * owner_hits, axis=1)
    slot_of = owner_of * capacity + rank_of
    slot_hits = slot_of[:, None] == jnp.arange(slots, dtype=jnp.int32)[None, :]
    asking = jnp.sum(jnp.where(slot_hits, local_of[:, None], 0), axis=0).reshape(owners, capacity)
    asked_ids = swap(asking).reshape(-1)

    active_rows = active_cells.astype(jnp.float32)
    active_flat = active_rows.reshape(per_owner, cells_x)
    links = face_links.reshape(per_owner, cells_x)
    base = (lax.axis_index("region") * layers).astype(jnp.int32).reshape(1)
    row_mask = (
        jnp.arange(data_slots, dtype=jnp.int32)[None, None, :] < data_counts[:, None, None]
    ).astype(jnp.float32)
    weight_sq = row_mask * (data_weight * data_weight)[:, None, :]
    mask = row_mask * data_weight[:, None, :]
    reg_rows = jnp.broadcast_to(reg_weight[:, None], (samples, cells_x))
    f32, bf16 = (jnp.float32, jnp.bfloat16)
    pred_shape = shape_of(f32, tiles, samples, data_slots)
    buffer_shape = shape_of(bf16, slots, samples, cells_x)

    def exchange(blocks):
        return swap(blocks.reshape(owners, capacity, samples, cells_x)).reshape(
            slots, samples, cells_x
        )

    def flat(field):
        return field.reshape(per_owner, samples, cells_x)

    def forward(arrived, norm, faces, edge_z, edge_y, rims, theirs):
        small = [weight_sq, norm, faces, edge_z, rims[1], theirs[0], edge_y, rims[3], theirs[1]]
        outs = [pred_shape, shape_of(f32, owners, samples, cells_x)]
        return tile_call(forward_kernel, slot_of, [arrived], sensitivity, small, outs, samples)

    grid = (depth_count, base, links, active_flat)
    model, bricks, *rims = prepare_call(start_model, active_rows)
    replies = flat(bricks)[asked_ids]
    arrived = exchange(replies)
    model_rims = edges(rims)
    pred, buffer = tile_call(
        residual_kernel,
        slot_of,
        [arrived],
        sensitivity,
        [weight_sq, observed],
        [pred_shape, buffer_shape],
        samples,
    )

    arrived = exchange(buffer)
    edge_z, edge_y, reg = reg_call(*grid, reg_rows, model, model_rims)
    replies, norm, *rims, grad, data_sum = sum_call(
        True, layers, asked_ids, arrived, active_flat, flat(reg)
    )
    arrived = exchange(replies)
    grad_rims = edges(rims)
    grad = grad.reshape(start_model.shape)
    faces = curvature_call(*grid, model, grad)
    step_pred, sums = forward(arrived, norm, faces, edge_z, edge_y, rims, grad_rims)
    got = swap(sums)
    (buffer,) = tile_call(
        backward_kernel, slot_of, [], sensitivity, [weight_sq, step_pred], [buffer_shape], samples
    )
    arrived = exchange(buffer)

    edge_z, edge_y, step, reg, model = reg_call(
        *grid, reg_rows, model, model_rims, (got, grad, grad_rims)
    )
    replies, norm, *rims, grad = sum_call(
        False, layers, asked_ids, arrived, active_flat, flat(reg), data_sum, step
    )
    arrived = exchange(replies)
    grad_rims = edges(rims, both=False)
    grad = grad.reshape(start_model.shape)
    faces = curvature_call(*grid, model, grad)
    last_pred, sums = forward(arrived, norm, faces, edge_z, edge_y, rims, grad_rims)
    got = swap(sums)
    return tuple(
        finish_call(got, reg_rows, step, mask, observed, pred, step_pred, last_pred, model, grad)
    )


def solution(mesh):
    return jax.shard_map(
        shards,
        mesh=mesh,
        in_specs=(
            P(("region", "survey"), None, None),
            P(("region", "survey"), None, None),
            P(("region", "survey"), None),
            P(("region", "survey")),
            P(("region", "survey"), None),
            P("region", "survey", None, None),
            P("region", "survey", None),
            P("region", "survey", None),
            P(),
        ),
        out_specs=(P("region", "survey", None, None), P(("region", "survey"), None, None)),
        check_vma=False,
    )
```

```python
import functools

import jax
import jax.numpy as jnp
from jax import lax
from jax.experimental import pallas as pl
from jax.experimental.pallas import tpu as pltpu
from jax.sharding import PartitionSpec as P


AXES = ("region", "survey")
EPS_SQ = 0.09
KERNEL_VMEM = 32 * 1024 * 1024
PARTS = {"residual": 1, "forward": 4, "backward": 2}
GROUP = 8


def swap(field):
    return lax.all_to_all(field, AXES, split_axis=0, concat_axis=0, tiled=True)


def edges(parts, both=True):
    rims = [[], []]
    for axis, (first, last) in (("region", parts[:2]), ("survey", parts[2:])):
        count = lax.axis_size(axis)
        rims[0].append(lax.ppermute(first, axis, [(i + 1, i) for i in range(count - 1)]))
        if both:
            rims[1].append(lax.ppermute(last, axis, [(i, i + 1) for i in range(count - 1)]))
    return rims[0] + rims[1]


WHOLE = pl.BlockSpec(memory_space=pltpu.VMEM)
FAR = pl.BlockSpec(memory_space=pltpu.HBM)


def far(array):
    return pltpu.with_memory_space_constraint(array, pltpu.HBM)


def kernel_call(kernel, table, near, distant, outs, distant_outs, scratch):
    near_specs = [WHOLE] * len(near)
    out_shapes = [pltpu.HBM(o.shape, o.dtype) for o in (*outs, *distant_outs)]
    return pl.pallas_call(
        kernel,
        out_shape=out_shapes,
        grid_spec=pltpu.PrefetchScalarGridSpec(
            num_scalar_prefetch=1,
            grid=(),
            in_specs=near_specs + [FAR] * len(distant),
            out_specs=[pl.BlockSpec(o.shape, functools.partial(origin, o.ndim)) for o in outs]
            + [FAR] * len(distant_outs),
            scratch_shapes=scratch,
        ),
        compiler_params=pltpu.CompilerParams(vmem_limit_bytes=KERNEL_VMEM),
    )(table, *near, *[far(d) for d in distant])


def origin(ndim, *_):
    return (0,) * ndim


def shape_of(dtype, *shape):
    return jax.ShapeDtypeStruct(shape, dtype)


def held(arrays):
    return [pltpu.VMEM(a.shape, a.dtype) for a in arrays] + [
        pltpu.SemaphoreType.DMA((len(arrays),))
    ]


def start_all(sources, targets, sems):
    copies = [
        pltpu.make_async_copy(source, target, sems.at[i])
        for i, (source, target) in enumerate(zip(sources, targets))
    ]
    for copy in copies:
        copy.start()
    return copies


def wait_all(copies):
    for copy in copies:
        copy.wait()


def start_pads(field_ref, pad, sem):
    layers, rows = field_ref.shape[:2]
    copy = pltpu.make_async_copy(field_ref, pad.at[pl.ds(0, layers), pl.ds(0, rows)], sem)
    copy.start()
    return copy


def fill_pads(pad, below, right):
    layers, rows = (pad.shape[0] - 1, pad.shape[1] - 1)
    pad[layers, pl.ds(0, rows)] = below[...].astype(pad.dtype)
    for layer in range(layers):
        pad[layer, rows] = right[layer].astype(pad.dtype)


def face(here, there, link):
    difference = here - there
    return difference, link * lax.rsqrt(difference * difference + EPS_SQ)


def levels(base, layer, depth_count):
    depth = (base + layer).astype(jnp.float32)
    return [1.0 + (2.0 * depth + offset) / depth_count for offset in (-1.0, 0.0, 1.0)]


def link_of(codes, number, level):
    return (lax.shift_right_logical(codes, number) & 1).astype(jnp.float32) * level


def next_lane(value):
    return pltpu.roll(value, value.shape[-1] - 1, value.ndim - 1)


def inner_lanes(cells):
    lane = lax.broadcasted_iota(jnp.int32, (GROUP, cells), 1)
    return (lane < cells - 1).astype(jnp.float32)


def step_from(got_ref, scale):
    sums = jnp.sum(got_ref[...], axis=0)
    norm, data, faces = (sums[:, i : i + 1] for i in range(3))
    return jnp.broadcast_to(norm / (data + scale[:, :1] * faces), scale.shape)


def prepare_kernel(start_ref, active_ref, model_ref, low_ref, top, bottom, left, right):
    block, rows = start_ref.shape[:2]

    def one(layer, carry):
        for start in range(0, rows, GROUP):
            live = active_ref[layer, pl.ds(start, GROUP), :].astype(jnp.float32)
            for k in range(GROUP):
                value = start_ref[layer, start + k] * live[k : k + 1]
                model_ref[layer, start + k] = value
                low_ref[layer, start + k] = value.astype(jnp.bfloat16)
        left[layer] = model_ref[layer, 0]
        right[layer] = model_ref[layer, rows - 1]
        return carry

    lax.fori_loop(0, block, one, 0)

    @pl.when(pl.program_id(0) == 0)
    def _():
        top[...] = model_ref[0]

    @pl.when(pl.program_id(0) == pl.num_programs(0) - 1)
    def _():
        bottom[...] = model_ref[block - 1]


def prepare_call(start_model, active):
    layers, rows, samples, cells = start_model.shape
    step = 4 if layers % 4 == 0 else 1
    block = pl.BlockSpec((step, rows, samples, cells), lambda i: (i, 0, 0, 0))
    layer = pl.BlockSpec((rows, samples, cells), lambda i: (0, 0, 0))
    column = pl.BlockSpec((step, samples, cells), lambda i: (i, 0, 0))
    outs = [
        (start_model.shape, jnp.float32),
        (start_model.shape, jnp.bfloat16),
        *[((rows, samples, cells), jnp.float32)] * 2,
        *[((layers, samples, cells), jnp.float32)] * 2,
    ]
    return pl.pallas_call(
        prepare_kernel,
        name="prepare",
        grid=(layers // step,),
        in_specs=[block, pl.BlockSpec((step, rows, cells), lambda i: (i, 0, 0))],
        out_specs=[block, block, layer, layer, column, column],
        out_shape=[
            jax.ShapeDtypeStruct(*o) if o[1] == jnp.bfloat16 else pltpu.HBM(*o) for o in outs
        ],
        compiler_params=pltpu.CompilerParams(vmem_limit_bytes=KERNEL_VMEM),
    )(far(start_model), far(active))


def reg_kernel(first, depth_count, base_ref, *refs):
    if not first:
        got_ref, *refs = refs
    small_refs, refs = (refs[: 7 if first else 11], refs[7 if first else 11 :])
    if first:
        field_ref, edge_z, edge_y, reg_ref, *refs = refs
        out, pad, flow, sems, *refs = refs
    else:
        field_ref, grad_ref, edge_z, edge_y, step_ref, reg_ref, new_ref, *refs = refs
        out, pad, flow, sems, gpad, *refs = refs
    small, small_sems = (refs[:-1], refs[-1])
    copies = [start_pads(field_ref, pad, sems.at[0])]
    if not first:
        copies.append(start_pads(grad_ref, gpad, sems.at[1]))
    wait_all(start_all(small_refs, small, small_sems))
    links_ref, active_ref, scale_ref, below, right, above, left = small[:7]
    layers, rows = field_ref.shape[:2]
    base = base_ref[0]
    scale = scale_ref[...]
    fill_pads(pad, below, right)
    if not first:
        gbelow, gright, gabove, gleft = small[7:]
        fill_pads(gpad, gbelow, gright)
        step = step_from(got_ref, scale)
        step_ref[...] = step
    wait_all(copies)
    if not first:

        def move(layer, carry):
            for row in range(rows + 1):
                pad[layer, row] = pad[layer, row] - step * gpad[layer, row]
            return carry

        lax.fori_loop(0, layers, move, 0)
        for row in range(rows):
            pad[layers, row] = pad[layers, row] - step * gpad[layers, row]
        store = pltpu.make_async_copy(
            pad.at[pl.ds(0, layers), pl.ds(0, rows)], new_ref, sems.at[2]
        )
        store.start()
    inner = inner_lanes(pad.shape[-1])

    def prior(ref, gref, index):
        value = ref[index]
        if first:
            return value
        return value - step * gref[index].astype(jnp.float32)

    for start in range(0, rows, GROUP):
        codes = links_ref[pl.ds(start, GROUP), :]
        link = link_of(codes, 0, levels(base, 0, depth_count)[0])
        for k in range(GROUP):
            row = start + k
            came = prior(above, None if first else gabove, row)
            difference, weight = face(came, pad[0, row], link[k : k + 1])
            flow[row] = weight * difference

    def one(layer, carry):
        _, level, level_below = levels(base, layer, depth_count)
        flow_y = None
        for start in range(0, rows, GROUP):
            place = pl.ds(pl.multiple_of(layer * rows + start, GROUP), GROUP)
            codes = links_ref[place, :]
            link_z = link_of(codes, 1, level_below)
            link_y = link_of(codes, 3, level)
            link_x = link_of(codes, 5, level) * inner
            live = active_ref[place, :].astype(jnp.float32) * level
            if start == 0:
                came = prior(left, None if first else gleft, layer)
                link = link_of(codes, 2, level)
                difference, weight = face(came, pad[layer, 0], link[:1])
                flow_y = weight * difference
            for k in range(GROUP):
                row = start + k
                one_row = slice(k, k + 1)
                here = pad[layer, row]
                total = live[one_row] * lax.rsqrt(here * here + EPS_SQ) * here
                difference, weight = face(here, next_lane(here), link_x[one_row])
                flow_x = weight * difference
                total = total + flow_x - pltpu.roll(flow_x, 1, 1)
                difference, weight = face(here, pad[layer, row + 1], link_y[one_row])
                if row == rows - 1:
                    edge_y[layer] = weight
                out_y = weight * difference
                total = total + out_y - flow_y
                flow_y = out_y
                difference, weight = face(here, pad[layer + 1, row], link_z[one_row])
                edge_z[row] = weight
                out_z = weight * difference
                total = total + out_z - flow[row]
                flow[row] = out_z
                out[layer, row] = scale * total
        return carry

    lax.fori_loop(0, layers, one, 0)
    final = pltpu.make_async_copy(out, reg_ref, sems.at[3])
    final.start()
    final.wait()
    if not first:
        store.wait()


def reg_call(depth_count, base, links, active, scale, field, rims, moved=()):
    layers, rows, samples, cells = field.shape
    f32 = jnp.float32
    pad = pltpu.VMEM((layers + 1, rows + 1, samples, cells), f32)
    scratch = [
        pltpu.VMEM(field.shape, f32),
        pad,
        pltpu.VMEM((rows, samples, cells), f32),
        pltpu.SemaphoreType.DMA((4,)),
    ]
    near = []
    small = [links, active, scale, *rims]
    distant = [field]
    outs = [shape_of(f32, rows, samples, cells), shape_of(f32, layers, samples, cells)]
    distant_outs = [shape_of(f32, *field.shape)]
    if moved:
        got, grad, grad_rims = moved
        near = [got]
        small += grad_rims
        distant.append(grad)
        scratch.append(pad)
        outs.append(shape_of(f32, samples, cells))
        distant_outs *= 2
    return kernel_call(
        functools.partial(reg_kernel, not moved, depth_count),
        base,
        near,
        small + distant,
        outs,
        distant_outs,
        scratch + held(small),
    )


def curvature_kernel(
    depth_count, base_ref, links_ref, active_ref, field_ref, grad_ref, curv_ref, *refs
):
    links, active, field, grad, sems = refs
    layers, rows = field.shape[:2]
    base = base_ref[0]
    wait_all(
        start_all((field_ref, grad_ref, links_ref, active_ref), (field, grad, links, active), sems)
    )
    inner = inner_lanes(field.shape[-1])

    def one(layer, total):
        _, level, level_below = levels(base, layer, depth_count)
        below = jnp.minimum(layer + 1, layers - 1)
        level_below = jnp.where(layer + 1 < layers, level_below, 0.0)
        for start in range(0, rows, GROUP):
            place = pl.ds(pl.multiple_of(layer * rows + start, GROUP), GROUP)
            codes = links[place, :]
            link_z = link_of(codes, 1, level_below)
            link_y = link_of(codes, 3, level)
            link_x = link_of(codes, 5, level) * inner
            live = active[place, :].astype(jnp.float32) * level
            for k in range(GROUP):
                row = start + k
                one_row = slice(k, k + 1)
                here = field[layer, row]
                slope = grad[layer, row]
                part = live[one_row] * lax.rsqrt(here * here + EPS_SQ) * slope * slope
                pairs = [
                    (next_lane(here), next_lane(slope), link_x),
                    (field[below, row], grad[below, row], link_z),
                ]
                if row + 1 < rows:
                    pairs.append((field[layer, row + 1], grad[layer, row + 1], link_y))
                for there, gthere, link in pairs:
                    _, weight = face(here, there, link[one_row])
                    change = slope - gthere
                    part = part + weight * change * change
                total = total + part
        return total

    curv_ref[...] = lax.fori_loop(0, layers, one, jnp.zeros(curv_ref.shape, jnp.float32))


def curvature_call(depth_count, base, links, active, field, grad):
    (curv,) = kernel_call(
        functools.partial(curvature_kernel, depth_count),
        base,
        [],
        [links, active, field, grad],
        [shape_of(jnp.float32, *field.shape[2:])],
        [],
        held([links, active, field, grad]),
    )
    return curv


def sensor_copies(sensor_ref, held_ref, sems):
    tiles, _, length = held_ref.shape
    parts = sems.shape[1]
    columns = length // parts
    return [
        [
            pltpu.make_async_copy(
                sensor_ref.at[tile, :, pl.ds(part * columns, columns)],
                held_ref.at[tile, :, pl.ds(part * columns, columns)],
                sems.at[tile, part],
            )
            for part in range(parts)
        ]
        for tile in range(tiles)
    ]


def start_copies(copies, small):
    flat = [copy for tile in copies for copy in tile]
    flat[0].start()
    wait_all(small)
    for copy in flat[1:]:
        copy.start()


def gather_rows(width, slot_ref, arrived_ref, rows_ref):
    cells = arrived_ref.shape[2]

    def one(tile, carry):
        for entry in range(width):
            slot = slot_ref[tile * width + entry]
            rows_ref[tile, :, entry * cells : (entry + 1) * cells] = arrived_ref[slot]
        return carry

    lax.fori_loop(0, rows_ref.shape[0], one, 0)


def scatter_rows(tile, width, slot_ref, blocks, first, buffer_ref):
    cells = buffer_ref.shape[2]
    for entry in range(blocks.shape[1] // cells):
        slot = slot_ref[tile * width + first + entry]
        block = blocks[:, entry * cells : (entry + 1) * cells]
        buffer_ref[slot] = block.astype(buffer_ref.dtype)


def project(tile, copies, rows_ref, held_ref):
    parts = len(copies[tile])
    columns = held_ref.shape[2] // parts
    pred = 0.0
    for part in range(parts):
        span = slice(part * columns, (part + 1) * columns)
        copies[tile][part].wait()
        pred += lax.dot_general(
            rows_ref[tile, :, span],
            held_ref[tile, :, span],
            (((1,), (1,)), ((), ())),
            preferred_element_type=jnp.float32,
        )
    return pred


def residual_kernel(slot_ref, arrived_ref, sensor_ref, *refs):
    small_refs, refs = (refs[:2], refs[2:])
    pred_ref, buffer_ref, rows_ref, held_ref, sems, *small, small_sems = refs
    tiles = pred_ref.shape[0]
    width = slot_ref.shape[0] // tiles
    copies = sensor_copies(sensor_ref, held_ref, sems)
    start_copies(copies, start_all(small_refs, small, small_sems))
    weight, observed = small
    buffer_ref[...] = jnp.zeros_like(buffer_ref)
    gather_rows(width, slot_ref, arrived_ref, rows_ref)
    blocks = None
    for tile in range(tiles):
        pred = project(tile, copies, rows_ref, held_ref)
        if tile > 0:
            scatter_rows(tile - 1, width, slot_ref, blocks, 0, buffer_ref)
        pred_ref[tile] = pred
        weighted = (weight[tile] * (pred - observed[tile])).astype(jnp.bfloat16)
        blocks = jnp.dot(weighted, held_ref[tile], preferred_element_type=jnp.float32)
    scatter_rows(tiles - 1, width, slot_ref, blocks, 0, buffer_ref)


def forward_kernel(slot_ref, arrived_ref, sensor_ref, *refs):
    small_refs, refs = (refs[:9], refs[9:])
    pred_ref, sent_ref, rows_ref, held_ref, sems, *small, small_sems = refs
    tiles = pred_ref.shape[0]
    width = slot_ref.shape[0] // tiles
    copies = sensor_copies(sensor_ref, held_ref, sems)
    start_copies(copies, [])
    small_copies = start_all(small_refs, small, small_sems)
    gather_rows(width, slot_ref, arrived_ref, rows_ref)
    for tile in range(tiles):
        pred_ref[tile] = project(tile, copies, rows_ref, held_ref)
    wait_all(small_copies)
    weight, norm, faces, *rims = small
    total = faces[...]
    for edge, mine, theirs in (rims[:3], rims[3:]):
        for row in range(edge.shape[0]):
            change = mine[row].astype(jnp.float32) - theirs[row].astype(jnp.float32)
            total = total + edge[row] * change * change
    data = sum(weight[tile] * pred_ref[tile] * pred_ref[tile] for tile in range(tiles))
    lane = lax.broadcasted_iota(jnp.int32, total.shape, 1)
    block = jnp.zeros(total.shape, jnp.float32)
    for i, value in enumerate((norm[...], data, total)):
        block = jnp.where(lane == i, jnp.sum(value, axis=1, keepdims=True), block)
    sent_ref[...] = jnp.broadcast_to(block[None], sent_ref.shape)


def backward_kernel(slot_ref, sensor_ref, *refs):
    small_refs, refs = (refs[:2], refs[2:])
    buffer_ref, held_ref, sems, *small, small_sems = refs
    weight, pred = small
    tiles, samples = pred.shape[:2]
    width = slot_ref.shape[0] // tiles
    parts = sems.shape[1]
    columns = held_ref.shape[2] // parts
    copies = sensor_copies(sensor_ref, held_ref, sems)
    start_copies(copies, start_all(small_refs, small, small_sems))
    buffer_ref[...] = jnp.zeros_like(buffer_ref)
    for tile in range(tiles):
        weighted = weight[tile] * pred[tile]
        upper = weighted.astype(jnp.bfloat16).astype(jnp.float32)
        both = jnp.concatenate([upper, weighted - upper], axis=0).astype(jnp.bfloat16)
        for part in range(parts):
            copies[tile][part].wait()
            blocks = jnp.dot(
                both,
                held_ref[tile, :, part * columns : (part + 1) * columns],
                preferred_element_type=jnp.float32,
            )
            scatter_rows(
                tile,
                width,
                slot_ref,
                blocks[:samples] + blocks[samples:],
                part * width // parts,
                buffer_ref,
            )


def tile_call(kernel, name, slot_of, near, sensor, small, outs, samples):
    tiles, _, length = sensor.shape
    parts = PARTS[name] if slot_of.shape[0] // tiles % PARTS[name] == 0 else 1
    scratch = [
        pltpu.VMEM(sensor.shape, jnp.bfloat16),
        pltpu.SemaphoreType.DMA((tiles, parts)),
    ]
    if near:
        scratch = [pltpu.VMEM((tiles, samples, length), jnp.bfloat16)] + scratch
    return kernel_call(kernel, slot_of, near, [sensor, *small], outs, [], scratch + held(small))


def sum_kernel(first, layers, ids_ref, arrived_ref, *refs):
    active_ref, reg_ref, *refs = refs
    if not first:
        base_ref, step_ref, *refs = refs
    reply_ref, norm_ref, top, bottom, left, right, grad_ref, *refs = refs
    if first:
        data_ref, *refs = refs
        total, grad, out_sems, active, reg, sems = refs
        sources, targets = ((active_ref, reg_ref), (active, reg))
    else:
        total, grad, out_sems, active, reg, base, step_rows, sems = refs
        sources = (active_ref, reg_ref, base_ref, step_ref)
        targets = (active, reg, base, step_rows)
    copies = start_all(sources, targets, sems)
    count = ids_ref.shape[0]
    bricks = grad.shape[0]
    rows = bricks // layers
    total[...] = jnp.zeros_like(total)

    def add(i, carry):
        for k in range(GROUP):
            j = i * GROUP + k
            row = ids_ref[j]
            total[row] += arrived_ref[j].astype(jnp.float32)
        return carry

    lax.fori_loop(0, count // GROUP, add, 0)
    wait_all(copies)
    if not first:
        step = step_rows[...]

    def combine(i, norm):
        live = active[pl.ds(pl.multiple_of(i * GROUP, GROUP), GROUP), :].astype(jnp.float32)
        for k in range(GROUP):
            j = i * GROUP + k
            data = total[j]
            if not first:
                data = base[j] - step * data
            value = live[k : k + 1] * data + reg[j]
            grad[j] = value
            norm = norm + value * value
        return norm

    norm = lax.fori_loop(0, bricks // GROUP, combine, jnp.zeros(norm_ref.shape, jnp.float32))
    norm_ref[...] = norm
    if first:
        stores = start_all((grad, total), (grad_ref, data_ref), out_sems)
    else:
        stores = start_all((grad,), (grad_ref,), out_sems)

    def reply(i, carry):
        for k in range(GROUP):
            j = i * GROUP + k
            reply_ref[j] = grad[ids_ref[j]].astype(reply_ref.dtype)
        return carry

    lax.fori_loop(0, count // GROUP, reply, 0)
    top[...] = grad[pl.ds(0, rows)].astype(top.dtype)
    bottom[...] = grad[pl.ds(bricks - rows, rows)].astype(bottom.dtype)
    for layer in range(layers):
        left[layer] = grad[layer * rows].astype(left.dtype)
        right[layer] = grad[layer * rows + rows - 1].astype(right.dtype)
    wait_all(stores)


def sum_call(first, layers, ids, arrived, active, reg, *more):
    bricks, samples, cells = reg.shape
    small = [active, reg, *more]
    field = shape_of(jnp.float32, bricks, samples, cells)
    outs = [shape_of(jnp.bfloat16, *arrived.shape), shape_of(jnp.float32, samples, cells)]
    for length in (bricks // layers, bricks // layers, layers, layers):
        outs.append(shape_of(jnp.bfloat16, length, samples, cells))
    scratch = [
        pltpu.VMEM(field.shape, jnp.float32),
        pltpu.VMEM(field.shape, jnp.float32),
        pltpu.SemaphoreType.DMA((2 if first else 1,)),
    ]
    return kernel_call(
        functools.partial(sum_kernel, first, layers),
        ids,
        [arrived],
        small,
        outs,
        [field, field] if first else [field],
        scratch + held(small),
    )


def finish_kernel(
    got_ref, scale_ref, before_ref, mask_ref, observed_ref, pred_ref, moved_ref, last_ref,
    field_ref, grad_ref, model_ref, misfit_ref
):
    step = step_from(got_ref, scale_ref[...])
    model_ref[...] = field_ref[...] - step[None, None] * grad_ref[...]

    @pl.when(pl.program_id(0) == 0)
    def _():
        for tile in range(pred_ref.shape[0]):
            pred = pred_ref[tile] - before_ref[:, :1] * moved_ref[tile]
            pred = pred - step[:, :1] * last_ref[tile]
            misfit_ref[tile] = mask_ref[tile] * (pred - observed_ref[tile])


def finish_call(got, scale, before, mask, observed, pred, moved, last, field, grad):
    layers, rows, samples, cells = field.shape
    block = 4 if layers % 4 == 0 else 1
    spec = pl.BlockSpec((block, rows, samples, cells), lambda i: (i, 0, 0, 0))

    def fixed(array):
        return pl.BlockSpec(array.shape, lambda i: (0,) * array.ndim)

    small = [scale, before, mask, observed, pred, moved, last]
    return pl.pallas_call(
        finish_kernel,
        name="finish",
        grid=(layers // block,),
        in_specs=[WHOLE] + [fixed(a) for a in small] + [spec, spec],
        out_specs=[spec, fixed(observed)],
        out_shape=[pltpu.HBM(a.shape, a.dtype) for a in (field, observed)],
        compiler_params=pltpu.CompilerParams(vmem_limit_bytes=KERNEL_VMEM),
    )(got, *[far(a) for a in (*small, field, grad)])


def shards(
    sensitivity,
    observed,
    data_weight,
    data_counts,
    tile_bricks,
    start_model,
    active_cells,
    face_links,
    reg_weight,
):
    layers, strip_rows, samples, cells_x = start_model.shape
    tiles, tile_width = tile_bricks.shape
    data_slots = sensitivity.shape[1]
    owners = lax.axis_size("region") * lax.axis_size("survey")
    per_owner = layers * strip_rows
    capacity = max(2, 2 * tiles * tile_width // owners)
    slots = owners * capacity
    depth_count = layers * lax.axis_size("region")
    requests = tile_bricks.reshape(-1)
    owner_of = requests // per_owner
    local_of = requests % per_owner
    owner_hits = (owner_of[:, None] == jnp.arange(owners, dtype=jnp.int32)[None, :]).astype(
        jnp.int32
    )
    before = jnp.cumsum(owner_hits, axis=0) - owner_hits
    rank_of = jnp.sum(before * owner_hits, axis=1)
    slot_of = owner_of * capacity + rank_of
    slot_hits = slot_of[:, None] == jnp.arange(slots, dtype=jnp.int32)[None, :]
    asking = jnp.sum(jnp.where(slot_hits, local_of[:, None], 0), axis=0).reshape(owners, capacity)
    asked_ids = swap(asking).reshape(-1)

    active_flat = active_cells.reshape(per_owner, cells_x)
    links = face_links.reshape(per_owner, cells_x)
    base = (lax.axis_index("region") * layers).astype(jnp.int32).reshape(1)
    row_mask = (
        jnp.arange(data_slots, dtype=jnp.int32)[None, None, :] < data_counts[:, None, None]
    ).astype(jnp.float32)
    weight_sq = row_mask * (data_weight * data_weight)[:, None, :]
    mask = row_mask * data_weight[:, None, :]
    reg_rows = jnp.broadcast_to(reg_weight[:, None], (samples, cells_x))
    f32, bf16 = (jnp.float32, jnp.bfloat16)
    pred_shape = shape_of(f32, tiles, samples, data_slots)
    buffer_shape = shape_of(bf16, slots, samples, cells_x)

    def exchange(blocks):
        return swap(blocks.reshape(owners, capacity, samples, cells_x)).reshape(
            slots, samples, cells_x
        )

    def flat(field):
        return field.reshape(per_owner, samples, cells_x)

    def forward(arrived, norm, faces, edge_z, edge_y, rims, theirs):
        small = [weight_sq, norm, faces, edge_z, rims[1], theirs[0], edge_y, rims[3], theirs[1]]
        outs = [pred_shape, shape_of(f32, owners, samples, cells_x)]
        return tile_call(
            forward_kernel, "forward", slot_of, [arrived], sensitivity, small, outs, samples
        )

    grid = (depth_count, base, links, active_flat)
    model, bricks, *rims = prepare_call(start_model, active_cells)
    replies = flat(bricks)[asked_ids]
    arrived = exchange(replies)
    model_rims = edges(rims)
    pred, buffer = tile_call(
        residual_kernel,
        "residual",
        slot_of,
        [arrived],
        sensitivity,
        [weight_sq, observed],
        [pred_shape, buffer_shape],
        samples,
    )

    arrived = exchange(buffer)
    edge_z, edge_y, reg = reg_call(*grid, reg_rows, model, model_rims)
    replies, norm, *rims, grad, data_sum = sum_call(
        True, layers, asked_ids, arrived, active_flat, flat(reg)
    )
    arrived = exchange(replies)
    grad_rims = edges(rims)
    grad = grad.reshape(start_model.shape)
    faces = curvature_call(*grid, model, grad)
    step_pred, sums = forward(arrived, norm, faces, edge_z, edge_y, rims, grad_rims)
    got = swap(sums)
    (buffer,) = tile_call(
        backward_kernel,
        "backward",
        slot_of,
        [],
        sensitivity,
        [weight_sq, step_pred],
        [buffer_shape],
        samples,
    )
    arrived = exchange(buffer)

    edge_z, edge_y, step, reg, model = reg_call(
        *grid, reg_rows, model, model_rims, (got, grad, grad_rims)
    )
    replies, norm, *rims, grad = sum_call(
        False, layers, asked_ids, arrived, active_flat, flat(reg), data_sum, step
    )
    arrived = exchange(replies)
    grad_rims = edges(rims, both=False)
    grad = grad.reshape(start_model.shape)
    faces = curvature_call(*grid, model, grad)
    last_pred, sums = forward(arrived, norm, faces, edge_z, edge_y, rims, grad_rims)
    got = swap(sums)
    return tuple(
        finish_call(got, reg_rows, step, mask, observed, pred, step_pred, last_pred, model, grad)
    )


def solution(mesh):
    return jax.shard_map(
        shards,
        mesh=mesh,
        in_specs=(
            P(("region", "survey"), None, None),
            P(("region", "survey"), None, None),
            P(("region", "survey"), None),
            P(("region", "survey")),
            P(("region", "survey"), None),
            P("region", "survey", None, None),
            P("region", "survey", None),
            P("region", "survey", None),
            P(),
        ),
        out_specs=(P("region", "survey", None, None), P(("region", "survey"), None, None)),
        check_vma=False,
    )
```

```python
import functools

import jax
import jax.numpy as jnp
from jax import lax
from jax.experimental import pallas as pl
from jax.experimental.pallas import tpu as pltpu
from jax.sharding import PartitionSpec as P


AXES = ("region", "survey")
EPS_SQ = 0.09
KERNEL_VMEM = 32 * 1024 * 1024
PARTS = {"residual": 1, "forward": 4, "both": 1}
GROUP = 8


def swap(field):
    return lax.all_to_all(field, AXES, split_axis=0, concat_axis=0, tiled=True)


def edges(parts, both=True):
    rims = [[], []]
    for axis, (first, last) in (("region", parts[:2]), ("survey", parts[2:])):
        count = lax.axis_size(axis)
        rims[0].append(lax.ppermute(first, axis, [(i + 1, i) for i in range(count - 1)]))
        if both:
            rims[1].append(lax.ppermute(last, axis, [(i, i + 1) for i in range(count - 1)]))
    return rims[0] + rims[1]


WHOLE = pl.BlockSpec(memory_space=pltpu.VMEM)
FAR = pl.BlockSpec(memory_space=pltpu.HBM)


def far(array):
    return pltpu.with_memory_space_constraint(array, pltpu.HBM)


def kernel_call(kernel, table, near, distant, outs, distant_outs, scratch):
    near_specs = [WHOLE] * len(near)
    out_shapes = [pltpu.HBM(o.shape, o.dtype) for o in (*outs, *distant_outs)]
    return pl.pallas_call(
        kernel,
        out_shape=out_shapes,
        grid_spec=pltpu.PrefetchScalarGridSpec(
            num_scalar_prefetch=1,
            grid=(),
            in_specs=near_specs + [FAR] * len(distant),
            out_specs=[pl.BlockSpec(o.shape, functools.partial(origin, o.ndim)) for o in outs]
            + [FAR] * len(distant_outs),
            scratch_shapes=scratch,
        ),
        compiler_params=pltpu.CompilerParams(vmem_limit_bytes=KERNEL_VMEM),
    )(table, *near, *[far(d) for d in distant])


def origin(ndim, *_):
    return (0,) * ndim


def shape_of(dtype, *shape):
    return jax.ShapeDtypeStruct(shape, dtype)


def held(arrays):
    return [pltpu.VMEM(a.shape, a.dtype) for a in arrays] + [
        pltpu.SemaphoreType.DMA((len(arrays),))
    ]


def start_all(sources, targets, sems, base=0):
    copies = [
        pltpu.make_async_copy(source, target, sems.at[base + i])
        for i, (source, target) in enumerate(zip(sources, targets))
    ]
    for copy in copies:
        copy.start()
    return copies


def wait_all(copies):
    for copy in copies:
        copy.wait()


def start_pads(field_ref, pad, sem):
    layers, rows = field_ref.shape[:2]
    copy = pltpu.make_async_copy(field_ref, pad.at[pl.ds(0, layers), pl.ds(0, rows)], sem)
    copy.start()
    return copy


def fill_pads(pad, below, right):
    layers, rows = (pad.shape[0] - 1, pad.shape[1] - 1)
    pad[layers, pl.ds(0, rows)] = below[...].astype(pad.dtype)
    for layer in range(layers):
        pad[layer, rows] = right[layer].astype(pad.dtype)


def face(here, there, link):
    difference = here - there
    return difference, link * lax.rsqrt(difference * difference + EPS_SQ)


def levels(base, layer, depth_count):
    depth = (base + layer).astype(jnp.float32)
    return [1.0 + (2.0 * depth + offset) / depth_count for offset in (-1.0, 0.0, 1.0)]


def link_of(codes, number, level):
    return (lax.shift_right_logical(codes, number) & 1).astype(jnp.float32) * level


def next_lane(value):
    return pltpu.roll(value, value.shape[-1] - 1, value.ndim - 1)


def inner_lanes(cells):
    lane = lax.broadcasted_iota(jnp.int32, (GROUP, cells), 1)
    return (lane < cells - 1).astype(jnp.float32)


def step_from(got_ref, scale):
    sums = jnp.sum(got_ref[...], axis=0)
    norm, data, faces = (sums[:, i : i + 1] for i in range(3))
    return jnp.broadcast_to(norm / (data + scale[:, :1] * faces), scale.shape)


def prepare_kernel(start_ref, active_ref, model_ref, low_ref, top, bottom, left, right):
    block, rows = start_ref.shape[:2]

    def one(layer, carry):
        for start in range(0, rows, GROUP):
            live = active_ref[layer, pl.ds(start, GROUP), :].astype(jnp.float32)
            for k in range(GROUP):
                value = start_ref[layer, start + k] * live[k : k + 1]
                model_ref[layer, start + k] = value
                low_ref[layer, start + k] = value.astype(jnp.bfloat16)
        left[layer] = model_ref[layer, 0]
        right[layer] = model_ref[layer, rows - 1]
        return carry

    lax.fori_loop(0, block, one, 0)

    @pl.when(pl.program_id(0) == 0)
    def _():
        top[...] = model_ref[0]

    @pl.when(pl.program_id(0) == pl.num_programs(0) - 1)
    def _():
        bottom[...] = model_ref[block - 1]


def prepare_call(start_model, active):
    layers, rows, samples, cells = start_model.shape
    step = 4 if layers % 4 == 0 else 1
    block = pl.BlockSpec((step, rows, samples, cells), lambda i: (i, 0, 0, 0))
    layer = pl.BlockSpec((rows, samples, cells), lambda i: (0, 0, 0))
    column = pl.BlockSpec((step, samples, cells), lambda i: (i, 0, 0))
    outs = [
        (start_model.shape, jnp.float32),
        (start_model.shape, jnp.bfloat16),
        *[((rows, samples, cells), jnp.float32)] * 2,
        *[((layers, samples, cells), jnp.float32)] * 2,
    ]
    return pl.pallas_call(
        prepare_kernel,
        name="prepare",
        grid=(layers // step,),
        in_specs=[block, pl.BlockSpec((step, rows, cells), lambda i: (i, 0, 0))],
        out_specs=[block, block, layer, layer, column, column],
        out_shape=[
            jax.ShapeDtypeStruct(*o) if o[1] == jnp.bfloat16 else pltpu.HBM(*o) for o in outs
        ],
        compiler_params=pltpu.CompilerParams(vmem_limit_bytes=KERNEL_VMEM),
    )(far(start_model), far(active))


def face_pass(depth_count, base, links_ref, active_ref, pad, flow, above, left, edges_out, put):
    edge_z, edge_y = edges_out
    layers, rows = (pad.shape[0] - 1, pad.shape[1] - 1)
    inner = inner_lanes(pad.shape[-1])
    for start in range(0, rows, GROUP):
        codes = links_ref[pl.ds(start, GROUP), :]
        link = link_of(codes, 0, levels(base, 0, depth_count)[0])
        for k in range(GROUP):
            difference, weight = face(above(start + k), pad[0, start + k], link[k : k + 1])
            flow[start + k] = weight * difference

    def one(layer, carry):
        _, level, level_below = levels(base, layer, depth_count)
        flow_y = None
        for start in range(0, rows, GROUP):
            place = pl.ds(pl.multiple_of(layer * rows + start, GROUP), GROUP)
            codes = links_ref[place, :]
            link_z = link_of(codes, 1, level_below)
            link_y = link_of(codes, 3, level)
            link_x = link_of(codes, 5, level) * inner
            live = active_ref[place, :].astype(jnp.float32)
            small = live * level
            if start == 0:
                link = link_of(codes, 2, level)
                difference, weight = face(left(layer), pad[layer, 0], link[:1])
                flow_y = weight * difference
            for k in range(GROUP):
                row = start + k
                one_row = slice(k, k + 1)
                here = pad[layer, row]
                total = small[one_row] * lax.rsqrt(here * here + EPS_SQ) * here
                difference, weight = face(here, next_lane(here), link_x[one_row])
                flow_x = weight * difference
                total = total + flow_x - pltpu.roll(flow_x, 1, 1)
                difference, weight = face(here, pad[layer, row + 1], link_y[one_row])
                if row == rows - 1:
                    edge_y[layer] = weight
                out_y = weight * difference
                total = total + out_y - flow_y
                flow_y = out_y
                difference, weight = face(here, pad[layer + 1, row], link_z[one_row])
                edge_z[row] = weight
                out_z = weight * difference
                total = total + out_z - flow[row]
                flow[row] = out_z
                carry = put(layer, row, live[one_row], total, carry)
        return carry

    return lax.fori_loop(0, layers, one, jnp.zeros(pad.shape[2:], jnp.float32))


def reg_kernel(depth_count, base_ref, *refs):
    small_refs, refs = (refs[:7], refs[7:])
    field_ref, edge_z, edge_y, reg_ref, out, pad, flow, sems, *small, small_sems = refs
    copies = start_all(small_refs, small, small_sems)
    field_copy = start_pads(field_ref, pad, sems.at[0])
    wait_all(copies)
    links_ref, active_ref, scale_ref, below, right, above, left = small
    scale = scale_ref[...]
    fill_pads(pad, below, right)
    field_copy.wait()

    def put(layer, row, live, value, carry):
        out[layer, row] = scale * value
        return carry

    face_pass(
        depth_count,
        base_ref[0],
        links_ref,
        active_ref,
        pad,
        flow,
        lambda row: above[row],
        lambda layer: left[layer],
        (edge_z, edge_y),
        put,
    )
    final = pltpu.make_async_copy(out, reg_ref, sems.at[1])
    final.start()
    final.wait()


def reg_call(depth_count, base, links, active, scale, field, rims):
    layers, rows, samples, cells = field.shape
    f32 = jnp.float32
    small = [links, active, scale, *rims]
    return kernel_call(
        functools.partial(reg_kernel, depth_count),
        base,
        [],
        [*small, field],
        [shape_of(f32, rows, samples, cells), shape_of(f32, layers, samples, cells)],
        [shape_of(f32, *field.shape)],
        [
            pltpu.VMEM(field.shape, f32),
            pltpu.VMEM((layers + 1, rows + 1, samples, cells), f32),
            pltpu.VMEM((rows, samples, cells), f32),
            pltpu.SemaphoreType.DMA((2,)),
        ]
        + held(small),
    )


def next_kernel(depth_count, capacity, ids_ref, arrived_ref, *refs):
    small_refs, refs = (refs[:11], refs[11:])
    field_ref, grad_ref, reg_ref, *refs = refs
    reply_ref, norm_ref, top, bottom, first, last, edge_z, edge_y, step_ref, *refs = refs
    new_ref, out_ref, total, out, reg, pad, gpad, flow, sems, *small, small_sems = refs
    layers, rows = field_ref.shape[:2]
    count = ids_ref.shape[0] - 1
    copies = start_all(small_refs, small, small_sems)
    big = [start_pads(field_ref, pad, sems.at[0]), start_pads(grad_ref, gpad, sems.at[1])]
    big += start_all((reg_ref,), (reg,), sems, 2)
    add_blocks(count, capacity, 1, ids_ref, arrived_ref, total)
    owners = count // capacity
    sums = lax.fori_loop(
        0,
        owners,
        lambda i, v: v + arrived_ref[i * (capacity + 1) + capacity].astype(jnp.float32),
        jnp.zeros(norm_ref.shape, jnp.float32),
    )
    norm, data, faces = (
        sums[:, i : i + 1] + sums[:, i + 1 : i + 2] + sums[:, i + 2 : i + 3] for i in (0, 3, 6)
    )
    wait_all(copies)
    links_ref, active_ref, scale_ref, below, right, above, left, *more = small
    gbelow, gright, gabove, gleft = more
    scale = scale_ref[...]
    step = jnp.broadcast_to(norm / (data + scale[:, :1] * faces), scale.shape)
    step_ref[...] = step
    fill_pads(pad, below, right)
    fill_pads(gpad, gbelow, gright)
    wait_all(big)

    def move(layer, carry):
        for row in range(rows + 1):
            pad[layer, row] = pad[layer, row] - step * gpad[layer, row]
        return carry

    lax.fori_loop(0, layers, move, 0)
    for row in range(rows):
        pad[layers, row] = pad[layers, row] - step * gpad[layers, row]
    inside = pad.at[pl.ds(0, layers), pl.ds(0, rows)]
    stores = start_all((inside,), (new_ref,), sems, 3)

    def put(layer, row, live, value, norm):
        data = step * (live * total[layer * rows + row])
        value = scale * value + (gpad[layer, row] - reg[layer, row] - data)
        out[layer, row] = value
        return norm + value * value

    norm_ref[...] = face_pass(
        depth_count,
        ids_ref[count],
        links_ref,
        active_ref,
        pad,
        flow,
        lambda row: above[row] - step * gabove[row].astype(jnp.float32),
        lambda layer: left[layer] - step * gleft[layer].astype(jnp.float32),
        (edge_z, edge_y),
        put,
    )
    stores += start_all((out,), (out_ref,), sems, 4)

    def reply(i, carry):
        for k in range(GROUP):
            j = i * GROUP + k
            row = ids_ref[j]
            brick = out[lax.div(row, rows), lax.rem(row, rows)]
            reply_ref[j] = brick.astype(reply_ref.dtype)
        return carry

    lax.fori_loop(0, count // GROUP, reply, 0)
    top[...] = out[0].astype(top.dtype)
    bottom[...] = out[layers - 1].astype(bottom.dtype)
    for layer in range(layers):
        first[layer] = out[layer, 0].astype(first.dtype)
        last[layer] = out[layer, rows - 1].astype(last.dtype)
    wait_all(stores)


def next_call(
    depth_count, base, links, active, scale, capacity, ids, arrived, field, rims, grad, grad_rims,
    reg
):
    layers, rows, samples, cells = field.shape
    f32, bf16 = (jnp.float32, jnp.bfloat16)
    small = [links, active, scale, *rims, *grad_rims]
    pad = pltpu.VMEM((layers + 1, rows + 1, samples, cells), f32)
    rim_z, rim_y = ((rows, samples, cells), (layers, samples, cells))
    outs = [
        shape_of(bf16, ids.shape[0], samples, cells),
        shape_of(f32, samples, cells),
        shape_of(bf16, *rim_z),
        shape_of(bf16, *rim_z),
        shape_of(bf16, *rim_y),
        shape_of(bf16, *rim_y),
        shape_of(f32, *rim_z),
        shape_of(f32, *rim_y),
        shape_of(f32, samples, cells),
    ]
    return kernel_call(
        functools.partial(next_kernel, depth_count, capacity),
        jnp.concatenate([ids, base]),
        [arrived],
        [*small, field, grad, reg],
        outs,
        [shape_of(f32, *field.shape)] * 2,
        [
            pltpu.VMEM((layers * rows, samples, cells), f32),
            pltpu.VMEM(field.shape, f32),
            pltpu.VMEM(field.shape, f32),
            pad,
            pad,
            pltpu.VMEM(rim_z, f32),
            pltpu.SemaphoreType.DMA((5,)),
        ]
        + held(small),
    )


def curvature_kernel(
    depth_count, base_ref, links_ref, active_ref, field_ref, grad_ref, curv_ref, *refs
):
    links, active, field, grad, sems = refs
    layers, rows = field.shape[:2]
    base = base_ref[0]
    wait_all(
        start_all((field_ref, grad_ref, links_ref, active_ref), (field, grad, links, active), sems)
    )
    inner = inner_lanes(field.shape[-1])

    def one(layer, total):
        _, level, level_below = levels(base, layer, depth_count)
        below = jnp.minimum(layer + 1, layers - 1)
        level_below = jnp.where(layer + 1 < layers, level_below, 0.0)
        for start in range(0, rows, GROUP):
            place = pl.ds(pl.multiple_of(layer * rows + start, GROUP), GROUP)
            codes = links[place, :]
            link_z = link_of(codes, 1, level_below)
            link_y = link_of(codes, 3, level)
            link_x = link_of(codes, 5, level) * inner
            live = active[place, :].astype(jnp.float32) * level
            for k in range(GROUP):
                row = start + k
                one_row = slice(k, k + 1)
                here = field[layer, row]
                slope = grad[layer, row]
                part = live[one_row] * lax.rsqrt(here * here + EPS_SQ) * slope * slope
                pairs = [
                    (next_lane(here), next_lane(slope), link_x),
                    (field[below, row], grad[below, row], link_z),
                ]
                if row + 1 < rows:
                    pairs.append((field[layer, row + 1], grad[layer, row + 1], link_y))
                for there, gthere, link in pairs:
                    _, weight = face(here, there, link[one_row])
                    change = slope - gthere
                    part = part + weight * change * change
                total = total + part
        return total

    curv_ref[...] = lax.fori_loop(0, layers, one, jnp.zeros(curv_ref.shape, jnp.float32))


def curvature_call(depth_count, base, links, active, field, grad):
    (curv,) = kernel_call(
        functools.partial(curvature_kernel, depth_count),
        base,
        [],
        [links, active, field, grad],
        [shape_of(jnp.float32, *field.shape[2:])],
        [],
        held([links, active, field, grad]),
    )
    return curv


def sensor_copies(sensor_ref, held_ref, sems):
    tiles, _, length = held_ref.shape
    parts = sems.shape[1]
    columns = length // parts
    return [
        [
            pltpu.make_async_copy(
                sensor_ref.at[tile, :, pl.ds(part * columns, columns)],
                held_ref.at[tile, :, pl.ds(part * columns, columns)],
                sems.at[tile, part],
            )
            for part in range(parts)
        ]
        for tile in range(tiles)
    ]


def start_copies(copies, small):
    flat = [copy for tile in copies for copy in tile]
    flat[0].start()
    wait_all(small)
    for copy in flat[1:]:
        copy.start()


def gather_rows(width, slot_ref, arrived_ref, rows_ref):
    cells = arrived_ref.shape[2]

    def one(tile, carry):
        for entry in range(width):
            slot = slot_ref[tile * width + entry]
            rows_ref[tile, :, entry * cells : (entry + 1) * cells] = arrived_ref[slot]
        return carry

    lax.fori_loop(0, rows_ref.shape[0], one, 0)


def spaced(slot, capacity, extra):
    if not extra:
        return slot
    return slot + lax.div(slot, capacity) * extra


def scatter_rows(tile, width, slot_ref, blocks, buffer_ref, capacity=1, extra=0):
    cells = buffer_ref.shape[2]
    for entry in range(width):
        slot = spaced(slot_ref[tile * width + entry], capacity, extra)
        block = blocks[:, entry * cells : (entry + 1) * cells]
        buffer_ref[slot] = block.astype(buffer_ref.dtype)


def project(tile, copies, rows_ref, held_ref):
    parts = len(copies[tile])
    columns = held_ref.shape[2] // parts
    pred = 0.0
    for part in range(parts):
        span = slice(part * columns, (part + 1) * columns)
        copies[tile][part].wait()
        pred += lax.dot_general(
            rows_ref[tile, :, span],
            held_ref[tile, :, span],
            (((1,), (1,)), ((), ())),
            preferred_element_type=jnp.float32,
        )
    return pred


def residual_kernel(slot_ref, arrived_ref, sensor_ref, *refs):
    small_refs, refs = (refs[:2], refs[2:])
    pred_ref, buffer_ref, rows_ref, held_ref, sems, *small, small_sems = refs
    tiles = pred_ref.shape[0]
    width = slot_ref.shape[0] // tiles
    copies = sensor_copies(sensor_ref, held_ref, sems)
    start_copies(copies, start_all(small_refs, small, small_sems))
    weight, observed = small
    buffer_ref[...] = jnp.zeros_like(buffer_ref)
    gather_rows(width, slot_ref, arrived_ref, rows_ref)
    blocks = None
    for tile in range(tiles):
        pred = project(tile, copies, rows_ref, held_ref)
        if tile > 0:
            scatter_rows(tile - 1, width, slot_ref, blocks, buffer_ref)
        pred_ref[tile] = pred
        weighted = (weight[tile] * (pred - observed[tile])).astype(jnp.bfloat16)
        blocks = jnp.dot(weighted, held_ref[tile], preferred_element_type=jnp.float32)
    scatter_rows(tiles - 1, width, slot_ref, blocks, buffer_ref)


def local_sums(weight, pred_ref, norm, faces, rims):
    total = faces[...]
    for edge, mine, theirs in (rims[:3], rims[3:]):
        for row in range(edge.shape[0]):
            change = mine[row].astype(jnp.float32) - theirs[row].astype(jnp.float32)
            total = total + edge[row] * change * change
    tiles = pred_ref.shape[0]
    data = sum(weight[tile] * pred_ref[tile] * pred_ref[tile] for tile in range(tiles))
    return [jnp.sum(value, axis=1, keepdims=True) for value in (norm[...], data, total)]


def columns_of(values, shape):
    lane = lax.broadcasted_iota(jnp.int32, shape, 1)
    block = jnp.zeros(shape, jnp.float32)
    for i, value in enumerate(values):
        block = jnp.where(lane == i, value, block)
    return block


def in_parts(value):
    parts = []
    for _ in range(3):
        parts.append(value.astype(jnp.bfloat16).astype(jnp.float32))
        value = value - parts[-1]
    return parts


def forward_kernel(slot_ref, arrived_ref, sensor_ref, *refs):
    small_refs, refs = (refs[:9], refs[9:])
    pred_ref, sent_ref, rows_ref, held_ref, sems, *small, small_sems = refs
    tiles = pred_ref.shape[0]
    width = slot_ref.shape[0] // tiles
    copies = sensor_copies(sensor_ref, held_ref, sems)
    start_copies(copies, [])
    small_copies = start_all(small_refs, small, small_sems)
    gather_rows(width, slot_ref, arrived_ref, rows_ref)
    for tile in range(tiles):
        pred_ref[tile] = project(tile, copies, rows_ref, held_ref)
    wait_all(small_copies)
    weight, norm, faces, *rims = small
    sums = local_sums(weight, pred_ref, norm, faces, rims)
    sent_ref[...] = jnp.broadcast_to(columns_of(sums, norm.shape)[None], sent_ref.shape)


def both_kernel(capacity, slot_ref, arrived_ref, sensor_ref, *refs):
    small_refs, refs = (refs[:9], refs[9:])
    pred_ref, buffer_ref, rows_ref, held_ref, sems, *small, small_sems = refs
    tiles, samples = pred_ref.shape[:2]
    width = slot_ref.shape[0] // tiles
    copies = sensor_copies(sensor_ref, held_ref, sems)
    start_copies(copies, start_all(small_refs[:1], small[:1], small_sems))
    later = start_all(small_refs[1:], small[1:], small_sems, 1)
    weight, norm, faces, *rims = small
    buffer_ref[...] = jnp.zeros_like(buffer_ref)
    gather_rows(width, slot_ref, arrived_ref, rows_ref)

    def put(tile, blocks):
        scatter_rows(
            tile, width, slot_ref, blocks[:samples] + blocks[samples:], buffer_ref, capacity, 1
        )

    blocks = None
    for tile in range(tiles):
        pred = project(tile, copies, rows_ref, held_ref)
        if tile > 0:
            put(tile - 1, blocks)
        pred_ref[tile] = pred
        weighted = weight[tile] * pred
        upper = weighted.astype(jnp.bfloat16).astype(jnp.float32)
        pair = jnp.concatenate([upper, weighted - upper], axis=0).astype(jnp.bfloat16)
        blocks = jnp.dot(pair, held_ref[tile], preferred_element_type=jnp.float32)
    put(tiles - 1, blocks)
    wait_all(later)
    sums = local_sums(weight, pred_ref, norm, faces, rims)
    split = [part for value in sums for part in in_parts(value)]
    block = columns_of(split, norm.shape).astype(buffer_ref.dtype)

    def send(owner, carry):
        buffer_ref[owner * (capacity + 1) + capacity] = block
        return carry

    lax.fori_loop(0, buffer_ref.shape[0] // (capacity + 1), send, 0)


def tile_call(kernel, name, slot_of, near, sensor, small, outs, samples):
    tiles, _, length = sensor.shape
    parts = PARTS[name] if slot_of.shape[0] // tiles % PARTS[name] == 0 else 1
    scratch = [
        pltpu.VMEM(sensor.shape, jnp.bfloat16),
        pltpu.SemaphoreType.DMA((tiles, parts)),
    ]
    if near:
        scratch = [pltpu.VMEM((tiles, samples, length), jnp.bfloat16)] + scratch
    return kernel_call(kernel, slot_of, near, [sensor, *small], outs, [], scratch + held(small))


def add_blocks(count, capacity, extra, ids_ref, arrived_ref, total):
    total[...] = jnp.zeros_like(total)

    def add(i, carry):
        for k in range(GROUP):
            j = i * GROUP + k
            row = ids_ref[j]
            total[row] += arrived_ref[spaced(j, capacity, extra)].astype(jnp.float32)
        return carry

    lax.fori_loop(0, count // GROUP, add, 0)


def sum_kernel(layers, ids_ref, arrived_ref, *refs):
    active_ref, reg_ref, reply_ref, norm_ref, top, bottom, left, right, *refs = refs
    grad_ref, total, grad, out_sems, active, reg, sems = refs
    copies = start_all((active_ref, reg_ref), (active, reg), sems)
    count = ids_ref.shape[0]
    bricks = grad.shape[0]
    rows = bricks // layers
    add_blocks(count, 1, 0, ids_ref, arrived_ref, total)
    wait_all(copies)

    def combine(i, norm):
        live = active[pl.ds(pl.multiple_of(i * GROUP, GROUP), GROUP), :].astype(jnp.float32)
        for k in range(GROUP):
            j = i * GROUP + k
            value = live[k : k + 1] * total[j] + reg[j]
            grad[j] = value
            norm = norm + value * value
        return norm

    norm = lax.fori_loop(0, bricks // GROUP, combine, jnp.zeros(norm_ref.shape, jnp.float32))
    norm_ref[...] = norm
    stores = start_all((grad,), (grad_ref,), out_sems)

    def reply(i, carry):
        for k in range(GROUP):
            j = i * GROUP + k
            reply_ref[j] = grad[ids_ref[j]].astype(reply_ref.dtype)
        return carry

    lax.fori_loop(0, count // GROUP, reply, 0)
    top[...] = grad[pl.ds(0, rows)].astype(top.dtype)
    bottom[...] = grad[pl.ds(bricks - rows, rows)].astype(bottom.dtype)
    for layer in range(layers):
        left[layer] = grad[layer * rows].astype(left.dtype)
        right[layer] = grad[layer * rows + rows - 1].astype(right.dtype)
    wait_all(stores)


def sum_call(layers, ids, arrived, active, reg):
    bricks, samples, cells = reg.shape
    small = [active, reg]
    field = shape_of(jnp.float32, bricks, samples, cells)
    outs = [shape_of(jnp.bfloat16, *arrived.shape), shape_of(jnp.float32, samples, cells)]
    for length in (bricks // layers, bricks // layers, layers, layers):
        outs.append(shape_of(jnp.bfloat16, length, samples, cells))
    scratch = [
        pltpu.VMEM(field.shape, jnp.float32),
        pltpu.VMEM(field.shape, jnp.float32),
        pltpu.SemaphoreType.DMA((1,)),
    ]
    return kernel_call(
        functools.partial(sum_kernel, layers),
        ids,
        [arrived],
        small,
        outs,
        [field],
        scratch + held(small),
    )


def finish_kernel(_, got_ref, *refs):
    small_refs, refs = (refs[:7], refs[7:])
    field_ref, grad_ref, model_ref, misfit_ref, field, grad, misfit, sems, *refs = refs
    small, small_sems = (refs[:-1], refs[-1])
    copies = start_all(small_refs, small, small_sems)
    layers = field.shape[0]
    chunks = sems.shape[0] // 3
    spans = [pl.ds(i * (layers // chunks), layers // chunks) for i in range(chunks)]
    loads = [
        start_all(
            (field_ref.at[span], grad_ref.at[span]),
            (field.at[span], grad.at[span]),
            sems,
            3 * i,
        )
        for i, span in enumerate(spans)
    ]
    wait_all(copies)
    scale, before, mask, observed, pred_ref, moved, last = small
    step = step_from(got_ref, scale[...])
    for tile in range(misfit.shape[0]):
        pred = pred_ref[tile] - before[:, :1] * moved[tile]
        pred = pred - step[:, :1] * last[tile]
        misfit[tile] = mask[tile] * (pred - observed[tile])
    stores = start_all((misfit,), (misfit_ref,), sems, 3 * chunks)
    for i, span in enumerate(spans):
        wait_all(loads[i])
        field[span] = field[span] - step[None, None] * grad[span]
        stores += start_all((field.at[span],), (model_ref.at[span],), sems, 3 * i + 2)
    wait_all(stores)


def finish_call(table, got, scale, before, mask, observed, pred, moved, last, field, grad):
    small = [scale, before, mask, observed, pred, moved, last]
    chunks = 4 if field.shape[0] % 4 == 0 else 1
    return kernel_call(
        finish_kernel,
        table,
        [got],
        [*small, field, grad],
        [],
        [shape_of(jnp.float32, *a.shape) for a in (field, observed)],
        [
            pltpu.VMEM(field.shape, jnp.float32),
            pltpu.VMEM(field.shape, jnp.float32),
            pltpu.VMEM(observed.shape, jnp.float32),
            pltpu.SemaphoreType.DMA((3 * chunks + 1,)),
        ]
        + held(small),
    )


def shards(
    sensitivity,
    observed,
    data_weight,
    data_counts,
    tile_bricks,
    start_model,
    active_cells,
    face_links,
    reg_weight,
):
    layers, strip_rows, samples, cells_x = start_model.shape
    tiles, tile_width = tile_bricks.shape
    data_slots = sensitivity.shape[1]
    owners = lax.axis_size("region") * lax.axis_size("survey")
    per_owner = layers * strip_rows
    capacity = max(2, 2 * tiles * tile_width // owners)
    slots = owners * capacity
    depth_count = layers * lax.axis_size("region")
    requests = tile_bricks.reshape(-1)
    owner_of = requests // per_owner
    local_of = requests % per_owner
    owner_hits = (owner_of[:, None] == jnp.arange(owners, dtype=jnp.int32)[None, :]).astype(
        jnp.int32
    )
    before = jnp.cumsum(owner_hits, axis=0) - owner_hits
    rank_of = jnp.sum(before * owner_hits, axis=1)
    slot_of = owner_of * capacity + rank_of
    slot_hits = slot_of[:, None] == jnp.arange(slots, dtype=jnp.int32)[None, :]
    asking = jnp.sum(jnp.where(slot_hits, local_of[:, None], 0), axis=0).reshape(owners, capacity)
    asked_ids = swap(asking).reshape(-1)

    active_flat = active_cells.reshape(per_owner, cells_x)
    links = face_links.reshape(per_owner, cells_x)
    base = (lax.axis_index("region") * layers).astype(jnp.int32).reshape(1)
    row_mask = (
        jnp.arange(data_slots, dtype=jnp.int32)[None, None, :] < data_counts[:, None, None]
    ).astype(jnp.float32)
    weight_sq = row_mask * (data_weight * data_weight)[:, None, :]
    mask = row_mask * data_weight[:, None, :]
    reg_rows = jnp.broadcast_to(reg_weight[:, None], (samples, cells_x))
    f32, bf16 = (jnp.float32, jnp.bfloat16)
    pred_shape = shape_of(f32, tiles, samples, data_slots)

    def exchange(blocks):
        sent = blocks.reshape(owners, blocks.shape[0] // owners, samples, cells_x)
        return swap(sent).reshape(blocks.shape)

    def flat(field):
        return field.reshape(per_owner, samples, cells_x)

    def tile_stage(kernel, name, arrived, small, out):
        return tile_call(
            kernel, name, slot_of, [arrived], sensitivity, small, [pred_shape, out], samples
        )

    def sums_inputs(norm, faces, edge_z, edge_y, mine, theirs):
        return [weight_sq, norm, faces, edge_z, mine[0], theirs[0], edge_y, mine[1], theirs[1]]

    grid = (depth_count, base, links, active_flat)
    model, bricks, *rims = prepare_call(start_model, active_cells)
    replies = flat(bricks)[asked_ids]
    arrived = exchange(replies)
    model_rims = edges(rims)
    blocks_shape = shape_of(bf16, slots, samples, cells_x)
    small = [weight_sq, observed]
    pred, buffer = tile_stage(residual_kernel, "residual", arrived, small, blocks_shape)

    arrived = exchange(buffer)
    edge_z, edge_y, reg = reg_call(*grid, reg_rows, model, model_rims)
    replies, norm, *rims, grad = sum_call(layers, asked_ids, arrived, active_flat, flat(reg))
    arrived = exchange(replies)
    grad_rims = edges(rims)
    grad = grad.reshape(start_model.shape)
    faces = curvature_call(*grid, model, grad)
    small = sums_inputs(norm, faces, edge_z, edge_y, rims[1::2], grad_rims)
    blocks_shape = shape_of(bf16, slots + owners, samples, cells_x)
    kernel = functools.partial(both_kernel, capacity)
    step_pred, buffer = tile_stage(kernel, "both", arrived, small, blocks_shape)
    arrived = exchange(buffer)

    replies, norm, *rims, edge_z, edge_y, step, model, grad = next_call(
        *grid, reg_rows, capacity, asked_ids, arrived, model, model_rims, grad, grad_rims, reg
    )
    arrived = exchange(replies)
    grad_rims = edges(rims, both=False)
    faces = curvature_call(*grid, model, grad)
    small = sums_inputs(norm, faces, edge_z, edge_y, rims[1::2], grad_rims)
    sums_shape = shape_of(f32, owners, samples, cells_x)
    last_pred, sums = tile_stage(forward_kernel, "forward", arrived, small, sums_shape)
    got = swap(sums)
    fields = (mask, observed, pred, step_pred, last_pred, model, grad)
    return tuple(finish_call(base, got, reg_rows, step, *fields))


def solution(mesh):
    return jax.shard_map(
        shards,
        mesh=mesh,
        in_specs=(
            P(("region", "survey"), None, None),
            P(("region", "survey"), None, None),
            P(("region", "survey"), None),
            P(("region", "survey")),
            P(("region", "survey"), None),
            P("region", "survey", None, None),
            P("region", "survey", None),
            P("region", "survey", None),
            P(),
        ),
        out_specs=(P("region", "survey", None, None), P(("region", "survey"), None, None)),
        check_vma=False,
    )
```

```python
import functools

import jax
import jax.numpy as jnp
from jax import lax
from jax.experimental import pallas as pl
from jax.experimental.pallas import tpu as pltpu
from jax.sharding import PartitionSpec as P


AXES = ("region", "survey")
EPS_SQ = 0.09
KERNEL_VMEM = 32 * 1024 * 1024
PARTS = {"residual": 1, "forward": 4, "both": 1}
GROUP = 8


def swap(field):
    return lax.all_to_all(field, AXES, split_axis=0, concat_axis=0, tiled=True)


def edges(parts, both=True):
    rims = [[], []]
    for axis, (first, last) in (("region", parts[:2]), ("survey", parts[2:])):
        count = lax.axis_size(axis)
        rims[0].append(lax.ppermute(first, axis, [(i + 1, i) for i in range(count - 1)]))
        if both:
            rims[1].append(lax.ppermute(last, axis, [(i, i + 1) for i in range(count - 1)]))
    return rims[0] + rims[1]


WHOLE = pl.BlockSpec(memory_space=pltpu.VMEM)
FAR = pl.BlockSpec(memory_space=pltpu.HBM)


class Free:
    def __init__(self, array):
        self.array = array
        self.shape, self.dtype = (array.shape, array.dtype)


def far(array):
    if isinstance(array, Free):
        return array.array
    return pltpu.with_memory_space_constraint(array, pltpu.HBM)


def far_spec(array):
    return pl.BlockSpec(memory_space=pl.ANY) if isinstance(array, Free) else FAR


def kernel_call(kernel, table, near, distant, outs, distant_outs, scratch):
    near_specs = [WHOLE] * len(near)
    out_shapes = [pltpu.HBM(o.shape, o.dtype) for o in (*outs, *distant_outs)]
    return pl.pallas_call(
        kernel,
        out_shape=out_shapes,
        grid_spec=pltpu.PrefetchScalarGridSpec(
            num_scalar_prefetch=1,
            grid=(),
            in_specs=near_specs + [far_spec(d) for d in distant],
            out_specs=[pl.BlockSpec(o.shape, functools.partial(origin, o.ndim)) for o in outs]
            + [FAR] * len(distant_outs),
            scratch_shapes=scratch,
        ),
        compiler_params=pltpu.CompilerParams(vmem_limit_bytes=KERNEL_VMEM),
    )(table, *near, *[far(d) for d in distant])


def origin(ndim, *_):
    return (0,) * ndim


def shape_of(dtype, *shape):
    return jax.ShapeDtypeStruct(shape, dtype)


def held(arrays):
    return [pltpu.VMEM(a.shape, a.dtype) for a in arrays] + [
        pltpu.SemaphoreType.DMA((len(arrays),))
    ]


def start_all(sources, targets, sems, base=0):
    copies = [
        pltpu.make_async_copy(source, target, sems.at[base + i])
        for i, (source, target) in enumerate(zip(sources, targets))
    ]
    for copy in copies:
        copy.start()
    return copies


def wait_all(copies):
    for copy in copies:
        copy.wait()


def start_pads(field_ref, pad, sem):
    layers, rows = field_ref.shape[:2]
    copy = pltpu.make_async_copy(field_ref, pad.at[pl.ds(0, layers), pl.ds(0, rows)], sem)
    copy.start()
    return copy


def fill_pads(pad, below, right):
    layers, rows = (pad.shape[0] - 1, pad.shape[1] - 1)
    pad[layers, pl.ds(0, rows)] = below[...].astype(pad.dtype)
    for layer in range(layers):
        pad[layer, rows] = right[layer].astype(pad.dtype)


def face(here, there, link):
    difference = here - there
    return difference, link * lax.rsqrt(difference * difference + EPS_SQ)


def levels(base, layer, depth_count):
    depth = (base + layer).astype(jnp.float32)
    return [1.0 + (2.0 * depth + offset) / depth_count for offset in (-1.0, 0.0, 1.0)]


def link_of(codes, number, level):
    return (lax.shift_right_logical(codes, number) & 1).astype(jnp.float32) * level


def next_lane(value):
    return pltpu.roll(value, value.shape[-1] - 1, value.ndim - 1)


def inner_lanes(cells):
    lane = lax.broadcasted_iota(jnp.int32, (GROUP, cells), 1)
    return (lane < cells - 1).astype(jnp.float32)


def step_from(got_ref, scale):
    sums = jnp.sum(got_ref[...], axis=0)
    norm, data, faces = (sums[:, i : i + 1] for i in range(3))
    return jnp.broadcast_to(norm / (data + scale[:, :1] * faces), scale.shape)


def prepare_kernel(start_ref, active_ref, model_ref, low_ref, top, bottom, left, right):
    block, rows = start_ref.shape[:2]

    def one(layer, carry):
        for start in range(0, rows, GROUP):
            live = active_ref[layer, pl.ds(start, GROUP), :].astype(jnp.float32)
            for k in range(GROUP):
                value = start_ref[layer, start + k] * live[k : k + 1]
                model_ref[layer, start + k] = value
                low_ref[layer, start + k] = value.astype(jnp.bfloat16)
        left[layer] = model_ref[layer, 0]
        right[layer] = model_ref[layer, rows - 1]
        return carry

    lax.fori_loop(0, block, one, 0)

    @pl.when(pl.program_id(0) == 0)
    def _():
        top[...] = model_ref[0]

    @pl.when(pl.program_id(0) == pl.num_programs(0) - 1)
    def _():
        bottom[...] = model_ref[block - 1]


def prepare_call(start_model, active):
    layers, rows, samples, cells = start_model.shape
    step = 4 if layers % 4 == 0 else 1
    block = pl.BlockSpec((step, rows, samples, cells), lambda i: (i, 0, 0, 0))
    layer = pl.BlockSpec((rows, samples, cells), lambda i: (0, 0, 0))
    column = pl.BlockSpec((step, samples, cells), lambda i: (i, 0, 0))
    outs = [
        (start_model.shape, jnp.float32),
        (start_model.shape, jnp.bfloat16),
        *[((rows, samples, cells), jnp.float32)] * 2,
        *[((layers, samples, cells), jnp.float32)] * 2,
    ]
    return pl.pallas_call(
        prepare_kernel,
        name="prepare",
        grid=(layers // step,),
        in_specs=[block, pl.BlockSpec((step, rows, cells), lambda i: (i, 0, 0))],
        out_specs=[block, block, layer, layer, column, column],
        out_shape=[
            jax.ShapeDtypeStruct(*o) if o[1] == jnp.bfloat16 else pltpu.HBM(*o) for o in outs
        ],
        compiler_params=pltpu.CompilerParams(vmem_limit_bytes=KERNEL_VMEM),
    )(far(start_model), far(active))


def face_pass(depth_count, base, links_ref, active_ref, pad, flow, above, left, edges_out, put):
    edge_z, edge_y = edges_out
    layers, rows = (pad.shape[0] - 1, pad.shape[1] - 1)
    inner = inner_lanes(pad.shape[-1])
    for start in range(0, rows, GROUP):
        codes = links_ref[pl.ds(start, GROUP), :]
        link = link_of(codes, 0, levels(base, 0, depth_count)[0])
        for k in range(GROUP):
            difference, weight = face(above(start + k), pad[0, start + k], link[k : k + 1])
            flow[start + k] = weight * difference

    def one(layer, carry):
        _, level, level_below = levels(base, layer, depth_count)
        flow_y = None
        for start in range(0, rows, GROUP):
            place = pl.ds(pl.multiple_of(layer * rows + start, GROUP), GROUP)
            codes = links_ref[place, :]
            link_z = link_of(codes, 1, level_below)
            link_y = link_of(codes, 3, level)
            link_x = link_of(codes, 5, level) * inner
            live = active_ref[place, :].astype(jnp.float32)
            small = live * level
            if start == 0:
                link = link_of(codes, 2, level)
                difference, weight = face(left(layer), pad[layer, 0], link[:1])
                flow_y = weight * difference
            for k in range(GROUP):
                row = start + k
                one_row = slice(k, k + 1)
                here = pad[layer, row]
                total = small[one_row] * lax.rsqrt(here * here + EPS_SQ) * here
                difference, weight = face(here, next_lane(here), link_x[one_row])
                flow_x = weight * difference
                total = total + flow_x - pltpu.roll(flow_x, 1, 1)
                difference, weight = face(here, pad[layer, row + 1], link_y[one_row])
                if row == rows - 1:
                    edge_y[layer] = weight
                out_y = weight * difference
                total = total + out_y - flow_y
                flow_y = out_y
                difference, weight = face(here, pad[layer + 1, row], link_z[one_row])
                edge_z[row] = weight
                out_z = weight * difference
                total = total + out_z - flow[row]
                flow[row] = out_z
                carry = put(layer, row, live[one_row], total, carry)
        return carry

    return lax.fori_loop(0, layers, one, jnp.zeros(pad.shape[2:], jnp.float32))


def reg_kernel(depth_count, base_ref, *refs):
    small_refs, refs = (refs[:7], refs[7:])
    field_ref, edge_z, edge_y, reg_ref, out, pad, flow, sems, *small, small_sems = refs
    copies = start_all(small_refs, small, small_sems)
    field_copy = start_pads(field_ref, pad, sems.at[0])
    wait_all(copies)
    links_ref, active_ref, scale_ref, below, right, above, left = small
    scale = scale_ref[...]
    fill_pads(pad, below, right)
    field_copy.wait()

    def put(layer, row, live, value, carry):
        out[layer, row] = scale * value
        return carry

    face_pass(
        depth_count,
        base_ref[0],
        links_ref,
        active_ref,
        pad,
        flow,
        lambda row: above[row],
        lambda layer: left[layer],
        (edge_z, edge_y),
        put,
    )
    final = pltpu.make_async_copy(out, reg_ref, sems.at[1])
    final.start()
    final.wait()


def reg_call(depth_count, base, links, active, scale, field, rims):
    layers, rows, samples, cells = field.shape
    f32 = jnp.float32
    small = [links, active, scale, *rims]
    return kernel_call(
        functools.partial(reg_kernel, depth_count),
        base,
        [],
        [*small, field],
        [shape_of(f32, rows, samples, cells), shape_of(f32, layers, samples, cells)],
        [shape_of(f32, *field.shape)],
        [
            pltpu.VMEM(field.shape, f32),
            pltpu.VMEM((layers + 1, rows + 1, samples, cells), f32),
            pltpu.VMEM((rows, samples, cells), f32),
            pltpu.SemaphoreType.DMA((2,)),
        ]
        + held(small),
    )


def next_kernel(depth_count, capacity, ids_ref, arrived_ref, *refs):
    small_refs, refs = (refs[:11], refs[11:])
    field_ref, grad_ref, reg_ref, *refs = refs
    reply_ref, norm_ref, top, bottom, first, last, edge_z, edge_y, step_ref, *refs = refs
    new_ref, out_ref, total, out, reg, pad, gpad, flow, sems, *small, small_sems = refs
    layers, rows = field_ref.shape[:2]
    count = ids_ref.shape[0] - 1
    copies = start_all(small_refs, small, small_sems)
    big = [start_pads(field_ref, pad, sems.at[0]), start_pads(grad_ref, gpad, sems.at[1])]
    big += start_all((reg_ref,), (reg,), sems, 2)
    add_blocks(count, capacity, 1, ids_ref, arrived_ref, total)
    owners = count // capacity
    sums = lax.fori_loop(
        0,
        owners,
        lambda i, v: v + arrived_ref[i * (capacity + 1) + capacity].astype(jnp.float32),
        jnp.zeros(norm_ref.shape, jnp.float32),
    )
    norm, data, faces = (
        sums[:, i : i + 1] + sums[:, i + 1 : i + 2] + sums[:, i + 2 : i + 3] for i in (0, 3, 6)
    )
    wait_all(copies)
    links_ref, active_ref, scale_ref, below, right, above, left, *more = small
    gbelow, gright, gabove, gleft = more
    scale = scale_ref[...]
    step = jnp.broadcast_to(norm / (data + scale[:, :1] * faces), scale.shape)
    step_ref[...] = step
    fill_pads(pad, below, right)
    fill_pads(gpad, gbelow, gright)
    wait_all(big)

    def move(layer, carry):
        for row in range(rows + 1):
            pad[layer, row] = pad[layer, row] - step * gpad[layer, row]
        return carry

    lax.fori_loop(0, layers, move, 0)
    for row in range(rows):
        pad[layers, row] = pad[layers, row] - step * gpad[layers, row]
    inside = pad.at[pl.ds(0, layers), pl.ds(0, rows)]
    stores = start_all((inside,), (new_ref,), sems, 3)

    def put(layer, row, live, value, norm):
        data = step * (live * total[layer * rows + row])
        value = scale * value + (gpad[layer, row] - reg[layer, row] - data)
        out[layer, row] = value
        return norm + value * value

    norm_ref[...] = face_pass(
        depth_count,
        ids_ref[count],
        links_ref,
        active_ref,
        pad,
        flow,
        lambda row: above[row] - step * gabove[row].astype(jnp.float32),
        lambda layer: left[layer] - step * gleft[layer].astype(jnp.float32),
        (edge_z, edge_y),
        put,
    )
    stores += start_all((out,), (out_ref,), sems, 4)

    def reply(i, carry):
        for k in range(GROUP):
            j = i * GROUP + k
            row = ids_ref[j]
            brick = out[lax.div(row, rows), lax.rem(row, rows)]
            reply_ref[j] = brick.astype(reply_ref.dtype)
        return carry

    lax.fori_loop(0, count // GROUP, reply, 0)
    top[...] = out[0].astype(top.dtype)
    bottom[...] = out[layers - 1].astype(bottom.dtype)
    for layer in range(layers):
        first[layer] = out[layer, 0].astype(first.dtype)
        last[layer] = out[layer, rows - 1].astype(last.dtype)
    wait_all(stores)


def next_call(
    depth_count, base, links, active, scale, capacity, ids, arrived, field, rims, grad, grad_rims,
    reg
):
    layers, rows, samples, cells = field.shape
    f32, bf16 = (jnp.float32, jnp.bfloat16)
    small = [links, active, scale, *rims, *(Free(rim) for rim in grad_rims)]
    pad = pltpu.VMEM((layers + 1, rows + 1, samples, cells), f32)
    rim_z, rim_y = ((rows, samples, cells), (layers, samples, cells))
    outs = [
        shape_of(bf16, ids.shape[0], samples, cells),
        shape_of(f32, samples, cells),
        shape_of(bf16, *rim_z),
        shape_of(bf16, *rim_z),
        shape_of(bf16, *rim_y),
        shape_of(bf16, *rim_y),
        shape_of(f32, *rim_z),
        shape_of(f32, *rim_y),
        shape_of(f32, samples, cells),
    ]
    return kernel_call(
        functools.partial(next_kernel, depth_count, capacity),
        jnp.concatenate([ids, base]),
        [arrived],
        [*small, field, grad, reg],
        outs,
        [shape_of(f32, *field.shape)] * 2,
        [
            pltpu.VMEM((layers * rows, samples, cells), f32),
            pltpu.VMEM(field.shape, f32),
            pltpu.VMEM(field.shape, f32),
            pad,
            pad,
            pltpu.VMEM(rim_z, f32),
            pltpu.SemaphoreType.DMA((5,)),
        ]
        + held(small),
    )


def curvature_kernel(
    depth_count, base_ref, links_ref, active_ref, field_ref, grad_ref, curv_ref, *refs
):
    links, active, field, grad, sems = refs
    layers, rows = field.shape[:2]
    base = base_ref[0]
    wait_all(
        start_all((field_ref, grad_ref, links_ref, active_ref), (field, grad, links, active), sems)
    )
    inner = inner_lanes(field.shape[-1])

    def one(layer, total):
        _, level, level_below = levels(base, layer, depth_count)
        below = jnp.minimum(layer + 1, layers - 1)
        level_below = jnp.where(layer + 1 < layers, level_below, 0.0)
        for start in range(0, rows, GROUP):
            place = pl.ds(pl.multiple_of(layer * rows + start, GROUP), GROUP)
            codes = links[place, :]
            link_z = link_of(codes, 1, level_below)
            link_y = link_of(codes, 3, level)
            link_x = link_of(codes, 5, level) * inner
            live = active[place, :].astype(jnp.float32) * level
            for k in range(GROUP):
                row = start + k
                one_row = slice(k, k + 1)
                here = field[layer, row]
                slope = grad[layer, row]
                part = live[one_row] * lax.rsqrt(here * here + EPS_SQ) * slope * slope
                pairs = [
                    (next_lane(here), next_lane(slope), link_x),
                    (field[below, row], grad[below, row], link_z),
                ]
                if row + 1 < rows:
                    pairs.append((field[layer, row + 1], grad[layer, row + 1], link_y))
                for there, gthere, link in pairs:
                    _, weight = face(here, there, link[one_row])
                    change = slope - gthere
                    part = part + weight * change * change
                total = total + part
        return total

    curv_ref[...] = lax.fori_loop(0, layers, one, jnp.zeros(curv_ref.shape, jnp.float32))


def curvature_call(depth_count, base, links, active, field, grad):
    (curv,) = kernel_call(
        functools.partial(curvature_kernel, depth_count),
        base,
        [],
        [links, active, field, grad],
        [shape_of(jnp.float32, *field.shape[2:])],
        [],
        held([links, active, field, grad]),
    )
    return curv


def sensor_copies(sensor_ref, held_ref, sems):
    tiles, _, length = held_ref.shape
    parts = sems.shape[1]
    columns = length // parts
    return [
        [
            pltpu.make_async_copy(
                sensor_ref.at[tile, :, pl.ds(part * columns, columns)],
                held_ref.at[tile, :, pl.ds(part * columns, columns)],
                sems.at[tile, part],
            )
            for part in range(parts)
        ]
        for tile in range(tiles)
    ]


def start_copies(copies, small):
    flat = [copy for tile in copies for copy in tile]
    flat[0].start()
    wait_all(small)
    for copy in flat[1:]:
        copy.start()


def gather_rows(width, slot_ref, arrived_ref, rows_ref):
    cells = arrived_ref.shape[2]

    def one(tile, carry):
        for entry in range(width):
            slot = slot_ref[tile * width + entry]
            rows_ref[tile, :, entry * cells : (entry + 1) * cells] = arrived_ref[slot]
        return carry

    lax.fori_loop(0, rows_ref.shape[0], one, 0)


def spaced(slot, capacity, extra):
    if not extra:
        return slot
    return slot + lax.div(slot, capacity) * extra


def scatter_rows(tile, width, slot_ref, blocks, buffer_ref, capacity=1, extra=0):
    cells = buffer_ref.shape[2]
    for entry in range(width):
        slot = spaced(slot_ref[tile * width + entry], capacity, extra)
        block = blocks[:, entry * cells : (entry + 1) * cells]
        buffer_ref[slot] = block.astype(buffer_ref.dtype)


def project(tile, copies, rows_ref, held_ref):
    parts = len(copies[tile])
    columns = held_ref.shape[2] // parts
    pred = 0.0
    for part in range(parts):
        span = slice(part * columns, (part + 1) * columns)
        copies[tile][part].wait()
        pred += lax.dot_general(
            rows_ref[tile, :, span],
            held_ref[tile, :, span],
            (((1,), (1,)), ((), ())),
            preferred_element_type=jnp.float32,
        )
    return pred


def residual_kernel(slot_ref, arrived_ref, sensor_ref, *refs):
    small_refs, refs = (refs[:2], refs[2:])
    pred_ref, buffer_ref, rows_ref, held_ref, sems, *small, small_sems = refs
    tiles = pred_ref.shape[0]
    width = slot_ref.shape[0] // tiles
    copies = sensor_copies(sensor_ref, held_ref, sems)
    start_copies(copies, start_all(small_refs, small, small_sems))
    weight, observed = small
    buffer_ref[...] = jnp.zeros_like(buffer_ref)
    gather_rows(width, slot_ref, arrived_ref, rows_ref)
    blocks = None
    for tile in range(tiles):
        pred = project(tile, copies, rows_ref, held_ref)
        if tile > 0:
            scatter_rows(tile - 1, width, slot_ref, blocks, buffer_ref)
        pred_ref[tile] = pred
        weighted = (weight[tile] * (pred - observed[tile])).astype(jnp.bfloat16)
        blocks = jnp.dot(weighted, held_ref[tile], preferred_element_type=jnp.float32)
    scatter_rows(tiles - 1, width, slot_ref, blocks, buffer_ref)


def local_sums(weight, pred_ref, norm, faces, rims):
    total = faces[...]
    for edge, mine, theirs in (rims[:3], rims[3:]):
        for row in range(edge.shape[0]):
            change = mine[row].astype(jnp.float32) - theirs[row].astype(jnp.float32)
            total = total + edge[row] * change * change
    tiles = pred_ref.shape[0]
    data = sum(weight[tile] * pred_ref[tile] * pred_ref[tile] for tile in range(tiles))
    return [jnp.sum(value, axis=1, keepdims=True) for value in (norm[...], data, total)]


def columns_of(values, shape):
    lane = lax.broadcasted_iota(jnp.int32, shape, 1)
    block = jnp.zeros(shape, jnp.float32)
    for i, value in enumerate(values):
        block = jnp.where(lane == i, value, block)
    return block


def in_parts(value):
    parts = []
    for _ in range(3):
        parts.append(value.astype(jnp.bfloat16).astype(jnp.float32))
        value = value - parts[-1]
    return parts


def forward_kernel(slot_ref, arrived_ref, sensor_ref, *refs):
    small_refs, refs = (refs[:9], refs[9:])
    pred_ref, sent_ref, rows_ref, held_ref, sems, *small, small_sems = refs
    tiles = pred_ref.shape[0]
    width = slot_ref.shape[0] // tiles
    copies = sensor_copies(sensor_ref, held_ref, sems)
    start_copies(copies, [])
    small_copies = start_all(small_refs, small, small_sems)
    gather_rows(width, slot_ref, arrived_ref, rows_ref)
    for tile in range(tiles):
        pred_ref[tile] = project(tile, copies, rows_ref, held_ref)
    wait_all(small_copies)
    weight, norm, faces, *rims = small
    sums = local_sums(weight, pred_ref, norm, faces, rims)
    sent_ref[...] = jnp.broadcast_to(columns_of(sums, norm.shape)[None], sent_ref.shape)


def both_kernel(capacity, slot_ref, arrived_ref, sensor_ref, *refs):
    small_refs, refs = (refs[:9], refs[9:])
    pred_ref, buffer_ref, rows_ref, held_ref, sems, *small, small_sems = refs
    tiles, samples = pred_ref.shape[:2]
    width = slot_ref.shape[0] // tiles
    copies = sensor_copies(sensor_ref, held_ref, sems)
    start_copies(copies, start_all(small_refs[:1], small[:1], small_sems))
    later = start_all(small_refs[1:], small[1:], small_sems, 1)
    weight, norm, faces, *rims = small
    buffer_ref[...] = jnp.zeros_like(buffer_ref)
    gather_rows(width, slot_ref, arrived_ref, rows_ref)

    def put(tile, blocks):
        scatter_rows(
            tile, width, slot_ref, blocks[:samples] + blocks[samples:], buffer_ref, capacity, 1
        )

    blocks = None
    for tile in range(tiles):
        pred = project(tile, copies, rows_ref, held_ref)
        if tile > 0:
            put(tile - 1, blocks)
        pred_ref[tile] = pred
        weighted = weight[tile] * pred
        upper = weighted.astype(jnp.bfloat16).astype(jnp.float32)
        pair = jnp.concatenate([upper, weighted - upper], axis=0).astype(jnp.bfloat16)
        blocks = jnp.dot(pair, held_ref[tile], preferred_element_type=jnp.float32)
    put(tiles - 1, blocks)
    wait_all(later)
    sums = local_sums(weight, pred_ref, norm, faces, rims)
    split = [part for value in sums for part in in_parts(value)]
    block = columns_of(split, norm.shape).astype(buffer_ref.dtype)

    def send(owner, carry):
        buffer_ref[owner * (capacity + 1) + capacity] = block
        return carry

    lax.fori_loop(0, buffer_ref.shape[0] // (capacity + 1), send, 0)


def tile_call(kernel, name, slot_of, near, sensor, small, outs, samples):
    tiles, _, length = sensor.shape
    parts = PARTS[name] if slot_of.shape[0] // tiles % PARTS[name] == 0 else 1
    scratch = [
        pltpu.VMEM(sensor.shape, jnp.bfloat16),
        pltpu.SemaphoreType.DMA((tiles, parts)),
    ]
    if near:
        scratch = [pltpu.VMEM((tiles, samples, length), jnp.bfloat16)] + scratch
    return kernel_call(kernel, slot_of, near, [sensor, *small], outs, [], scratch + held(small))


def add_blocks(count, capacity, extra, ids_ref, arrived_ref, total):
    total[...] = jnp.zeros_like(total)

    def add(i, carry):
        for k in range(GROUP):
            j = i * GROUP + k
            row = ids_ref[j]
            total[row] += arrived_ref[spaced(j, capacity, extra)].astype(jnp.float32)
        return carry

    lax.fori_loop(0, count // GROUP, add, 0)


def sum_kernel(layers, ids_ref, arrived_ref, *refs):
    active_ref, reg_ref, reply_ref, norm_ref, top, bottom, left, right, *refs = refs
    grad_ref, total, grad, out_sems, active, reg, sems = refs
    copies = start_all((active_ref, reg_ref), (active, reg), sems)
    count = ids_ref.shape[0]
    bricks = grad.shape[0]
    rows = bricks // layers
    add_blocks(count, 1, 0, ids_ref, arrived_ref, total)
    wait_all(copies)

    def combine(i, norm):
        live = active[pl.ds(pl.multiple_of(i * GROUP, GROUP), GROUP), :].astype(jnp.float32)
        for k in range(GROUP):
            j = i * GROUP + k
            value = live[k : k + 1] * total[j] + reg[j]
            grad[j] = value
            norm = norm + value * value
        return norm

    norm = lax.fori_loop(0, bricks // GROUP, combine, jnp.zeros(norm_ref.shape, jnp.float32))
    norm_ref[...] = norm
    stores = start_all((grad,), (grad_ref,), out_sems)

    def reply(i, carry):
        for k in range(GROUP):
            j = i * GROUP + k
            reply_ref[j] = grad[ids_ref[j]].astype(reply_ref.dtype)
        return carry

    lax.fori_loop(0, count // GROUP, reply, 0)
    top[...] = grad[pl.ds(0, rows)].astype(top.dtype)
    bottom[...] = grad[pl.ds(bricks - rows, rows)].astype(bottom.dtype)
    for layer in range(layers):
        left[layer] = grad[layer * rows].astype(left.dtype)
        right[layer] = grad[layer * rows + rows - 1].astype(right.dtype)
    wait_all(stores)


def sum_call(layers, ids, arrived, active, reg):
    bricks, samples, cells = reg.shape
    small = [active, reg]
    field = shape_of(jnp.float32, bricks, samples, cells)
    outs = [shape_of(jnp.bfloat16, *arrived.shape), shape_of(jnp.float32, samples, cells)]
    for length in (bricks // layers, bricks // layers, layers, layers):
        outs.append(shape_of(jnp.bfloat16, length, samples, cells))
    scratch = [
        pltpu.VMEM(field.shape, jnp.float32),
        pltpu.VMEM(field.shape, jnp.float32),
        pltpu.SemaphoreType.DMA((1,)),
    ]
    return kernel_call(
        functools.partial(sum_kernel, layers),
        ids,
        [arrived],
        small,
        outs,
        [field],
        scratch + held(small),
    )


def finish_kernel(_, got_ref, *refs):
    small_refs, refs = (refs[:7], refs[7:])
    field_ref, grad_ref, model_ref, misfit_ref, field, grad, misfit, sems, *refs = refs
    small, small_sems = (refs[:-1], refs[-1])
    copies = start_all(small_refs, small, small_sems)
    layers = field.shape[0]
    chunks = sems.shape[0] // 3
    spans = [pl.ds(i * (layers // chunks), layers // chunks) for i in range(chunks)]
    loads = [
        start_all(
            (field_ref.at[span], grad_ref.at[span]),
            (field.at[span], grad.at[span]),
            sems,
            3 * i,
        )
        for i, span in enumerate(spans)
    ]
    wait_all(copies)
    scale, before, mask, observed, pred_ref, moved, last = small
    step = step_from(got_ref, scale[...])
    for tile in range(misfit.shape[0]):
        pred = pred_ref[tile] - before[:, :1] * moved[tile]
        pred = pred - step[:, :1] * last[tile]
        misfit[tile] = mask[tile] * (pred - observed[tile])
    stores = start_all((misfit,), (misfit_ref,), sems, 3 * chunks)
    for i, span in enumerate(spans):
        wait_all(loads[i])
        field[span] = field[span] - step[None, None] * grad[span]
        stores += start_all((field.at[span],), (model_ref.at[span],), sems, 3 * i + 2)
    wait_all(stores)


def finish_call(table, got, scale, before, mask, observed, pred, moved, last, field, grad):
    small = [scale, before, mask, observed, pred, moved, last]
    chunks = 4 if field.shape[0] % 4 == 0 else 1
    return kernel_call(
        finish_kernel,
        table,
        [got],
        [*small, field, grad],
        [],
        [shape_of(jnp.float32, *a.shape) for a in (field, observed)],
        [
            pltpu.VMEM(field.shape, jnp.float32),
            pltpu.VMEM(field.shape, jnp.float32),
            pltpu.VMEM(observed.shape, jnp.float32),
            pltpu.SemaphoreType.DMA((3 * chunks + 1,)),
        ]
        + held(small),
    )


def shards(
    sensitivity,
    observed,
    data_weight,
    data_counts,
    tile_bricks,
    start_model,
    active_cells,
    face_links,
    reg_weight,
):
    layers, strip_rows, samples, cells_x = start_model.shape
    tiles, tile_width = tile_bricks.shape
    data_slots = sensitivity.shape[1]
    owners = lax.axis_size("region") * lax.axis_size("survey")
    per_owner = layers * strip_rows
    capacity = max(2, 2 * tiles * tile_width // owners)
    slots = owners * capacity
    depth_count = layers * lax.axis_size("region")
    requests = tile_bricks.reshape(-1)
    owner_of = requests // per_owner
    local_of = requests % per_owner
    owner_hits = (owner_of[:, None] == jnp.arange(owners, dtype=jnp.int32)[None, :]).astype(
        jnp.int32
    )
    before = jnp.cumsum(owner_hits, axis=0) - owner_hits
    rank_of = jnp.sum(before * owner_hits, axis=1)
    slot_of = owner_of * capacity + rank_of
    slot_hits = slot_of[:, None] == jnp.arange(slots, dtype=jnp.int32)[None, :]
    asking = jnp.sum(jnp.where(slot_hits, local_of[:, None], 0), axis=0).reshape(owners, capacity)
    asked_ids = swap(asking).reshape(-1)

    active_flat = active_cells.reshape(per_owner, cells_x)
    links = face_links.reshape(per_owner, cells_x)
    base = (lax.axis_index("region") * layers).astype(jnp.int32).reshape(1)
    row_mask = (
        jnp.arange(data_slots, dtype=jnp.int32)[None, None, :] < data_counts[:, None, None]
    ).astype(jnp.float32)
    weight_sq = row_mask * (data_weight * data_weight)[:, None, :]
    mask = row_mask * data_weight[:, None, :]
    reg_rows = jnp.broadcast_to(reg_weight[:, None], (samples, cells_x))
    f32, bf16 = (jnp.float32, jnp.bfloat16)
    pred_shape = shape_of(f32, tiles, samples, data_slots)

    def exchange(blocks):
        sent = blocks.reshape(owners, blocks.shape[0] // owners, samples, cells_x)
        return swap(sent).reshape(blocks.shape)

    def flat(field):
        return field.reshape(per_owner, samples, cells_x)

    def tile_stage(kernel, name, arrived, small, out):
        return tile_call(
            kernel, name, slot_of, [arrived], sensitivity, small, [pred_shape, out], samples
        )

    def sums_inputs(norm, faces, edge_z, edge_y, mine, theirs):
        below, right = (Free(rim) for rim in theirs[:2])
        return [weight_sq, norm, faces, edge_z, mine[0], below, edge_y, mine[1], right]

    grid = (depth_count, base, links, active_flat)
    model, bricks, *rims = prepare_call(start_model, active_cells)
    replies = flat(bricks)[asked_ids]
    arrived = exchange(replies)
    model_rims = edges(rims)
    blocks_shape = shape_of(bf16, slots, samples, cells_x)
    small = [weight_sq, observed]
    pred, buffer = tile_stage(residual_kernel, "residual", arrived, small, blocks_shape)

    arrived = exchange(buffer)
    edge_z, edge_y, reg = reg_call(*grid, reg_rows, model, model_rims)
    replies, norm, *rims, grad = sum_call(layers, asked_ids, arrived, active_flat, flat(reg))
    arrived = exchange(replies)
    grad_rims = edges(rims)
    grad = grad.reshape(start_model.shape)
    faces = curvature_call(*grid, model, grad)
    small = sums_inputs(norm, faces, edge_z, edge_y, rims[1::2], grad_rims)
    blocks_shape = shape_of(bf16, slots + owners, samples, cells_x)
    kernel = functools.partial(both_kernel, capacity)
    step_pred, buffer = tile_stage(kernel, "both", arrived, small, blocks_shape)
    arrived = exchange(buffer)

    replies, norm, *rims, edge_z, edge_y, step, model, grad = next_call(
        *grid, reg_rows, capacity, asked_ids, arrived, model, model_rims, grad, grad_rims, reg
    )
    arrived = exchange(replies)
    grad_rims = edges(rims, both=False)
    faces = curvature_call(*grid, model, grad)
    small = sums_inputs(norm, faces, edge_z, edge_y, rims[1::2], grad_rims)
    sums_shape = shape_of(f32, owners, samples, cells_x)
    last_pred, sums = tile_stage(forward_kernel, "forward", arrived, small, sums_shape)
    got = swap(sums)
    fields = (mask, observed, pred, step_pred, last_pred, model, grad)
    return tuple(finish_call(base, got, reg_rows, step, *fields))


def solution(mesh):
    return jax.shard_map(
        shards,
        mesh=mesh,
        in_specs=(
            P(("region", "survey"), None, None),
            P(("region", "survey"), None, None),
            P(("region", "survey"), None),
            P(("region", "survey")),
            P(("region", "survey"), None),
            P("region", "survey", None, None),
            P("region", "survey", None),
            P("region", "survey", None),
            P(),
        ),
        out_specs=(P("region", "survey", None, None), P(("region", "survey"), None, None)),
        check_vma=False,
    )
```

```python
import functools

import jax
import jax.numpy as jnp
from jax import lax
from jax.experimental import pallas as pl
from jax.experimental.pallas import tpu as pltpu
from jax.sharding import PartitionSpec as P


AXES = ("region", "survey")
EPS_SQ = 0.09
KERNEL_VMEM = 32 * 1024 * 1024
PARTS = {"residual": 1, "forward": 8, "both": 1}
GROUP = 8
TRIP = 32


def swap(field):
    return lax.all_to_all(field, AXES, split_axis=0, concat_axis=0, tiled=True)


def edges(parts, both=True):
    rims = [[], []]
    for axis, (first, last) in (("region", parts[:2]), ("survey", parts[2:])):
        count = lax.axis_size(axis)
        rims[0].append(lax.ppermute(first, axis, [(i + 1, i) for i in range(count - 1)]))
        if both:
            rims[1].append(lax.ppermute(last, axis, [(i, i + 1) for i in range(count - 1)]))
    return rims[0] + rims[1]


WHOLE = pl.BlockSpec(memory_space=pltpu.VMEM)
FAR = pl.BlockSpec(memory_space=pltpu.HBM)


class Free:
    def __init__(self, array):
        self.array = array
        self.shape, self.dtype = (array.shape, array.dtype)


def far(array):
    if isinstance(array, Free):
        return array.array
    return pltpu.with_memory_space_constraint(array, pltpu.HBM)


def far_spec(array):
    return pl.BlockSpec(memory_space=pl.ANY) if isinstance(array, Free) else FAR


def kernel_call(kernel, table, near, distant, outs, distant_outs, scratch):
    near_specs = [WHOLE] * len(near)
    out_shapes = [pltpu.HBM(o.shape, o.dtype) for o in (*outs, *distant_outs)]
    return pl.pallas_call(
        kernel,
        out_shape=out_shapes,
        grid_spec=pltpu.PrefetchScalarGridSpec(
            num_scalar_prefetch=1,
            grid=(),
            in_specs=near_specs + [far_spec(d) for d in distant],
            out_specs=[pl.BlockSpec(o.shape, functools.partial(origin, o.ndim)) for o in outs]
            + [FAR] * len(distant_outs),
            scratch_shapes=scratch,
        ),
        compiler_params=pltpu.CompilerParams(vmem_limit_bytes=KERNEL_VMEM),
    )(table, *near, *[far(d) for d in distant])


def origin(ndim, *_):
    return (0,) * ndim


def shape_of(dtype, *shape):
    return jax.ShapeDtypeStruct(shape, dtype)


def held(arrays):
    return [pltpu.VMEM(a.shape, a.dtype) for a in arrays] + [
        pltpu.SemaphoreType.DMA((len(arrays),))
    ]


def start_all(sources, targets, sems, base=0):
    copies = [
        pltpu.make_async_copy(source, target, sems.at[base + i])
        for i, (source, target) in enumerate(zip(sources, targets))
    ]
    for copy in copies:
        copy.start()
    return copies


def wait_all(copies):
    for copy in copies:
        copy.wait()


def start_pads(field_ref, pad, sem):
    layers, rows = field_ref.shape[:2]
    copy = pltpu.make_async_copy(field_ref, pad.at[pl.ds(0, layers), pl.ds(0, rows)], sem)
    copy.start()
    return copy


def fill_pads(pad, below, right):
    layers, rows = (pad.shape[0] - 1, pad.shape[1] - 1)
    pad[layers, pl.ds(0, rows)] = below[...].astype(pad.dtype)
    for layer in range(layers):
        pad[layer, rows] = right[layer].astype(pad.dtype)


def face(here, there, link):
    difference = here - there
    return difference, link * lax.rsqrt(difference * difference + EPS_SQ)


def levels(base, layer, depth_count):
    depth = (base + layer).astype(jnp.float32)
    return [1.0 + (2.0 * depth + offset) / depth_count for offset in (-1.0, 0.0, 1.0)]


def link_of(codes, number, level):
    return (lax.shift_right_logical(codes, number) & 1).astype(jnp.float32) * level


def next_lane(value):
    return pltpu.roll(value, value.shape[-1] - 1, value.ndim - 1)


def inner_lanes(cells):
    lane = lax.broadcasted_iota(jnp.int32, (GROUP, cells), 1)
    return (lane < cells - 1).astype(jnp.float32)


def step_from(got_ref, scale):
    sums = jnp.sum(got_ref[...], axis=0)
    norm, data, faces = (sums[:, i : i + 1] for i in range(3))
    return jnp.broadcast_to(norm / (data + scale[:, :1] * faces), scale.shape)


def prepare_kernel(start_ref, active_ref, model_ref, low_ref, top, bottom, left, right):
    block, rows = start_ref.shape[:2]

    def one(layer, carry):
        for start in range(0, rows, GROUP):
            live = active_ref[layer, pl.ds(start, GROUP), :].astype(jnp.float32)
            for k in range(GROUP):
                value = start_ref[layer, start + k] * live[k : k + 1]
                model_ref[layer, start + k] = value
                low_ref[layer, start + k] = value.astype(jnp.bfloat16)
        left[layer] = model_ref[layer, 0]
        right[layer] = model_ref[layer, rows - 1]
        return carry

    lax.fori_loop(0, block, one, 0)

    @pl.when(pl.program_id(0) == 0)
    def _():
        top[...] = model_ref[0]

    @pl.when(pl.program_id(0) == pl.num_programs(0) - 1)
    def _():
        bottom[...] = model_ref[block - 1]


def prepare_call(start_model, active):
    layers, rows, samples, cells = start_model.shape
    step = 4 if layers % 4 == 0 else 1
    block = pl.BlockSpec((step, rows, samples, cells), lambda i: (i, 0, 0, 0))
    layer = pl.BlockSpec((rows, samples, cells), lambda i: (0, 0, 0))
    column = pl.BlockSpec((step, samples, cells), lambda i: (i, 0, 0))
    outs = [
        (start_model.shape, jnp.float32),
        (start_model.shape, jnp.bfloat16),
        *[((rows, samples, cells), jnp.float32)] * 2,
        *[((layers, samples, cells), jnp.float32)] * 2,
    ]
    return pl.pallas_call(
        prepare_kernel,
        name="prepare",
        grid=(layers // step,),
        in_specs=[block, pl.BlockSpec((step, rows, cells), lambda i: (i, 0, 0))],
        out_specs=[block, block, layer, layer, column, column],
        out_shape=[
            jax.ShapeDtypeStruct(*o) if o[1] == jnp.bfloat16 else pltpu.HBM(*o) for o in outs
        ],
        compiler_params=pltpu.CompilerParams(vmem_limit_bytes=KERNEL_VMEM),
    )(far(start_model), far(active))


def face_pass(depth_count, base, links_ref, active_ref, pad, flow, above, left, edges_out, put):
    edge_z, edge_y = edges_out
    layers, rows = (pad.shape[0] - 1, pad.shape[1] - 1)
    inner = inner_lanes(pad.shape[-1])
    for start in range(0, rows, GROUP):
        codes = links_ref[pl.ds(start, GROUP), :]
        link = link_of(codes, 0, levels(base, 0, depth_count)[0])
        for k in range(GROUP):
            difference, weight = face(above(start + k), pad[0, start + k], link[k : k + 1])
            flow[start + k] = weight * difference

    def one(layer, carry):
        _, level, level_below = levels(base, layer, depth_count)
        flow_y = None
        for start in range(0, rows, GROUP):
            place = pl.ds(pl.multiple_of(layer * rows + start, GROUP), GROUP)
            codes = links_ref[place, :]
            link_z = link_of(codes, 1, level_below)
            link_y = link_of(codes, 3, level)
            link_x = link_of(codes, 5, level) * inner
            live = active_ref[place, :].astype(jnp.float32)
            small = live * level
            if start == 0:
                link = link_of(codes, 2, level)
                difference, weight = face(left(layer), pad[layer, 0], link[:1])
                flow_y = weight * difference
            for k in range(GROUP):
                row = start + k
                one_row = slice(k, k + 1)
                here = pad[layer, row]
                total = small[one_row] * lax.rsqrt(here * here + EPS_SQ) * here
                difference, weight = face(here, next_lane(here), link_x[one_row])
                flow_x = weight * difference
                total = total + flow_x - pltpu.roll(flow_x, 1, 1)
                difference, weight = face(here, pad[layer, row + 1], link_y[one_row])
                if row == rows - 1:
                    edge_y[layer] = weight
                out_y = weight * difference
                total = total + out_y - flow_y
                flow_y = out_y
                difference, weight = face(here, pad[layer + 1, row], link_z[one_row])
                edge_z[row] = weight
                out_z = weight * difference
                total = total + out_z - flow[row]
                flow[row] = out_z
                carry = put(layer, row, live[one_row], total, carry)
        return carry

    return lax.fori_loop(0, layers, one, jnp.zeros(pad.shape[2:], jnp.float32))


def reg_kernel(depth_count, base_ref, *refs):
    small_refs, refs = (refs[:7], refs[7:])
    field_ref, edge_z, edge_y, reg_ref, out, pad, flow, sems, *small, small_sems = refs
    copies = start_all(small_refs, small, small_sems)
    field_copy = start_pads(field_ref, pad, sems.at[0])
    wait_all(copies)
    links_ref, active_ref, scale_ref, below, right, above, left = small
    scale = scale_ref[...]
    fill_pads(pad, below, right)
    field_copy.wait()

    def put(layer, row, live, value, carry):
        out[layer, row] = scale * value
        return carry

    face_pass(
        depth_count,
        base_ref[0],
        links_ref,
        active_ref,
        pad,
        flow,
        lambda row: above[row],
        lambda layer: left[layer],
        (edge_z, edge_y),
        put,
    )
    final = pltpu.make_async_copy(out, reg_ref, sems.at[1])
    final.start()
    final.wait()


def reg_call(depth_count, base, links, active, scale, field, rims):
    layers, rows, samples, cells = field.shape
    f32 = jnp.float32
    small = [links, active, scale, *rims]
    return kernel_call(
        functools.partial(reg_kernel, depth_count),
        base,
        [],
        [*small, field],
        [shape_of(f32, rows, samples, cells), shape_of(f32, layers, samples, cells)],
        [shape_of(f32, *field.shape)],
        [
            pltpu.VMEM(field.shape, f32),
            pltpu.VMEM((layers + 1, rows + 1, samples, cells), f32),
            pltpu.VMEM((rows, samples, cells), f32),
            pltpu.SemaphoreType.DMA((2,)),
        ]
        + held(small),
    )


def next_kernel(depth_count, capacity, ids_ref, arrived_ref, *refs):
    small_refs, refs = (refs[:11], refs[11:])
    field_ref, grad_ref, reg_ref, *refs = refs
    reply_ref, norm_ref, top, bottom, first, last, edge_z, edge_y, step_ref, *refs = refs
    new_ref, out_ref, total, out, reg, pad, gpad, flow, sems, *small, small_sems = refs
    layers, rows = field_ref.shape[:2]
    count = ids_ref.shape[0] - 1
    copies = start_all(small_refs, small, small_sems)
    big = [start_pads(field_ref, pad, sems.at[0]), start_pads(grad_ref, gpad, sems.at[1])]
    big += start_all((reg_ref,), (reg,), sems, 2)
    add_blocks(count, capacity, 1, ids_ref, arrived_ref, total)
    owners = count // capacity
    sums = lax.fori_loop(
        0,
        owners,
        lambda i, v: v + arrived_ref[i * (capacity + 1) + capacity].astype(jnp.float32),
        jnp.zeros(norm_ref.shape, jnp.float32),
    )
    norm, data, faces = (
        sums[:, i : i + 1] + sums[:, i + 1 : i + 2] + sums[:, i + 2 : i + 3] for i in (0, 3, 6)
    )
    wait_all(copies)
    links_ref, active_ref, scale_ref, below, right, above, left, *more = small
    gbelow, gright, gabove, gleft = more
    scale = scale_ref[...]
    step = jnp.broadcast_to(norm / (data + scale[:, :1] * faces), scale.shape)
    step_ref[...] = step
    fill_pads(pad, below, right)
    fill_pads(gpad, gbelow, gright)
    wait_all(big)

    def move(layer, carry):
        for row in range(rows + 1):
            pad[layer, row] = pad[layer, row] - step * gpad[layer, row]
        return carry

    lax.fori_loop(0, layers, move, 0)
    for row in range(rows):
        pad[layers, row] = pad[layers, row] - step * gpad[layers, row]
    inside = pad.at[pl.ds(0, layers), pl.ds(0, rows)]
    stores = start_all((inside,), (new_ref,), sems, 3)

    def put(layer, row, live, value, norm):
        data = step * (live * total[layer * rows + row])
        value = scale * value + (gpad[layer, row] - reg[layer, row] - data)
        out[layer * rows + row] = value
        return norm + value * value

    norm_ref[...] = face_pass(
        depth_count,
        ids_ref[count],
        links_ref,
        active_ref,
        pad,
        flow,
        lambda row: above[row] - step * gabove[row].astype(jnp.float32),
        lambda layer: left[layer] - step * gleft[layer].astype(jnp.float32),
        (edge_z, edge_y),
        put,
    )
    stores += start_all((out,), (out_ref,), sems, 4)

    trip = trip_of(count)

    def reply(i, carry):
        for k in range(trip):
            j = i * trip + k
            reply_ref[j] = out[ids_ref[j]].astype(reply_ref.dtype)
        return carry

    lax.fori_loop(0, count // trip, reply, 0)
    top[...] = out[pl.ds(0, rows)].astype(top.dtype)
    bottom[...] = out[pl.ds((layers - 1) * rows, rows)].astype(bottom.dtype)
    for layer in range(layers):
        first[layer] = out[layer * rows].astype(first.dtype)
        last[layer] = out[layer * rows + rows - 1].astype(last.dtype)
    wait_all(stores)


def next_call(
    depth_count, base, links, active, scale, capacity, ids, arrived, field, rims, grad, grad_rims,
    reg
):
    layers, rows, samples, cells = field.shape
    f32, bf16 = (jnp.float32, jnp.bfloat16)
    small = [links, active, scale, *rims, *(Free(rim) for rim in grad_rims)]
    pad = pltpu.VMEM((layers + 1, rows + 1, samples, cells), f32)
    rim_z, rim_y = ((rows, samples, cells), (layers, samples, cells))
    outs = [
        shape_of(bf16, ids.shape[0], samples, cells),
        shape_of(f32, samples, cells),
        shape_of(bf16, *rim_z),
        shape_of(bf16, *rim_z),
        shape_of(bf16, *rim_y),
        shape_of(bf16, *rim_y),
        shape_of(f32, *rim_z),
        shape_of(f32, *rim_y),
        shape_of(f32, samples, cells),
    ]
    return kernel_call(
        functools.partial(next_kernel, depth_count, capacity),
        jnp.concatenate([ids, base]),
        [arrived],
        [*small, field, grad, reg],
        outs,
        [shape_of(f32, *field.shape), shape_of(f32, layers * rows, samples, cells)],
        [
            pltpu.VMEM((layers * rows, samples, cells), f32),
            pltpu.VMEM((layers * rows, samples, cells), f32),
            pltpu.VMEM(field.shape, f32),
            pad,
            pad,
            pltpu.VMEM(rim_z, f32),
            pltpu.SemaphoreType.DMA((5,)),
        ]
        + held(small),
    )


def curvature_kernel(
    depth_count, base_ref, links_ref, active_ref, field_ref, grad_ref, curv_ref, *refs
):
    links, active, field, grad, sems = refs
    layers, rows = field.shape[:2]
    base = base_ref[0]
    wait_all(
        start_all((field_ref, grad_ref, links_ref, active_ref), (field, grad, links, active), sems)
    )
    inner = inner_lanes(field.shape[-1])

    def one(layer, total):
        _, level, level_below = levels(base, layer, depth_count)
        below = jnp.minimum(layer + 1, layers - 1)
        level_below = jnp.where(layer + 1 < layers, level_below, 0.0)
        for start in range(0, rows, GROUP):
            place = pl.ds(pl.multiple_of(layer * rows + start, GROUP), GROUP)
            codes = links[place, :]
            link_z = link_of(codes, 1, level_below)
            link_y = link_of(codes, 3, level)
            link_x = link_of(codes, 5, level) * inner
            live = active[place, :].astype(jnp.float32) * level
            for k in range(GROUP):
                row = start + k
                one_row = slice(k, k + 1)
                here = field[layer, row]
                slope = grad[layer, row]
                part = live[one_row] * lax.rsqrt(here * here + EPS_SQ) * slope * slope
                pairs = [
                    (next_lane(here), next_lane(slope), link_x),
                    (field[below, row], grad[below, row], link_z),
                ]
                if row + 1 < rows:
                    pairs.append((field[layer, row + 1], grad[layer, row + 1], link_y))
                for there, gthere, link in pairs:
                    _, weight = face(here, there, link[one_row])
                    change = slope - gthere
                    part = part + weight * change * change
                total = total + part
        return total

    curv_ref[...] = lax.fori_loop(0, layers, one, jnp.zeros(curv_ref.shape, jnp.float32))


def curvature_call(depth_count, base, links, active, field, grad):
    (curv,) = kernel_call(
        functools.partial(curvature_kernel, depth_count),
        base,
        [],
        [links, active, field, grad],
        [shape_of(jnp.float32, *field.shape[2:])],
        [],
        held([links, active, field, grad]),
    )
    return curv


def sensor_copies(sensor_ref, held_ref, sems):
    tiles, _, length = held_ref.shape
    parts = sems.shape[1]
    columns = length // parts
    return [
        [
            pltpu.make_async_copy(
                sensor_ref.at[tile, :, pl.ds(part * columns, columns)],
                held_ref.at[tile, :, pl.ds(part * columns, columns)],
                sems.at[tile, part],
            )
            for part in range(parts)
        ]
        for tile in range(tiles)
    ]


def start_copies(copies, small):
    flat = [copy for tile in copies for copy in tile]
    flat[0].start()
    wait_all(small)
    for copy in flat[1:]:
        copy.start()


def gather_rows(width, slot_ref, arrived_ref, rows_ref):
    cells = arrived_ref.shape[2]

    def one(tile, carry):
        for entry in range(width):
            slot = slot_ref[tile * width + entry]
            rows_ref[tile, :, entry * cells : (entry + 1) * cells] = arrived_ref[slot]
        return carry

    lax.fori_loop(0, rows_ref.shape[0], one, 0)


def spaced(slot, capacity, extra):
    if not extra:
        return slot
    return slot + lax.div(slot, capacity) * extra


def scatter_rows(tile, width, slot_ref, blocks, buffer_ref, capacity=1, extra=0):
    cells = buffer_ref.shape[2]
    for entry in range(width):
        slot = spaced(slot_ref[tile * width + entry], capacity, extra)
        block = blocks[:, entry * cells : (entry + 1) * cells]
        buffer_ref[slot] = block.astype(buffer_ref.dtype)


def project(tile, copies, rows_ref, held_ref):
    parts = len(copies[tile])
    columns = held_ref.shape[2] // parts
    pred = 0.0
    for part in range(parts):
        span = slice(part * columns, (part + 1) * columns)
        copies[tile][part].wait()
        pred += lax.dot_general(
            rows_ref[tile, :, span],
            held_ref[tile, :, span],
            (((1,), (1,)), ((), ())),
            preferred_element_type=jnp.float32,
        )
    return pred


def residual_kernel(slot_ref, arrived_ref, sensor_ref, *refs):
    small_refs, refs = (refs[:2], refs[2:])
    pred_ref, buffer_ref, rows_ref, held_ref, sems, *small, small_sems = refs
    tiles = pred_ref.shape[0]
    width = slot_ref.shape[0] // tiles
    copies = sensor_copies(sensor_ref, held_ref, sems)
    start_copies(copies, start_all(small_refs, small, small_sems))
    weight, observed = small
    buffer_ref[...] = jnp.zeros_like(buffer_ref)
    gather_rows(width, slot_ref, arrived_ref, rows_ref)
    blocks = None
    for tile in range(tiles):
        pred = project(tile, copies, rows_ref, held_ref)
        if tile > 0:
            scatter_rows(tile - 1, width, slot_ref, blocks, buffer_ref)
        pred_ref[tile] = pred
        weighted = (weight[tile] * (pred - observed[tile])).astype(jnp.bfloat16)
        blocks = jnp.dot(weighted, held_ref[tile], preferred_element_type=jnp.float32)
    scatter_rows(tiles - 1, width, slot_ref, blocks, buffer_ref)


def local_sums(weight, pred_ref, norm, faces, rims):
    total = faces[...]
    for edge, mine, theirs in (rims[:3], rims[3:]):
        for row in range(edge.shape[0]):
            change = mine[row].astype(jnp.float32) - theirs[row].astype(jnp.float32)
            total = total + edge[row] * change * change
    tiles = pred_ref.shape[0]
    data = sum(weight[tile] * pred_ref[tile] * pred_ref[tile] for tile in range(tiles))
    return [jnp.sum(value, axis=1, keepdims=True) for value in (norm[...], data, total)]


def columns_of(values, shape):
    lane = lax.broadcasted_iota(jnp.int32, shape, 1)
    block = jnp.zeros(shape, jnp.float32)
    for i, value in enumerate(values):
        block = jnp.where(lane == i, value, block)
    return block


def in_parts(value):
    parts = []
    for _ in range(3):
        parts.append(value.astype(jnp.bfloat16).astype(jnp.float32))
        value = value - parts[-1]
    return parts


def forward_kernel(slot_ref, arrived_ref, sensor_ref, *refs):
    small_refs, refs = (refs[:9], refs[9:])
    pred_ref, sent_ref, rows_ref, held_ref, sems, *small, small_sems = refs
    tiles = pred_ref.shape[0]
    width = slot_ref.shape[0] // tiles
    copies = sensor_copies(sensor_ref, held_ref, sems)
    start_copies(copies, [])
    small_copies = start_all(small_refs, small, small_sems)
    gather_rows(width, slot_ref, arrived_ref, rows_ref)
    for tile in range(tiles):
        pred_ref[tile] = project(tile, copies, rows_ref, held_ref)
    wait_all(small_copies)
    weight, norm, faces, *rims = small
    sums = local_sums(weight, pred_ref, norm, faces, rims)
    sent_ref[...] = jnp.broadcast_to(columns_of(sums, norm.shape)[None], sent_ref.shape)


def both_kernel(capacity, slot_ref, arrived_ref, sensor_ref, *refs):
    small_refs, refs = (refs[:9], refs[9:])
    pred_ref, buffer_ref, rows_ref, held_ref, sems, *small, small_sems = refs
    tiles, samples = pred_ref.shape[:2]
    width = slot_ref.shape[0] // tiles
    copies = sensor_copies(sensor_ref, held_ref, sems)
    start_copies(copies, start_all(small_refs[:1], small[:1], small_sems))
    later = start_all(small_refs[1:], small[1:], small_sems, 1)
    weight, norm, faces, *rims = small
    buffer_ref[...] = jnp.zeros_like(buffer_ref)
    gather_rows(width, slot_ref, arrived_ref, rows_ref)

    def put(tile, blocks):
        scatter_rows(
            tile, width, slot_ref, blocks[:samples] + blocks[samples:], buffer_ref, capacity, 1
        )

    blocks = None
    for tile in range(tiles):
        pred = project(tile, copies, rows_ref, held_ref)
        if tile > 0:
            put(tile - 1, blocks)
        pred_ref[tile] = pred
        weighted = weight[tile] * pred
        upper = weighted.astype(jnp.bfloat16).astype(jnp.float32)
        pair = jnp.concatenate([upper, weighted - upper], axis=0).astype(jnp.bfloat16)
        blocks = jnp.dot(pair, held_ref[tile], preferred_element_type=jnp.float32)
    put(tiles - 1, blocks)
    wait_all(later)
    sums = local_sums(weight, pred_ref, norm, faces, rims)
    split = [part for value in sums for part in in_parts(value)]
    block = columns_of(split, norm.shape).astype(buffer_ref.dtype)

    def send(owner, carry):
        buffer_ref[owner * (capacity + 1) + capacity] = block
        return carry

    lax.fori_loop(0, buffer_ref.shape[0] // (capacity + 1), send, 0)


def tile_call(kernel, name, slot_of, near, sensor, small, outs, samples):
    tiles, _, length = sensor.shape
    parts = PARTS[name] if slot_of.shape[0] // tiles % PARTS[name] == 0 else 1
    scratch = [
        pltpu.VMEM(sensor.shape, jnp.bfloat16),
        pltpu.SemaphoreType.DMA((tiles, parts)),
    ]
    if near:
        scratch = [pltpu.VMEM((tiles, samples, length), jnp.bfloat16)] + scratch
    return kernel_call(kernel, slot_of, near, [sensor, *small], outs, [], scratch + held(small))


def trip_of(count):
    return TRIP if count % TRIP == 0 else GROUP


def add_blocks(count, capacity, extra, ids_ref, arrived_ref, total):
    total[...] = jnp.zeros_like(total)

    trip = trip_of(count)

    def add(i, carry):
        for k in range(trip):
            j = i * trip + k
            row = ids_ref[j]
            total[row] += arrived_ref[spaced(j, capacity, extra)].astype(jnp.float32)
        return carry

    lax.fori_loop(0, count // trip, add, 0)


def sum_kernel(layers, ids_ref, arrived_ref, *refs):
    active_ref, reg_ref, reply_ref, norm_ref, top, bottom, left, right, *refs = refs
    grad_ref, total, grad, out_sems, active, reg, sems = refs
    copies = start_all((active_ref, reg_ref), (active, reg), sems)
    count = ids_ref.shape[0]
    bricks = grad.shape[0]
    rows = bricks // layers
    add_blocks(count, 1, 0, ids_ref, arrived_ref, total)
    wait_all(copies)

    trip = trip_of(bricks)

    def combine(i, norm):
        live = active[pl.ds(pl.multiple_of(i * trip, GROUP), trip), :].astype(jnp.float32)
        squares = []
        for k in range(trip):
            j = i * trip + k
            value = live[k : k + 1] * total[j] + reg[j]
            grad[j] = value
            squares.append(value * value)
        while len(squares) > 1:
            squares = [sum(squares[k : k + 2]) for k in range(0, len(squares), 2)]
        return norm + squares[0]

    norm = lax.fori_loop(0, bricks // trip, combine, jnp.zeros(norm_ref.shape, jnp.float32))
    norm_ref[...] = norm
    stores = start_all((grad,), (grad_ref,), out_sems)

    trip = trip_of(count)

    def reply(i, carry):
        for k in range(trip):
            j = i * trip + k
            reply_ref[j] = grad[ids_ref[j]].astype(reply_ref.dtype)
        return carry

    lax.fori_loop(0, count // trip, reply, 0)
    top[...] = grad[pl.ds(0, rows)].astype(top.dtype)
    bottom[...] = grad[pl.ds(bricks - rows, rows)].astype(bottom.dtype)
    for layer in range(layers):
        left[layer] = grad[layer * rows].astype(left.dtype)
        right[layer] = grad[layer * rows + rows - 1].astype(right.dtype)
    wait_all(stores)


def sum_call(layers, ids, arrived, active, reg):
    bricks, samples, cells = reg.shape
    small = [active, reg]
    field = shape_of(jnp.float32, bricks, samples, cells)
    outs = [shape_of(jnp.bfloat16, *arrived.shape), shape_of(jnp.float32, samples, cells)]
    for length in (bricks // layers, bricks // layers, layers, layers):
        outs.append(shape_of(jnp.bfloat16, length, samples, cells))
    scratch = [
        pltpu.VMEM(field.shape, jnp.float32),
        pltpu.VMEM(field.shape, jnp.float32),
        pltpu.SemaphoreType.DMA((1,)),
    ]
    return kernel_call(
        functools.partial(sum_kernel, layers),
        ids,
        [arrived],
        small,
        outs,
        [field],
        scratch + held(small),
    )


def finish_kernel(_, got_ref, *refs):
    small_refs, refs = (refs[:7], refs[7:])
    field_ref, grad_ref, model_ref, misfit_ref, field, grad, misfit, sems, *refs = refs
    small, small_sems = (refs[:-1], refs[-1])
    copies = start_all(small_refs, small, small_sems)
    layers = field.shape[0]
    chunks = sems.shape[0] // 3
    spans = [pl.ds(i * (layers // chunks), layers // chunks) for i in range(chunks)]
    loads = [
        start_all(
            (field_ref.at[span], grad_ref.at[span]),
            (field.at[span], grad.at[span]),
            sems,
            3 * i,
        )
        for i, span in enumerate(spans)
    ]
    wait_all(copies)
    scale, before, mask, observed, pred_ref, moved, last = small
    step = step_from(got_ref, scale[...])
    for tile in range(misfit.shape[0]):
        pred = pred_ref[tile] - before[:, :1] * moved[tile]
        pred = pred - step[:, :1] * last[tile]
        misfit[tile] = mask[tile] * (pred - observed[tile])
    stores = start_all((misfit,), (misfit_ref,), sems, 3 * chunks)
    for i, span in enumerate(spans):
        wait_all(loads[i])
        field[span] = field[span] - step[None, None] * grad[span]
        stores += start_all((field.at[span],), (model_ref.at[span],), sems, 3 * i + 2)
    wait_all(stores)


def finish_call(table, got, scale, before, mask, observed, pred, moved, last, field, grad):
    small = [scale, before, mask, observed, pred, moved, last]
    chunks = 4 if field.shape[0] % 4 == 0 else 1
    return kernel_call(
        finish_kernel,
        table,
        [got],
        [*small, field, grad],
        [],
        [shape_of(jnp.float32, *a.shape) for a in (field, observed)],
        [
            pltpu.VMEM(field.shape, jnp.float32),
            pltpu.VMEM(field.shape, jnp.float32),
            pltpu.VMEM(observed.shape, jnp.float32),
            pltpu.SemaphoreType.DMA((3 * chunks + 1,)),
        ]
        + held(small),
    )


def shards(
    sensitivity,
    observed,
    data_weight,
    data_counts,
    tile_bricks,
    start_model,
    active_cells,
    face_links,
    reg_weight,
):
    layers, strip_rows, samples, cells_x = start_model.shape
    tiles, tile_width = tile_bricks.shape
    data_slots = sensitivity.shape[1]
    owners = lax.axis_size("region") * lax.axis_size("survey")
    per_owner = layers * strip_rows
    capacity = max(2, 2 * tiles * tile_width // owners)
    slots = owners * capacity
    depth_count = layers * lax.axis_size("region")
    requests = tile_bricks.reshape(-1)
    owner_of = requests // per_owner
    local_of = requests % per_owner
    owner_hits = (owner_of[:, None] == jnp.arange(owners, dtype=jnp.int32)[None, :]).astype(
        jnp.int32
    )
    before = jnp.cumsum(owner_hits, axis=0) - owner_hits
    rank_of = jnp.sum(before * owner_hits, axis=1)
    slot_of = owner_of * capacity + rank_of
    slot_hits = slot_of[:, None] == jnp.arange(slots, dtype=jnp.int32)[None, :]
    asking = jnp.sum(jnp.where(slot_hits, local_of[:, None], 0), axis=0).reshape(owners, capacity)
    asked_ids = swap(asking).reshape(-1)

    active_flat = active_cells.reshape(per_owner, cells_x)
    links = face_links.reshape(per_owner, cells_x)
    base = (lax.axis_index("region") * layers).astype(jnp.int32).reshape(1)
    row_mask = (
        jnp.arange(data_slots, dtype=jnp.int32)[None, None, :] < data_counts[:, None, None]
    ).astype(jnp.float32)
    weight_sq = row_mask * (data_weight * data_weight)[:, None, :]
    mask = row_mask * data_weight[:, None, :]
    reg_rows = jnp.broadcast_to(reg_weight[:, None], (samples, cells_x))
    f32, bf16 = (jnp.float32, jnp.bfloat16)
    pred_shape = shape_of(f32, tiles, samples, data_slots)

    def exchange(blocks):
        sent = blocks.reshape(owners, blocks.shape[0] // owners, samples, cells_x)
        return swap(sent).reshape(blocks.shape)

    def flat(field):
        return field.reshape(per_owner, samples, cells_x)

    def tile_stage(kernel, name, arrived, small, out):
        return tile_call(
            kernel, name, slot_of, [arrived], sensitivity, small, [pred_shape, out], samples
        )

    def sums_inputs(norm, faces, edge_z, edge_y, mine, theirs):
        below, right = (Free(rim) for rim in theirs[:2])
        return [weight_sq, norm, faces, edge_z, mine[0], below, edge_y, mine[1], right]

    grid = (depth_count, base, links, active_flat)
    model, bricks, *rims = prepare_call(start_model, active_cells)
    replies = flat(bricks)[asked_ids]
    arrived = exchange(replies)
    model_rims = edges(rims)
    blocks_shape = shape_of(bf16, slots, samples, cells_x)
    small = [weight_sq, observed]
    pred, buffer = tile_stage(residual_kernel, "residual", arrived, small, blocks_shape)

    arrived = exchange(buffer)
    edge_z, edge_y, reg = reg_call(*grid, reg_rows, model, model_rims)
    replies, norm, *rims, grad = sum_call(layers, asked_ids, arrived, active_flat, flat(reg))
    arrived = exchange(replies)
    grad_rims = edges(rims)
    grad = grad.reshape(start_model.shape)
    faces = curvature_call(*grid, model, grad)
    small = sums_inputs(norm, faces, edge_z, edge_y, rims[1::2], grad_rims)
    blocks_shape = shape_of(bf16, slots + owners, samples, cells_x)
    kernel = functools.partial(both_kernel, capacity)
    step_pred, buffer = tile_stage(kernel, "both", arrived, small, blocks_shape)
    arrived = exchange(buffer)

    replies, norm, *rims, edge_z, edge_y, step, model, grad = next_call(
        *grid, reg_rows, capacity, asked_ids, arrived, model, model_rims, grad, grad_rims, reg
    )
    arrived = exchange(replies)
    grad_rims = edges(rims, both=False)
    grad = grad.reshape(start_model.shape)
    faces = curvature_call(*grid, model, grad)
    small = sums_inputs(norm, faces, edge_z, edge_y, rims[1::2], grad_rims)
    sums_shape = shape_of(f32, owners, samples, cells_x)
    last_pred, sums = tile_stage(forward_kernel, "forward", arrived, small, sums_shape)
    got = swap(sums)
    fields = (mask, observed, pred, step_pred, last_pred, model, grad)
    return tuple(finish_call(base, got, reg_rows, step, *fields))


def solution(mesh):
    return jax.shard_map(
        shards,
        mesh=mesh,
        in_specs=(
            P(("region", "survey"), None, None),
            P(("region", "survey"), None, None),
            P(("region", "survey"), None),
            P(("region", "survey")),
            P(("region", "survey"), None),
            P("region", "survey", None, None),
            P("region", "survey", None),
            P("region", "survey", None),
            P(),
        ),
        out_specs=(P("region", "survey", None, None), P(("region", "survey"), None, None)),
        check_vma=False,
    )
```
